256 devices in a mesh: aux: 2 (over core), row: 8 (over z), col: 16 (over x, y).
Axes of the slice: x: 4, y: 4, z: 8, core: 2. Of those that a mesh axis runs over, the one named last changes fastest.
Arguments:
- coulomb: bfloat16 [64, 2048, 2048], P('aux', 'row', 'col'), may hold values from -6 to 6
- occupied: bfloat16 [2048, 2048], P('row'), may hold values from -0.125 to 0.125
- virtual: bfloat16 [2048, 2048], P('row'), may hold values from -0.125 to 0.125
- tile_mask: int32 [16, 16], replicated, may hold values 0 or 1
Outputs:
- chi: float32 [64, 64], P('aux')
The draws below stay inside these ranges and needn't reach their ends.
All inputs are finite; a program needn't handle non-finite values.
Results may differ from the reference program's by a relative error of at most 0.0042.
Values may be sent and summed in bfloat16 or wider, within the bound.
A program may use at most 128 MiB of HBM per device.

```python
import jax
import jax.numpy as jnp
from jax import lax

NAO = 2048
TILE = 128
NAUX = 64
NT = 16


def place_ends(entries, rng, least, largest):
    place = [jax.random.randint(jax.random.fold_in(rng, axis), (), 0, length) for axis, length in enumerate(entries.shape)]
    longest = entries.shape.index(max(entries.shape))
    neighbour = place[:longest] + [(place[longest] + 1) % entries.shape[longest]] + place[longest + 1:]
    return entries.at[tuple(place)].set(least).at[tuple(neighbour)].set(largest)


def level_of(own_key, dims, pieces, smallest, largest):
    level, own = 1.0, jax.random.fold_in(own_key, 6)
    for dim, parts in pieces:
        heights = jnp.exp(jax.random.uniform(jax.random.fold_in(own, dim), (parts,), jnp.float32, smallest / len(pieces), largest / len(pieces)))
        level = level * jnp.repeat(heights, dims[dim] // parts).reshape([-1 if axis == dim else 1 for axis in range(len(dims))])
    return level


def centred(rng, extent, spread, most, cuts=(), dtype=jnp.bfloat16):
    result = spread * jax.random.normal(rng, extent, jnp.float32)
    if cuts:
        result = result * level_of(rng, extent, cuts, -0.22, 0.18)
    return jnp.clip(result, -most, most).astype(dtype)


def setup_inputs(seed: int = 0) -> dict:
    streams_of = jax.random.split(jax.random.key(seed), 5)
    coulomb = centred(streams_of[0], (NAUX, NAO, NAO), 1.0, 6.0, ((0, 2), (1, 8), (2, 16)))
    occupied = centred(streams_of[1], (NAO, NAO), NAO ** -0.5, 0.125, ((0, 8),))
    virtual = centred(streams_of[2], (NAO, NAO), NAO ** -0.5, 0.125, ((0, 8),))
    tile_mask = place_ends((jax.random.randint(streams_of[3], (NT, NT), 0, 4) < 3).astype(jnp.int32), jax.random.fold_in(streams_of[3], 1), 0, 1)
    return {"coulomb": coulomb, "occupied": occupied, "virtual": virtual, "tile_mask": tile_mask}


def reference(coulomb, occupied, virtual, tile_mask):
    full_mask = jnp.repeat(jnp.repeat(tile_mask, TILE, axis=0), TILE, axis=1)
    screened = coulomb * full_mask.astype(jnp.bfloat16)[None]
    left_t = occupied.T

    def dress_one(block):
        half = jnp.dot(left_t, block, preferred_element_type=jnp.float32).astype(jnp.bfloat16)
        return jnp.dot(half, virtual, preferred_element_type=jnp.float32).astype(jnp.bfloat16)

    dressed = lax.map(dress_one, screened)
    flat_x = dressed.reshape(NAUX, NAO * NAO)
    flat_b = screened.reshape(NAUX, NAO * NAO)
    chi = jnp.dot(flat_x, flat_b.T, preferred_element_type=jnp.float32)
    return chi / NAO
```

```python
import jax
import jax.numpy as jnp
from jax import lax
from jax.sharding import PartitionSpec as P

NAO = 2048
TILE = 128


def swapped(value, axis, apart):
    mask = 2**apart
    pairs = [(source, source ^ mask) for source in range(lax.axis_size(axis))]
    return lax.ppermute(value, axis, pairs)


def shards(coulomb, occupied, virtual, tile_mask):
    rows = lax.axis_size("row")
    cols = lax.axis_size("col")
    pdev, mrow, ncol = coulomb.shape
    nao = mrow * rows
    row_idx = lax.axis_index("row")
    col_idx = lax.axis_index("col")
    aux_idx = lax.axis_index("aux")
    tiles_r = mrow // TILE
    tiles_c = ncol // TILE
    local_tiles = lax.dynamic_slice(
        tile_mask, (row_idx * tiles_r, col_idx * tiles_c), (tiles_r, tiles_c)
    )
    local_mask = jnp.repeat(jnp.repeat(local_tiles, TILE, axis=0), TILE, axis=1).astype(
        jnp.bfloat16
    )
    screened = coulomb * local_mask[None]
    moved = lax.all_to_all(screened, "row", split_axis=0, concat_axis=1, tiled=True)
    pieces = moved.shape[0]
    occ_all, virt_all = (
        lax.all_gather(occupied, "row", axis=0, tiled=True),
        lax.all_gather(virtual, "row", axis=0, tiled=True),
    )
    half = jnp.einsum("ml,pmn->pln", occ_all, moved, preferred_element_type=jnp.float32).astype(
        jnp.bfloat16
    )
    jpart = mrow // cols
    shaped = half.reshape(pieces, rows, cols, jpart, ncol)
    spread = lax.all_to_all(shaped, "col", split_axis=2, concat_axis=4, tiled=True)
    spread = spread.reshape(pieces, rows * jpart, nao)
    dressed = jnp.einsum(
        "pln,ns->pls", spread, virt_all, preferred_element_type=jnp.float32
    ).astype(jnp.bfloat16)
    layered = dressed.reshape(pieces, rows, 1, jpart, cols, ncol)
    returned = lax.all_to_all(
        lax.all_to_all(layered, "row", split_axis=1, concat_axis=0, tiled=True),
        "col",
        split_axis=4,
        concat_axis=2,
        tiled=True,
    )
    aligned = returned.reshape(pdev, mrow, ncol)
    theirs = swapped(screened, "aux", 0)
    with_mine = jnp.einsum("pls,qls->pq", aligned, screened, preferred_element_type=jnp.float32)
    with_theirs = jnp.einsum("pls,qls->pq", aligned, theirs, preferred_element_type=jnp.float32)
    first_half = jnp.where(aux_idx == 0, with_mine, with_theirs)
    second_half = jnp.where(aux_idx == 0, with_theirs, with_mine)
    partial_chi = jnp.concatenate([first_half, second_half], axis=1)
    slots = lax.axis_size("aux")
    placed = jnp.zeros((slots,) + partial_chi.shape, partial_chi.dtype)
    placed = lax.dynamic_update_index_in_dim(placed, partial_chi, aux_idx, 0)
    total = lax.psum(placed, ("aux", "row", "col"))
    total_chi = lax.dynamic_index_in_dim(total, aux_idx, 0, keepdims=False)
    return total_chi / NAO


def solution(mesh):
    placed = (P("aux", "row", "col"), P("row", None), P("row", None), P())
    return jax.shard_map(
        shards, mesh=mesh, in_specs=placed, out_specs=P("aux", None), check_vma=False
    )
```

```python
import jax
import jax.numpy as jnp
from jax import lax
from jax.sharding import PartitionSpec as P

NAO = 2048
TILE = 128


def swapped(value, axis, apart):
    mask = 2**apart
    pairs = [(source, source ^ mask) for source in range(lax.axis_size(axis))]
    return lax.ppermute(value, axis, pairs)


def spread_density(local):
    cols = lax.axis_size("col")
    cores = lax.axis_size("aux")
    width = local.shape[1] // cols
    piece = lax.dynamic_slice_in_dim(local, lax.axis_index("col") * width, width, axis=1)
    column = lax.all_gather(piece, "row", axis=0, tiled=True)
    height = column.shape[0] // cores
    part = lax.dynamic_slice_in_dim(column, lax.axis_index("aux") * height, height, axis=0)
    rows = lax.all_gather(part, "col", axis=1, tiled=True)
    return lax.all_gather(rows, "aux", axis=0, tiled=True)


def shards(coulomb, occupied, virtual, tile_mask):
    rows = lax.axis_size("row")
    cols = lax.axis_size("col")
    pdev, mrow, ncol = coulomb.shape
    nao = mrow * rows
    row_idx = lax.axis_index("row")
    col_idx = lax.axis_index("col")
    aux_idx = lax.axis_index("aux")
    tiles_r = mrow // TILE
    tiles_c = ncol // TILE
    local_tiles = lax.dynamic_slice(
        tile_mask, (row_idx * tiles_r, col_idx * tiles_c), (tiles_r, tiles_c)
    )
    local_mask = jnp.repeat(jnp.repeat(local_tiles, TILE, axis=0), TILE, axis=1).astype(
        jnp.bfloat16
    )
    screened = coulomb * local_mask[None]
    moved = lax.all_to_all(screened, "row", split_axis=0, concat_axis=1, tiled=True)
    pieces = moved.shape[0]
    occ_all, virt_all = spread_density(occupied), spread_density(virtual)
    half = jnp.einsum("ml,pmn->pln", occ_all, moved, preferred_element_type=jnp.float32).astype(
        jnp.bfloat16
    )
    jpart = mrow // cols
    shaped = half.reshape(pieces, rows, cols, jpart, ncol)
    spread = lax.all_to_all(shaped, "col", split_axis=2, concat_axis=4, tiled=True)
    spread = spread.reshape(pieces, rows * jpart, nao)
    dressed = jnp.einsum(
        "pln,ns->pls", spread, virt_all, preferred_element_type=jnp.float32
    ).astype(jnp.bfloat16)
    layered = dressed.reshape(pieces, rows, 1, jpart, cols, ncol)
    returned = lax.all_to_all(
        lax.all_to_all(layered, "row", split_axis=1, concat_axis=0, tiled=True),
        "col",
        split_axis=4,
        concat_axis=2,
        tiled=True,
    )
    aligned = returned.reshape(pdev, mrow, ncol)
    theirs = swapped(screened, "aux", 0)
    with_mine = jnp.einsum("pls,qls->pq", aligned, screened, preferred_element_type=jnp.float32)
    with_theirs = jnp.einsum("pls,qls->pq", aligned, theirs, preferred_element_type=jnp.float32)
    first_half = jnp.where(aux_idx == 0, with_mine, with_theirs)
    second_half = jnp.where(aux_idx == 0, with_theirs, with_mine)
    partial_chi = jnp.concatenate([first_half, second_half], axis=1)
    slots = lax.axis_size("aux")
    placed = jnp.zeros((slots,) + partial_chi.shape, partial_chi.dtype)
    placed = lax.dynamic_update_index_in_dim(placed, partial_chi, aux_idx, 0)
    total = lax.psum(placed, ("aux", "row", "col"))
    total_chi = lax.dynamic_index_in_dim(total, aux_idx, 0, keepdims=False)
    return total_chi / NAO


def solution(mesh):
    placed = (P("aux", "row", "col"), P("row", None), P("row", None), P())
    return jax.shard_map(
        shards, mesh=mesh, in_specs=placed, out_specs=P("aux", None), check_vma=False
    )
```

```python
import functools

import jax
import jax.numpy as jnp
from jax import lax
from jax.sharding import PartitionSpec as P
from jax.experimental import pallas as pl
from jax.experimental.pallas import tpu as pltpu

NAO = 2048
TILE = 128


def swapped(value, axis, apart):
    mask = 2**apart
    pairs = [(source, source ^ mask) for source in range(lax.axis_size(axis))]
    return lax.ppermute(value, axis, pairs)


def partner_rounds():
    rounds = []
    for axis in ("col", "row"):
        bit = 1
        while bit < lax.axis_size(axis):
            rounds.append((axis, bit))
            bit *= 2
    return rounds


def doubling_kernel(rounds, x_ref, o_ref, recv, send_sem, recv_sem):
    here = {name: lax.axis_index(name) for name in ("aux", "row", "col")}

    def partner(axis, bit):
        place = dict(here)
        place[axis] = here[axis] ^ bit
        return (place["aux"], place["row"], place["col"])

    barrier = pltpu.get_barrier_semaphore()
    for axis, bit in rounds:
        pl.semaphore_signal(
            barrier, inc=1, device_id=partner(axis, bit), device_id_type=pl.DeviceIdType.MESH
        )
    pl.semaphore_wait(barrier, len(rounds))

    o_ref[...] = x_ref[...]
    for step, (axis, bit) in enumerate(rounds):
        copy = pltpu.make_async_remote_copy(
            src_ref=o_ref,
            dst_ref=recv.at[step],
            send_sem=send_sem.at[step],
            recv_sem=recv_sem.at[step],
            device_id=partner(axis, bit),
            device_id_type=pl.DeviceIdType.MESH,
        )
        copy.start()
        copy.wait()
        o_ref[...] = o_ref[...] + recv[step]


def doubling_sum(partial):
    rounds = partner_rounds()
    return pl.pallas_call(
        functools.partial(doubling_kernel, rounds),
        out_shape=jax.ShapeDtypeStruct(partial.shape, partial.dtype),
        in_specs=[pl.BlockSpec(memory_space=pltpu.VMEM)],
        out_specs=pl.BlockSpec(memory_space=pltpu.VMEM),
        scratch_shapes=[
            pltpu.VMEM((len(rounds),) + partial.shape, partial.dtype),
            pltpu.SemaphoreType.DMA((len(rounds),)),
            pltpu.SemaphoreType.DMA((len(rounds),)),
        ],
        compiler_params=pltpu.CompilerParams(collective_id=0, has_side_effects=True),
    )(partial)


def shards(coulomb, occupied, virtual, tile_mask):
    rows = lax.axis_size("row")
    cols = lax.axis_size("col")
    pdev, mrow, ncol = coulomb.shape
    nao = mrow * rows
    row_idx = lax.axis_index("row")
    col_idx = lax.axis_index("col")
    aux_idx = lax.axis_index("aux")
    tiles_r = mrow // TILE
    tiles_c = ncol // TILE
    local_tiles = lax.dynamic_slice(
        tile_mask, (row_idx * tiles_r, col_idx * tiles_c), (tiles_r, tiles_c)
    )
    local_mask = jnp.repeat(jnp.repeat(local_tiles, TILE, axis=0), TILE, axis=1).astype(
        jnp.bfloat16
    )
    screened = coulomb * local_mask[None]
    moved = lax.all_to_all(screened, "row", split_axis=0, concat_axis=1, tiled=True)
    pieces = moved.shape[0]
    occ_all, virt_all = (
        lax.all_gather(occupied, "row", axis=0, tiled=True),
        lax.all_gather(virtual, "row", axis=0, tiled=True),
    )
    half = jnp.einsum("ml,pmn->pln", occ_all, moved, preferred_element_type=jnp.float32).astype(
        jnp.bfloat16
    )
    jpart = mrow // cols
    shaped = half.reshape(pieces, rows, cols, jpart, ncol)
    spread = lax.all_to_all(shaped, "col", split_axis=2, concat_axis=4, tiled=True)
    spread = spread.reshape(pieces, rows * jpart, nao)
    dressed = jnp.einsum(
        "pln,ns->pls", spread, virt_all, preferred_element_type=jnp.float32
    ).astype(jnp.bfloat16)
    layered = dressed.reshape(pieces, rows, 1, jpart, cols, ncol)
    returned = lax.all_to_all(
        lax.all_to_all(layered, "row", split_axis=1, concat_axis=0, tiled=True),
        "col",
        split_axis=4,
        concat_axis=2,
        tiled=True,
    )
    aligned = returned.reshape(pdev, mrow, ncol)
    theirs = swapped(screened, "aux", 0)
    with_mine = jnp.einsum("pls,qls->pq", aligned, screened, preferred_element_type=jnp.float32)
    with_theirs = jnp.einsum("pls,qls->pq", aligned, theirs, preferred_element_type=jnp.float32)
    first_half = jnp.where(aux_idx == 0, with_mine, with_theirs)
    second_half = jnp.where(aux_idx == 0, with_theirs, with_mine)
    partial_chi = jnp.concatenate([first_half, second_half], axis=1)
    total_chi = doubling_sum(partial_chi)
    return total_chi / NAO


def solution(mesh):
    placed = (P("aux", "row", "col"), P("row", None), P("row", None), P())
    return jax.shard_map(
        shards, mesh=mesh, in_specs=placed, out_specs=P("aux", None), check_vma=False
    )
```

```python
import functools

import jax
import jax.numpy as jnp
from jax import lax
from jax.sharding import PartitionSpec as P
from jax.experimental import pallas as pl
from jax.experimental.pallas import tpu as pltpu

NAO = 2048
TILE = 128


def swapped(value, axis, apart):
    mask = 2**apart
    pairs = [(source, source ^ mask) for source in range(lax.axis_size(axis))]
    return lax.ppermute(value, axis, pairs)


def partner_rounds():
    rounds = []
    for axis in ("col", "row"):
        bit = 1
        while bit < lax.axis_size(axis):
            rounds.append((axis, bit))
            bit *= 2
    return rounds


def doubling_kernel(rounds, x_ref, o_ref, recv, send_sem, recv_sem):
    here = {name: lax.axis_index(name) for name in ("aux", "row", "col")}

    def partner(axis, bit):
        place = dict(here)
        place[axis] = here[axis] ^ bit
        return (place["aux"], place["row"], place["col"])

    barrier = pltpu.get_barrier_semaphore()
    for axis, bit in rounds:
        pl.semaphore_signal(
            barrier, inc=1, device_id=partner(axis, bit), device_id_type=pl.DeviceIdType.MESH
        )
    pl.semaphore_wait(barrier, len(rounds))

    o_ref[...] = x_ref[...]
    for step, (axis, bit) in enumerate(rounds):
        copy = pltpu.make_async_remote_copy(
            src_ref=o_ref,
            dst_ref=recv.at[step],
            send_sem=send_sem.at[step],
            recv_sem=recv_sem.at[step],
            device_id=partner(axis, bit),
            device_id_type=pl.DeviceIdType.MESH,
        )
        copy.start()
        copy.wait()
        o_ref[...] = o_ref[...] + recv[step]


def doubling_sum(partial):
    rounds = partner_rounds()
    return pl.pallas_call(
        functools.partial(doubling_kernel, rounds),
        out_shape=jax.ShapeDtypeStruct(partial.shape, partial.dtype),
        in_specs=[pl.BlockSpec(memory_space=pltpu.VMEM)],
        out_specs=pl.BlockSpec(memory_space=pltpu.VMEM),
        scratch_shapes=[
            pltpu.VMEM((len(rounds),) + partial.shape, partial.dtype),
            pltpu.SemaphoreType.DMA((len(rounds),)),
            pltpu.SemaphoreType.DMA((len(rounds),)),
        ],
        compiler_params=pltpu.CompilerParams(collective_id=0, has_side_effects=True),
    )(partial)


def gather_half(local):
    width = local.shape[1] // 2
    part = lax.dynamic_slice_in_dim(local, lax.axis_index("aux") * width, width, axis=1)
    return lax.all_gather(part, "row", axis=0, tiled=True)


def join_halves(own, other, axis):
    first = lax.axis_index("aux") == 0
    return jnp.where(
        first,
        jnp.concatenate([own, other], axis=axis),
        jnp.concatenate([other, own], axis=axis),
    )


def swapped_core(value):
    return lax.ppermute(value, "aux", [(0, 1), (1, 0)])


def shards(coulomb, occupied, virtual, tile_mask):
    rows = lax.axis_size("row")
    cols = lax.axis_size("col")
    pdev, mrow, ncol = coulomb.shape
    nao = mrow * rows
    row_idx = lax.axis_index("row")
    col_idx = lax.axis_index("col")
    aux_idx = lax.axis_index("aux")
    tiles_r = mrow // TILE
    tiles_c = ncol // TILE
    local_tiles = lax.dynamic_slice(
        tile_mask, (row_idx * tiles_r, col_idx * tiles_c), (tiles_r, tiles_c)
    )
    local_mask = jnp.repeat(jnp.repeat(local_tiles, TILE, axis=0), TILE, axis=1).astype(
        jnp.bfloat16
    )
    screened = coulomb * local_mask[None]
    occ_own, virt_own = gather_half(occupied), gather_half(virtual)
    moved = lax.all_to_all(screened, "row", split_axis=0, concat_axis=1, tiled=True)
    occ_own, virt_own, moved = lax.optimization_barrier((occ_own, virt_own, moved))
    pieces = moved.shape[0]
    occ_other = swapped_core(occ_own)
    virt_all = join_halves(virt_own, swapped_core(virt_own), axis=1)
    half_own = jnp.einsum("ml,pmn->pln", occ_own, moved, preferred_element_type=jnp.float32)
    half_other = jnp.einsum("ml,pmn->pln", occ_other, moved, preferred_element_type=jnp.float32)
    half = join_halves(half_own.astype(jnp.bfloat16), half_other.astype(jnp.bfloat16), axis=1)
    jpart = mrow // cols
    shaped = half.reshape(pieces, rows, cols, jpart, ncol)
    spread = lax.all_to_all(shaped, "col", split_axis=2, concat_axis=4, tiled=True)
    spread = spread.reshape(pieces, rows * jpart, nao)
    dressed = jnp.einsum(
        "pln,ns->pls", spread, virt_all, preferred_element_type=jnp.float32
    ).astype(jnp.bfloat16)
    layered = dressed.reshape(pieces, rows, 1, jpart, cols, ncol)
    returned = lax.all_to_all(
        lax.all_to_all(layered, "row", split_axis=1, concat_axis=0, tiled=True),
        "col",
        split_axis=4,
        concat_axis=2,
        tiled=True,
    )
    aligned = returned.reshape(pdev, mrow, ncol)
    theirs = swapped(screened, "aux", 0)
    with_mine = jnp.einsum("pls,qls->pq", aligned, screened, preferred_element_type=jnp.float32)
    with_theirs = jnp.einsum("pls,qls->pq", aligned, theirs, preferred_element_type=jnp.float32)
    first_half = jnp.where(aux_idx == 0, with_mine, with_theirs)
    second_half = jnp.where(aux_idx == 0, with_theirs, with_mine)
    partial_chi = jnp.concatenate([first_half, second_half], axis=1)
    total_chi = doubling_sum(partial_chi)
    return total_chi / NAO


def solution(mesh):
    placed = (P("aux", "row", "col"), P("row", None), P("row", None), P())
    return jax.shard_map(
        shards, mesh=mesh, in_specs=placed, out_specs=P("aux", None), check_vma=False
    )
```

```python
import functools

import jax
import jax.numpy as jnp
from jax import lax
from jax.sharding import PartitionSpec as P
from jax.experimental import pallas as pl
from jax.experimental.pallas import tpu as pltpu

NAO = 2048
TILE = 128


def swapped(value, axis, apart):
    mask = 2**apart
    pairs = [(source, source ^ mask) for source in range(lax.axis_size(axis))]
    return lax.ppermute(value, axis, pairs)


def partner_rounds():
    rounds = []
    for axis in ("col", "row"):
        bit = 1
        while bit < lax.axis_size(axis):
            rounds.append((axis, bit))
            bit *= 2
    return rounds


def doubling_kernel(rounds, x_ref, o_ref, recv, send_sem, recv_sem):
    here = {name: lax.axis_index(name) for name in ("aux", "row", "col")}

    def partner(axis, bit):
        place = dict(here)
        place[axis] = here[axis] ^ bit
        return (place["aux"], place["row"], place["col"])

    barrier = pltpu.get_barrier_semaphore()
    for axis, bit in rounds:
        pl.semaphore_signal(
            barrier, inc=1, device_id=partner(axis, bit), device_id_type=pl.DeviceIdType.MESH
        )
    pl.semaphore_wait(barrier, len(rounds))

    o_ref[...] = x_ref[...]
    for step, (axis, bit) in enumerate(rounds):
        copy = pltpu.make_async_remote_copy(
            src_ref=o_ref,
            dst_ref=recv.at[step],
            send_sem=send_sem.at[step],
            recv_sem=recv_sem.at[step],
            device_id=partner(axis, bit),
            device_id_type=pl.DeviceIdType.MESH,
        )
        copy.start()
        copy.wait()
        o_ref[...] = o_ref[...] + recv[step]


def doubling_sum(partial):
    rounds = partner_rounds()
    return pl.pallas_call(
        functools.partial(doubling_kernel, rounds),
        out_shape=jax.ShapeDtypeStruct(partial.shape, partial.dtype),
        in_specs=[pl.BlockSpec(memory_space=pltpu.VMEM)],
        out_specs=pl.BlockSpec(memory_space=pltpu.VMEM),
        scratch_shapes=[
            pltpu.VMEM((len(rounds),) + partial.shape, partial.dtype),
            pltpu.SemaphoreType.DMA((len(rounds),)),
            pltpu.SemaphoreType.DMA((len(rounds),)),
        ],
        compiler_params=pltpu.CompilerParams(collective_id=0, has_side_effects=True),
    )(partial)


def gather_half(local):
    width = local.shape[1] // 2
    part = lax.dynamic_slice_in_dim(local, lax.axis_index("aux") * width, width, axis=1)
    return lax.all_gather(part, "row", axis=0, tiled=True)


def join_halves(own, other, axis):
    first = lax.axis_index("aux") == 0
    return jnp.where(
        first,
        jnp.concatenate([own, other], axis=axis),
        jnp.concatenate([other, own], axis=axis),
    )


def swapped_core(value):
    return lax.ppermute(value, "aux", [(0, 1), (1, 0)])


def shards(coulomb, occupied, virtual, tile_mask):
    rows = lax.axis_size("row")
    cols = lax.axis_size("col")
    pdev, mrow, ncol = coulomb.shape
    nao = mrow * rows
    row_idx = lax.axis_index("row")
    col_idx = lax.axis_index("col")
    aux_idx = lax.axis_index("aux")
    tiles_r = mrow // TILE
    tiles_c = ncol // TILE
    local_tiles = lax.dynamic_slice(
        tile_mask, (row_idx * tiles_r, col_idx * tiles_c), (tiles_r, tiles_c)
    )
    local_mask = jnp.repeat(jnp.repeat(local_tiles, TILE, axis=0), TILE, axis=1).astype(
        jnp.bfloat16
    )
    screened = coulomb * local_mask[None]
    occ_own, virt_own = gather_half(occupied), gather_half(virtual)
    moved = lax.all_to_all(screened, "row", split_axis=0, concat_axis=1, tiled=True)
    occ_own, moved = lax.optimization_barrier((occ_own, moved))
    pieces = moved.shape[0]
    occ_other = swapped_core(occ_own)
    half_own = jnp.einsum("ml,pmn->pln", occ_own, moved, preferred_element_type=jnp.float32)
    half_other = jnp.einsum("ml,pmn->pln", occ_other, moved, preferred_element_type=jnp.float32)
    half = join_halves(half_own.astype(jnp.bfloat16), half_other.astype(jnp.bfloat16), axis=1)
    jpart = mrow // cols
    shaped = half.reshape(pieces, rows, cols, jpart, ncol)
    spread = lax.all_to_all(shaped, "col", split_axis=2, concat_axis=4, tiled=True)
    spread = spread.reshape(pieces, rows * jpart, nao)
    virt_own, spread = lax.optimization_barrier((virt_own, spread))
    virt_all = join_halves(virt_own, swapped_core(virt_own), axis=1)
    dressed = jnp.einsum(
        "pln,ns->pls", spread, virt_all, preferred_element_type=jnp.float32
    ).astype(jnp.bfloat16)
    layered = dressed.reshape(pieces, rows, 1, jpart, cols, ncol)
    returned = lax.all_to_all(
        lax.all_to_all(layered, "row", split_axis=1, concat_axis=0, tiled=True),
        "col",
        split_axis=4,
        concat_axis=2,
        tiled=True,
    )
    aligned = returned.reshape(pdev, mrow, ncol)
    theirs = swapped(screened, "aux", 0)
    with_mine = jnp.einsum("pls,qls->pq", aligned, screened, preferred_element_type=jnp.float32)
    with_theirs = jnp.einsum("pls,qls->pq", aligned, theirs, preferred_element_type=jnp.float32)
    first_half = jnp.where(aux_idx == 0, with_mine, with_theirs)
    second_half = jnp.where(aux_idx == 0, with_theirs, with_mine)
    partial_chi = jnp.concatenate([first_half, second_half], axis=1)
    total_chi = doubling_sum(partial_chi)
    return total_chi / NAO


def solution(mesh):
    placed = (P("aux", "row", "col"), P("row", None), P("row", None), P())
    return jax.shard_map(
        shards, mesh=mesh, in_specs=placed, out_specs=P("aux", None), check_vma=False
    )
```

```python
import functools

import jax
import jax.numpy as jnp
from jax import lax
from jax.sharding import PartitionSpec as P
from jax.experimental import pallas as pl
from jax.experimental.pallas import tpu as pltpu

NAO = 2048
TILE = 128


def swapped(value, axis, apart):
    mask = 2**apart
    pairs = [(source, source ^ mask) for source in range(lax.axis_size(axis))]
    return lax.ppermute(value, axis, pairs)


def partner_rounds():
    rounds = []
    for axis in ("col", "row"):
        bit = 1
        while bit < lax.axis_size(axis):
            rounds.append((axis, bit))
            bit *= 2
    return rounds


def doubling_kernel(rounds, x_ref, o_ref, recv, send_sem, recv_sem):
    here = {name: lax.axis_index(name) for name in ("aux", "row", "col")}

    def partner(axis, bit):
        place = dict(here)
        place[axis] = here[axis] ^ bit
        return (place["aux"], place["row"], place["col"])

    barrier = pltpu.get_barrier_semaphore()
    for axis, bit in rounds:
        pl.semaphore_signal(
            barrier, inc=1, device_id=partner(axis, bit), device_id_type=pl.DeviceIdType.MESH
        )
    pl.semaphore_wait(barrier, len(rounds))

    o_ref[...] = x_ref[...]
    for step, (axis, bit) in enumerate(rounds):
        copy = pltpu.make_async_remote_copy(
            src_ref=o_ref,
            dst_ref=recv.at[step],
            send_sem=send_sem.at[step],
            recv_sem=recv_sem.at[step],
            device_id=partner(axis, bit),
            device_id_type=pl.DeviceIdType.MESH,
        )
        copy.start()
        copy.wait()
        o_ref[...] = o_ref[...] + recv[step]


def doubling_sum(partial):
    rounds = partner_rounds()
    return pl.pallas_call(
        functools.partial(doubling_kernel, rounds),
        out_shape=jax.ShapeDtypeStruct(partial.shape, partial.dtype),
        in_specs=[pl.BlockSpec(memory_space=pltpu.VMEM)],
        out_specs=pl.BlockSpec(memory_space=pltpu.VMEM),
        scratch_shapes=[
            pltpu.VMEM((len(rounds),) + partial.shape, partial.dtype),
            pltpu.SemaphoreType.DMA((len(rounds),)),
            pltpu.SemaphoreType.DMA((len(rounds),)),
        ],
        compiler_params=pltpu.CompilerParams(collective_id=0, has_side_effects=True),
    )(partial)


def gather_half(local):
    width = local.shape[1] // 2
    part = lax.dynamic_slice_in_dim(local, lax.axis_index("aux") * width, width, axis=1)
    return lax.all_gather(part, "row", axis=0, tiled=True)


def join_halves(own, other, axis):
    first = lax.axis_index("aux") == 0
    return jnp.where(
        first,
        jnp.concatenate([own, other], axis=axis),
        jnp.concatenate([other, own], axis=axis),
    )


def swapped_core(value):
    return lax.ppermute(value, "aux", [(0, 1), (1, 0)])


def exchange_kernel(x_ref, o_ref, send_sem, recv_sem, local_sem):
    here = {name: lax.axis_index(name) for name in ("aux", "row", "col")}
    me, n = here["row"], lax.axis_size("row")
    depth = x_ref.shape[0] // n
    height = x_ref.shape[1]

    def device(index):
        return (here["aux"], index, here["col"])

    def piece(index):
        return x_ref.at[pl.ds(index * depth, depth)]

    def slot(index):
        return o_ref.at[:, pl.ds(index * height, height)]

    barrier = pltpu.get_barrier_semaphore()
    for step in range(1, n):
        pl.semaphore_signal(
            barrier, inc=1, device_id=device(lax.rem(me + step, n)),
            device_id_type=pl.DeviceIdType.MESH,
        )
    pl.semaphore_wait(barrier, n - 1)

    local = pltpu.make_async_copy(piece(me), slot(me), local_sem)
    local.start()
    sends = []
    for step in range(1, n):
        dest = lax.rem(me + step, n)
        copy = pltpu.make_async_remote_copy(
            src_ref=piece(dest),
            dst_ref=slot(me),
            send_sem=send_sem.at[step],
            recv_sem=recv_sem.at[step],
            device_id=device(dest),
            device_id_type=pl.DeviceIdType.MESH,
        )
        copy.start()
        sends.append(copy)
    for step in range(1, n):
        source = lax.rem(me + n - step, n)
        incoming = pltpu.make_async_remote_copy(
            src_ref=piece(me),
            dst_ref=slot(source),
            send_sem=send_sem.at[step],
            recv_sem=recv_sem.at[step],
            device_id=device(source),
            device_id_type=pl.DeviceIdType.MESH,
        )
        incoming.wait_recv()
        sends[step - 1].wait_send()
    local.wait()


def exchange_rows(x):
    n = lax.axis_size("row")
    shape = (x.shape[0] // n, x.shape[1] * n) + x.shape[2:]
    nbytes = x.size * x.dtype.itemsize
    return pl.pallas_call(
        exchange_kernel,
        out_shape=jax.ShapeDtypeStruct(shape, x.dtype),
        in_specs=[pl.BlockSpec(memory_space=pl.ANY)],
        out_specs=pl.BlockSpec(memory_space=pl.ANY),
        scratch_shapes=[
            pltpu.SemaphoreType.DMA((n,)),
            pltpu.SemaphoreType.DMA((n,)),
            pltpu.SemaphoreType.DMA(()),
        ],
        compiler_params=pltpu.CompilerParams(collective_id=1, has_side_effects=True),
        cost_estimate=pl.CostEstimate(flops=0, bytes_accessed=2 * nbytes, transcendentals=0),
    )(x)


def shards(coulomb, occupied, virtual, tile_mask):
    rows = lax.axis_size("row")
    cols = lax.axis_size("col")
    pdev, mrow, ncol = coulomb.shape
    nao = mrow * rows
    row_idx = lax.axis_index("row")
    col_idx = lax.axis_index("col")
    aux_idx = lax.axis_index("aux")
    tiles_r = mrow // TILE
    tiles_c = ncol // TILE
    local_tiles = lax.dynamic_slice(
        tile_mask, (row_idx * tiles_r, col_idx * tiles_c), (tiles_r, tiles_c)
    )
    local_mask = jnp.repeat(jnp.repeat(local_tiles, TILE, axis=0), TILE, axis=1).astype(
        jnp.bfloat16
    )
    screened = coulomb * local_mask[None]
    occ_own, virt_own = gather_half(occupied), gather_half(virtual)
    moved = exchange_rows(screened)
    occ_own, moved = lax.optimization_barrier((occ_own, moved))
    pieces = moved.shape[0]
    occ_other = swapped_core(occ_own)
    half_own = jnp.einsum("ml,pmn->pln", occ_own, moved, preferred_element_type=jnp.float32)
    half_other = jnp.einsum("ml,pmn->pln", occ_other, moved, preferred_element_type=jnp.float32)
    half = join_halves(half_own.astype(jnp.bfloat16), half_other.astype(jnp.bfloat16), axis=1)
    jpart = mrow // cols
    shaped = half.reshape(pieces, rows, cols, jpart, ncol)
    spread = lax.all_to_all(shaped, "col", split_axis=2, concat_axis=4, tiled=True)
    spread = spread.reshape(pieces, rows * jpart, nao)
    virt_own, spread = lax.optimization_barrier((virt_own, spread))
    virt_all = join_halves(virt_own, swapped_core(virt_own), axis=1)
    dressed = jnp.einsum(
        "pln,ns->pls", spread, virt_all, preferred_element_type=jnp.float32
    ).astype(jnp.bfloat16)
    layered = dressed.reshape(pieces, rows, 1, jpart, cols, ncol)
    returned = lax.all_to_all(
        lax.all_to_all(layered, "row", split_axis=1, concat_axis=0, tiled=True),
        "col",
        split_axis=4,
        concat_axis=2,
        tiled=True,
    )
    aligned = returned.reshape(pdev, mrow, ncol)
    theirs = swapped(screened, "aux", 0)
    with_mine = jnp.einsum("pls,qls->pq", aligned, screened, preferred_element_type=jnp.float32)
    with_theirs = jnp.einsum("pls,qls->pq", aligned, theirs, preferred_element_type=jnp.float32)
    first_half = jnp.where(aux_idx == 0, with_mine, with_theirs)
    second_half = jnp.where(aux_idx == 0, with_theirs, with_mine)
    partial_chi = jnp.concatenate([first_half, second_half], axis=1)
    total_chi = doubling_sum(partial_chi)
    return total_chi / NAO


def solution(mesh):
    placed = (P("aux", "row", "col"), P("row", None), P("row", None), P())
    return jax.shard_map(
        shards, mesh=mesh, in_specs=placed, out_specs=P("aux", None), check_vma=False
    )
```

```python
import functools

import jax
import jax.numpy as jnp
from jax import lax
from jax.sharding import PartitionSpec as P
from jax.experimental import pallas as pl
from jax.experimental.pallas import tpu as pltpu

NAO = 2048
TILE = 128


def swapped(value, axis, apart):
    mask = 2**apart
    pairs = [(source, source ^ mask) for source in range(lax.axis_size(axis))]
    return lax.ppermute(value, axis, pairs)


def partner_rounds():
    rounds = []
    for axis in ("col", "row"):
        bit = 1
        while bit < lax.axis_size(axis):
            rounds.append((axis, bit))
            bit *= 2
    return rounds


def doubling_kernel(rounds, x_ref, o_ref, recv, send_sem, recv_sem):
    here = {name: lax.axis_index(name) for name in ("aux", "row", "col")}

    def partner(axis, bit):
        place = dict(here)
        place[axis] = here[axis] ^ bit
        return (place["aux"], place["row"], place["col"])

    barrier = pltpu.get_barrier_semaphore()
    for axis, bit in rounds:
        pl.semaphore_signal(
            barrier, inc=1, device_id=partner(axis, bit), device_id_type=pl.DeviceIdType.MESH
        )
    pl.semaphore_wait(barrier, len(rounds))

    o_ref[...] = x_ref[...]
    for step, (axis, bit) in enumerate(rounds):
        copy = pltpu.make_async_remote_copy(
            src_ref=o_ref,
            dst_ref=recv.at[step],
            send_sem=send_sem.at[step],
            recv_sem=recv_sem.at[step],
            device_id=partner(axis, bit),
            device_id_type=pl.DeviceIdType.MESH,
        )
        copy.start()
        copy.wait()
        o_ref[...] = o_ref[...] + recv[step]


def doubling_sum(partial):
    rounds = partner_rounds()
    return pl.pallas_call(
        functools.partial(doubling_kernel, rounds),
        out_shape=jax.ShapeDtypeStruct(partial.shape, partial.dtype),
        in_specs=[pl.BlockSpec(memory_space=pltpu.VMEM)],
        out_specs=pl.BlockSpec(memory_space=pltpu.VMEM),
        scratch_shapes=[
            pltpu.VMEM((len(rounds),) + partial.shape, partial.dtype),
            pltpu.SemaphoreType.DMA((len(rounds),)),
            pltpu.SemaphoreType.DMA((len(rounds),)),
        ],
        compiler_params=pltpu.CompilerParams(collective_id=0, has_side_effects=True),
    )(partial)


def gather_half(local):
    width = local.shape[1] // 2
    part = lax.dynamic_slice_in_dim(local, lax.axis_index("aux") * width, width, axis=1)
    return lax.all_gather(part, "row", axis=0, tiled=True)


def join_halves(own, other, axis):
    first = lax.axis_index("aux") == 0
    return jnp.where(
        first,
        jnp.concatenate([own, other], axis=axis),
        jnp.concatenate([other, own], axis=axis),
    )


def swapped_core(value):
    return lax.ppermute(value, "aux", [(0, 1), (1, 0)])


def sliced(ref, axis, start, size):
    index = [slice(None)] * len(ref.shape)
    index[axis] = pl.ds(start, size)
    return ref.at[tuple(index)]


def exchange_kernel(split_axis, concat_axis, x_ref, o_ref, send_sem, recv_sem, local_sem):
    here = {name: lax.axis_index(name) for name in ("aux", "row", "col")}
    me, n = here["row"], lax.axis_size("row")
    depth = x_ref.shape[split_axis] // n
    height = o_ref.shape[concat_axis] // n

    def device(index):
        return (here["aux"], index, here["col"])

    def piece(index):
        return sliced(x_ref, split_axis, index * depth, depth)

    def slot(index):
        return sliced(o_ref, concat_axis, index * height, height)

    barrier = pltpu.get_barrier_semaphore()
    for step in range(1, n):
        pl.semaphore_signal(
            barrier, inc=1, device_id=device(lax.rem(me + step, n)),
            device_id_type=pl.DeviceIdType.MESH,
        )
    pl.semaphore_wait(barrier, n - 1)

    local = pltpu.make_async_copy(piece(me), slot(me), local_sem)
    local.start()
    sends = []
    for step in range(1, n):
        dest = lax.rem(me + step, n)
        copy = pltpu.make_async_remote_copy(
            src_ref=piece(dest),
            dst_ref=slot(me),
            send_sem=send_sem.at[step],
            recv_sem=recv_sem.at[step],
            device_id=device(dest),
            device_id_type=pl.DeviceIdType.MESH,
        )
        copy.start()
        sends.append(copy)
    for step in range(1, n):
        source = lax.rem(me + n - step, n)
        incoming = pltpu.make_async_remote_copy(
            src_ref=piece(me),
            dst_ref=slot(source),
            send_sem=send_sem.at[step],
            recv_sem=recv_sem.at[step],
            device_id=device(source),
            device_id_type=pl.DeviceIdType.MESH,
        )
        incoming.wait_recv()
        sends[step - 1].wait_send()
    local.wait()


def exchange_rows(x, split_axis, concat_axis, collective_id):
    n = lax.axis_size("row")
    shape = list(x.shape)
    shape[split_axis] //= n
    shape[concat_axis] *= n
    nbytes = x.size * x.dtype.itemsize
    return pl.pallas_call(
        functools.partial(exchange_kernel, split_axis, concat_axis),
        out_shape=jax.ShapeDtypeStruct(tuple(shape), x.dtype),
        in_specs=[pl.BlockSpec(memory_space=pl.ANY)],
        out_specs=pl.BlockSpec(memory_space=pl.ANY),
        scratch_shapes=[
            pltpu.SemaphoreType.DMA((n,)),
            pltpu.SemaphoreType.DMA((n,)),
            pltpu.SemaphoreType.DMA(()),
        ],
        compiler_params=pltpu.CompilerParams(
            collective_id=collective_id, has_side_effects=True
        ),
        cost_estimate=pl.CostEstimate(flops=0, bytes_accessed=2 * nbytes, transcendentals=0),
    )(x)


def shards(coulomb, occupied, virtual, tile_mask):
    rows = lax.axis_size("row")
    cols = lax.axis_size("col")
    pdev, mrow, ncol = coulomb.shape
    nao = mrow * rows
    row_idx = lax.axis_index("row")
    col_idx = lax.axis_index("col")
    aux_idx = lax.axis_index("aux")
    tiles_r = mrow // TILE
    tiles_c = ncol // TILE
    local_tiles = lax.dynamic_slice(
        tile_mask, (row_idx * tiles_r, col_idx * tiles_c), (tiles_r, tiles_c)
    )
    local_mask = jnp.repeat(jnp.repeat(local_tiles, TILE, axis=0), TILE, axis=1).astype(
        jnp.bfloat16
    )
    screened = coulomb * local_mask[None]
    occ_own, virt_own = gather_half(occupied), gather_half(virtual)
    moved = exchange_rows(screened, 0, 1, 1)
    occ_own, moved = lax.optimization_barrier((occ_own, moved))
    pieces = moved.shape[0]
    occ_other = swapped_core(occ_own)
    half_own = jnp.einsum("ml,pmn->pln", occ_own, moved, preferred_element_type=jnp.float32)
    half_other = jnp.einsum("ml,pmn->pln", occ_other, moved, preferred_element_type=jnp.float32)
    half = join_halves(half_own.astype(jnp.bfloat16), half_other.astype(jnp.bfloat16), axis=1)
    jpart = mrow // cols
    shaped = half.reshape(pieces, rows, cols, jpart, ncol)
    spread = lax.all_to_all(shaped, "col", split_axis=2, concat_axis=4, tiled=True)
    spread = spread.reshape(pieces, rows * jpart, nao)
    virt_own, spread = lax.optimization_barrier((virt_own, spread))
    virt_all = join_halves(virt_own, swapped_core(virt_own), axis=1)
    dressed = jnp.einsum(
        "pln,ns->pls", spread, virt_all, preferred_element_type=jnp.float32
    ).astype(jnp.bfloat16)
    by_row = exchange_rows(dressed, 1, 0, 2).reshape(pdev, 1, 1, jpart, cols, ncol)
    returned = lax.all_to_all(
        by_row,
        "col",
        split_axis=4,
        concat_axis=2,
        tiled=True,
    )
    aligned = returned.reshape(pdev, mrow, ncol)
    theirs = swapped(screened, "aux", 0)
    with_mine = jnp.einsum("pls,qls->pq", aligned, screened, preferred_element_type=jnp.float32)
    with_theirs = jnp.einsum("pls,qls->pq", aligned, theirs, preferred_element_type=jnp.float32)
    first_half = jnp.where(aux_idx == 0, with_mine, with_theirs)
    second_half = jnp.where(aux_idx == 0, with_theirs, with_mine)
    partial_chi = jnp.concatenate([first_half, second_half], axis=1)
    total_chi = doubling_sum(partial_chi)
    return total_chi / NAO


def solution(mesh):
    placed = (P("aux", "row", "col"), P("row", None), P("row", None), P())
    return jax.shard_map(
        shards, mesh=mesh, in_specs=placed, out_specs=P("aux", None), check_vma=False
    )
```

```python
import functools

import jax
import jax.numpy as jnp
from jax import lax
from jax.sharding import PartitionSpec as P
from jax.experimental import pallas as pl
from jax.experimental.pallas import tpu as pltpu

NAO = 2048
TILE = 128


def swapped(value, axis, apart):
    mask = 2**apart
    pairs = [(source, source ^ mask) for source in range(lax.axis_size(axis))]
    return lax.ppermute(value, axis, pairs)


def gather_round(axis, here, own, slots, send_sem, recv_sem):
    me, n = here[axis], lax.axis_size(axis)

    def device(index):
        place = dict(here)
        place[axis] = index
        return (place["aux"], place["row"], place["col"])

    slots[me] = own
    sends = []
    for step in range(1, n):
        dest = lax.rem(me + step, n)
        copy = pltpu.make_async_remote_copy(
            src_ref=slots.at[me],
            dst_ref=slots.at[me],
            send_sem=send_sem.at[step],
            recv_sem=recv_sem.at[step],
            device_id=device(dest),
            device_id_type=pl.DeviceIdType.MESH,
        )
        copy.start()
        sends.append(copy)
    for step in range(1, n):
        source = lax.rem(me + n - step, n)
        incoming = pltpu.make_async_remote_copy(
            src_ref=slots.at[me],
            dst_ref=slots.at[source],
            send_sem=send_sem.at[step],
            recv_sem=recv_sem.at[step],
            device_id=device(source),
            device_id_type=pl.DeviceIdType.MESH,
        )
        incoming.wait_recv()
        sends[step - 1].wait_send()
    total = slots[0]
    for index in range(1, n):
        total = total + slots[index]
    return total


def two_round_kernel(x_ref, o_ref, col_slots, row_slots, send_a, recv_a, send_b, recv_b):
    here = {name: lax.axis_index(name) for name in ("aux", "row", "col")}
    peers = []
    for axis in ("col", "row"):
        n = lax.axis_size(axis)
        for step in range(1, n):
            place = dict(here)
            place[axis] = lax.rem(here[axis] + step, n)
            peers.append((place["aux"], place["row"], place["col"]))
    barrier = pltpu.get_barrier_semaphore()
    for peer in peers:
        pl.semaphore_signal(barrier, inc=1, device_id=peer, device_id_type=pl.DeviceIdType.MESH)
    pl.semaphore_wait(barrier, len(peers))
    by_col = gather_round("col", here, x_ref[...], col_slots, send_a, recv_a)
    o_ref[...] = gather_round("row", here, by_col, row_slots, send_b, recv_b)


def doubling_sum(partial):
    cols, rows = lax.axis_size("col"), lax.axis_size("row")
    return pl.pallas_call(
        two_round_kernel,
        out_shape=jax.ShapeDtypeStruct(partial.shape, partial.dtype),
        in_specs=[pl.BlockSpec(memory_space=pltpu.VMEM)],
        out_specs=pl.BlockSpec(memory_space=pltpu.VMEM),
        scratch_shapes=[
            pltpu.VMEM((cols,) + partial.shape, partial.dtype),
            pltpu.VMEM((rows,) + partial.shape, partial.dtype),
            pltpu.SemaphoreType.DMA((cols,)),
            pltpu.SemaphoreType.DMA((cols,)),
            pltpu.SemaphoreType.DMA((rows,)),
            pltpu.SemaphoreType.DMA((rows,)),
        ],
        compiler_params=pltpu.CompilerParams(collective_id=0, has_side_effects=True),
    )(partial)


def gather_half(local):
    width = local.shape[1] // 2
    part = lax.dynamic_slice_in_dim(local, lax.axis_index("aux") * width, width, axis=1)
    return lax.all_gather(part, "row", axis=0, tiled=True)


def join_halves(own, other, axis):
    first = lax.axis_index("aux") == 0
    return jnp.where(
        first,
        jnp.concatenate([own, other], axis=axis),
        jnp.concatenate([other, own], axis=axis),
    )


def swapped_core(value):
    return lax.ppermute(value, "aux", [(0, 1), (1, 0)])


def exchange_kernel(x_ref, o_ref, send_sem, recv_sem, local_sem):
    here = {name: lax.axis_index(name) for name in ("aux", "row", "col")}
    me, n = here["row"], lax.axis_size("row")
    depth = x_ref.shape[0] // n
    height = x_ref.shape[1]

    def device(index):
        return (here["aux"], index, here["col"])

    def piece(index):
        return x_ref.at[pl.ds(index * depth, depth)]

    def slot(index):
        return o_ref.at[:, pl.ds(index * height, height)]

    barrier = pltpu.get_barrier_semaphore()
    for step in range(1, n):
        pl.semaphore_signal(
            barrier, inc=1, device_id=device(lax.rem(me + step, n)),
            device_id_type=pl.DeviceIdType.MESH,
        )
    pl.semaphore_wait(barrier, n - 1)

    local = pltpu.make_async_copy(piece(me), slot(me), local_sem)
    local.start()
    sends = []
    for step in range(1, n):
        dest = lax.rem(me + step, n)
        copy = pltpu.make_async_remote_copy(
            src_ref=piece(dest),
            dst_ref=slot(me),
            send_sem=send_sem.at[step],
            recv_sem=recv_sem.at[step],
            device_id=device(dest),
            device_id_type=pl.DeviceIdType.MESH,
        )
        copy.start()
        sends.append(copy)
    for step in range(1, n):
        source = lax.rem(me + n - step, n)
        incoming = pltpu.make_async_remote_copy(
            src_ref=piece(me),
            dst_ref=slot(source),
            send_sem=send_sem.at[step],
            recv_sem=recv_sem.at[step],
            device_id=device(source),
            device_id_type=pl.DeviceIdType.MESH,
        )
        incoming.wait_recv()
        sends[step - 1].wait_send()
    local.wait()


def exchange_rows(x):
    n = lax.axis_size("row")
    shape = (x.shape[0] // n, x.shape[1] * n) + x.shape[2:]
    nbytes = x.size * x.dtype.itemsize
    return pl.pallas_call(
        exchange_kernel,
        out_shape=jax.ShapeDtypeStruct(shape, x.dtype),
        in_specs=[pl.BlockSpec(memory_space=pl.ANY)],
        out_specs=pl.BlockSpec(memory_space=pl.ANY),
        scratch_shapes=[
            pltpu.SemaphoreType.DMA((n,)),
            pltpu.SemaphoreType.DMA((n,)),
            pltpu.SemaphoreType.DMA(()),
        ],
        compiler_params=pltpu.CompilerParams(collective_id=1, has_side_effects=True),
        cost_estimate=pl.CostEstimate(flops=0, bytes_accessed=2 * nbytes, transcendentals=0),
    )(x)


def shards(coulomb, occupied, virtual, tile_mask):
    rows = lax.axis_size("row")
    cols = lax.axis_size("col")
    pdev, mrow, ncol = coulomb.shape
    nao = mrow * rows
    row_idx = lax.axis_index("row")
    col_idx = lax.axis_index("col")
    aux_idx = lax.axis_index("aux")
    tiles_r = mrow // TILE
    tiles_c = ncol // TILE
    local_tiles = lax.dynamic_slice(
        tile_mask, (row_idx * tiles_r, col_idx * tiles_c), (tiles_r, tiles_c)
    )
    local_mask = jnp.repeat(jnp.repeat(local_tiles, TILE, axis=0), TILE, axis=1).astype(
        jnp.bfloat16
    )
    screened = coulomb * local_mask[None]
    occ_own, virt_own = gather_half(occupied), gather_half(virtual)
    moved = exchange_rows(screened)
    occ_own, moved = lax.optimization_barrier((occ_own, moved))
    pieces = moved.shape[0]
    occ_other = swapped_core(occ_own)
    half_own = jnp.einsum("ml,pmn->pln", occ_own, moved, preferred_element_type=jnp.float32)
    half_other = jnp.einsum("ml,pmn->pln", occ_other, moved, preferred_element_type=jnp.float32)
    half = join_halves(half_own.astype(jnp.bfloat16), half_other.astype(jnp.bfloat16), axis=1)
    jpart = mrow // cols
    shaped = half.reshape(pieces, rows, cols, jpart, ncol)
    spread = lax.all_to_all(shaped, "col", split_axis=2, concat_axis=4, tiled=True)
    spread = spread.reshape(pieces, rows * jpart, nao)
    virt_own, spread = lax.optimization_barrier((virt_own, spread))
    virt_all = join_halves(virt_own, swapped_core(virt_own), axis=1)
    dressed = jnp.einsum(
        "pln,ns->pls", spread, virt_all, preferred_element_type=jnp.float32
    ).astype(jnp.bfloat16)
    layered = dressed.reshape(pieces, rows, 1, jpart, cols, ncol)
    returned = lax.all_to_all(
        lax.all_to_all(layered, "row", split_axis=1, concat_axis=0, tiled=True),
        "col",
        split_axis=4,
        concat_axis=2,
        tiled=True,
    )
    aligned = returned.reshape(pdev, mrow, ncol)
    theirs = swapped(screened, "aux", 0)
    with_mine = jnp.einsum("pls,qls->pq", aligned, screened, preferred_element_type=jnp.float32)
    with_theirs = jnp.einsum("pls,qls->pq", aligned, theirs, preferred_element_type=jnp.float32)
    first_half = jnp.where(aux_idx == 0, with_mine, with_theirs)
    second_half = jnp.where(aux_idx == 0, with_theirs, with_mine)
    partial_chi = jnp.concatenate([first_half, second_half], axis=1)
    total_chi = doubling_sum(partial_chi)
    return total_chi / NAO


def solution(mesh):
    placed = (P("aux", "row", "col"), P("row", None), P("row", None), P())
    return jax.shard_map(
        shards, mesh=mesh, in_specs=placed, out_specs=P("aux", None), check_vma=False
    )
```

```python
import functools

import jax
import jax.numpy as jnp
from jax import lax
from jax.sharding import PartitionSpec as P
from jax.experimental import pallas as pl
from jax.experimental.pallas import tpu as pltpu

NAO = 2048
TILE = 128


def swapped(value, axis, apart):
    mask = 2**apart
    pairs = [(source, source ^ mask) for source in range(lax.axis_size(axis))]
    return lax.ppermute(value, axis, pairs)


def gather_round(axis, here, own, slots, send_sem, recv_sem):
    me, n = here[axis], lax.axis_size(axis)

    def device(index):
        place = dict(here)
        place[axis] = index
        return (place["aux"], place["row"], place["col"])

    slots[me] = own
    sends = []
    for step in range(1, n):
        dest = lax.rem(me + step, n)
        copy = pltpu.make_async_remote_copy(
            src_ref=slots.at[me],
            dst_ref=slots.at[me],
            send_sem=send_sem.at[step],
            recv_sem=recv_sem.at[step],
            device_id=device(dest),
            device_id_type=pl.DeviceIdType.MESH,
        )
        copy.start()
        sends.append(copy)
    for step in range(1, n):
        source = lax.rem(me + n - step, n)
        incoming = pltpu.make_async_remote_copy(
            src_ref=slots.at[me],
            dst_ref=slots.at[source],
            send_sem=send_sem.at[step],
            recv_sem=recv_sem.at[step],
            device_id=device(source),
            device_id_type=pl.DeviceIdType.MESH,
        )
        incoming.wait_recv()
        sends[step - 1].wait_send()
    total = slots[0]
    for index in range(1, n):
        total = total + slots[index]
    return total


def two_round_kernel(x_ref, o_ref, col_slots, row_slots, send_a, recv_a, send_b, recv_b):
    here = {name: lax.axis_index(name) for name in ("aux", "row", "col")}
    peers = []
    for axis in ("col", "row"):
        n = lax.axis_size(axis)
        for step in range(1, n):
            place = dict(here)
            place[axis] = lax.rem(here[axis] + step, n)
            peers.append((place["aux"], place["row"], place["col"]))
    barrier = pltpu.get_barrier_semaphore()
    for peer in peers:
        pl.semaphore_signal(barrier, inc=1, device_id=peer, device_id_type=pl.DeviceIdType.MESH)
    pl.semaphore_wait(barrier, len(peers))
    by_col = gather_round("col", here, x_ref[...], col_slots, send_a, recv_a)
    o_ref[...] = gather_round("row", here, by_col, row_slots, send_b, recv_b)


def doubling_sum(partial):
    cols, rows = lax.axis_size("col"), lax.axis_size("row")
    return pl.pallas_call(
        two_round_kernel,
        out_shape=jax.ShapeDtypeStruct(partial.shape, partial.dtype),
        in_specs=[pl.BlockSpec(memory_space=pltpu.VMEM)],
        out_specs=pl.BlockSpec(memory_space=pltpu.VMEM),
        scratch_shapes=[
            pltpu.VMEM((cols,) + partial.shape, partial.dtype),
            pltpu.VMEM((rows,) + partial.shape, partial.dtype),
            pltpu.SemaphoreType.DMA((cols,)),
            pltpu.SemaphoreType.DMA((cols,)),
            pltpu.SemaphoreType.DMA((rows,)),
            pltpu.SemaphoreType.DMA((rows,)),
        ],
        compiler_params=pltpu.CompilerParams(collective_id=0, has_side_effects=True),
    )(partial)


def gather_half(local):
    width = local.shape[1] // 2
    part = lax.dynamic_slice_in_dim(local, lax.axis_index("aux") * width, width, axis=1)
    return lax.all_gather(part, "row", axis=0, tiled=True)


def join_halves(own, other, axis):
    first = lax.axis_index("aux") == 0
    return jnp.where(
        first,
        jnp.concatenate([own, other], axis=axis),
        jnp.concatenate([other, own], axis=axis),
    )


def swapped_core(value):
    return lax.ppermute(value, "aux", [(0, 1), (1, 0)])


def sliced(ref, axis, start, size):
    index = [slice(None)] * len(ref.shape)
    index[axis] = pl.ds(start, size)
    return ref.at[tuple(index)]


def exchange_kernel(mesh_axis, split_axis, concat_axis, x_ref, o_ref, send_sem, recv_sem, local_sem):
    here = {name: lax.axis_index(name) for name in ("aux", "row", "col")}
    me, n = here[mesh_axis], lax.axis_size(mesh_axis)
    depth = x_ref.shape[split_axis] // n
    height = o_ref.shape[concat_axis] // n

    def device(index):
        place = dict(here)
        place[mesh_axis] = index
        return (place["aux"], place["row"], place["col"])

    def piece(index):
        return sliced(x_ref, split_axis, index * depth, depth)

    def slot(index):
        return sliced(o_ref, concat_axis, index * height, height)

    barrier = pltpu.get_barrier_semaphore()
    for step in range(1, n):
        pl.semaphore_signal(
            barrier, inc=1, device_id=device(lax.rem(me + step, n)),
            device_id_type=pl.DeviceIdType.MESH,
        )
    pl.semaphore_wait(barrier, n - 1)

    local = pltpu.make_async_copy(piece(me), slot(me), local_sem)
    local.start()
    sends = []
    for step in range(1, n):
        dest = lax.rem(me + step, n)
        copy = pltpu.make_async_remote_copy(
            src_ref=piece(dest),
            dst_ref=slot(me),
            send_sem=send_sem.at[step],
            recv_sem=recv_sem.at[step],
            device_id=device(dest),
            device_id_type=pl.DeviceIdType.MESH,
        )
        copy.start()
        sends.append(copy)
    for step in range(1, n):
        source = lax.rem(me + n - step, n)
        incoming = pltpu.make_async_remote_copy(
            src_ref=piece(me),
            dst_ref=slot(source),
            send_sem=send_sem.at[step],
            recv_sem=recv_sem.at[step],
            device_id=device(source),
            device_id_type=pl.DeviceIdType.MESH,
        )
        incoming.wait_recv()
        sends[step - 1].wait_send()
    local.wait()


def exchange(x, mesh_axis, split_axis, concat_axis, collective_id):
    n = lax.axis_size(mesh_axis)
    shape = list(x.shape)
    shape[split_axis] //= n
    shape[concat_axis] *= n
    nbytes = x.size * x.dtype.itemsize
    return pl.pallas_call(
        functools.partial(exchange_kernel, mesh_axis, split_axis, concat_axis),
        out_shape=jax.ShapeDtypeStruct(tuple(shape), x.dtype),
        in_specs=[pl.BlockSpec(memory_space=pl.ANY)],
        out_specs=pl.BlockSpec(memory_space=pl.ANY),
        scratch_shapes=[
            pltpu.SemaphoreType.DMA((n,)),
            pltpu.SemaphoreType.DMA((n,)),
            pltpu.SemaphoreType.DMA(()),
        ],
        compiler_params=pltpu.CompilerParams(
            collective_id=collective_id, has_side_effects=True
        ),
        cost_estimate=pl.CostEstimate(flops=0, bytes_accessed=2 * nbytes, transcendentals=0),
    )(x)


def shards(coulomb, occupied, virtual, tile_mask):
    rows = lax.axis_size("row")
    cols = lax.axis_size("col")
    pdev, mrow, ncol = coulomb.shape
    nao = mrow * rows
    row_idx = lax.axis_index("row")
    col_idx = lax.axis_index("col")
    aux_idx = lax.axis_index("aux")
    tiles_r = mrow // TILE
    tiles_c = ncol // TILE
    local_tiles = lax.dynamic_slice(
        tile_mask, (row_idx * tiles_r, col_idx * tiles_c), (tiles_r, tiles_c)
    )
    local_mask = jnp.repeat(jnp.repeat(local_tiles, TILE, axis=0), TILE, axis=1).astype(
        jnp.bfloat16
    )
    screened = coulomb * local_mask[None]
    occ_own, virt_own = gather_half(occupied), gather_half(virtual)
    moved = exchange(screened, "row", 0, 1, 1)
    occ_own, moved = lax.optimization_barrier((occ_own, moved))
    pieces = moved.shape[0]
    occ_other = swapped_core(occ_own)
    half_own = jnp.einsum("ml,pmn->pln", occ_own, moved, preferred_element_type=jnp.float32)
    half_other = jnp.einsum("ml,pmn->pln", occ_other, moved, preferred_element_type=jnp.float32)
    half = join_halves(half_own.astype(jnp.bfloat16), half_other.astype(jnp.bfloat16), axis=1)
    jpart = mrow // cols
    shaped = half.reshape(pieces, rows, mrow, ncol)
    spread = exchange(shaped, "col", 2, 3, 3).reshape(pieces, rows * jpart, nao)
    virt_own, spread = lax.optimization_barrier((virt_own, spread))
    virt_all = join_halves(virt_own, swapped_core(virt_own), axis=1)
    dressed = jnp.einsum(
        "pln,ns->pls", spread, virt_all, preferred_element_type=jnp.float32
    ).astype(jnp.bfloat16)
    by_row = exchange(dressed, "row", 1, 0, 2)
    aligned = exchange(by_row, "col", 2, 1, 4)
    theirs = swapped(screened, "aux", 0)
    with_mine = jnp.einsum("pls,qls->pq", aligned, screened, preferred_element_type=jnp.float32)
    with_theirs = jnp.einsum("pls,qls->pq", aligned, theirs, preferred_element_type=jnp.float32)
    first_half = jnp.where(aux_idx == 0, with_mine, with_theirs)
    second_half = jnp.where(aux_idx == 0, with_theirs, with_mine)
    partial_chi = jnp.concatenate([first_half, second_half], axis=1)
    total_chi = doubling_sum(partial_chi)
    return total_chi / NAO


def solution(mesh):
    placed = (P("aux", "row", "col"), P("row", None), P("row", None), P())
    return jax.shard_map(
        shards, mesh=mesh, in_specs=placed, out_specs=P("aux", None), check_vma=False
    )
```

```python
import functools

import jax
import jax.numpy as jnp
from jax import lax
from jax.sharding import PartitionSpec as P
from jax.experimental import pallas as pl
from jax.experimental.pallas import tpu as pltpu

NAO = 2048
TILE = 128


def swapped(value, axis, apart):
    mask = 2**apart
    pairs = [(source, source ^ mask) for source in range(lax.axis_size(axis))]
    return lax.ppermute(value, axis, pairs)


def gather_round(axis, here, own, slots, send_sem, recv_sem):
    me, n = here[axis], lax.axis_size(axis)

    def device(index):
        place = dict(here)
        place[axis] = index
        return (place["aux"], place["row"], place["col"])

    slots[me] = own
    sends = []
    for step in range(1, n):
        dest = lax.rem(me + step, n)
        copy = pltpu.make_async_remote_copy(
            src_ref=slots.at[me],
            dst_ref=slots.at[me],
            send_sem=send_sem.at[step],
            recv_sem=recv_sem.at[step],
            device_id=device(dest),
            device_id_type=pl.DeviceIdType.MESH,
        )
        copy.start()
        sends.append(copy)
    for step in range(1, n):
        source = lax.rem(me + n - step, n)
        incoming = pltpu.make_async_remote_copy(
            src_ref=slots.at[me],
            dst_ref=slots.at[source],
            send_sem=send_sem.at[step],
            recv_sem=recv_sem.at[step],
            device_id=device(source),
            device_id_type=pl.DeviceIdType.MESH,
        )
        incoming.wait_recv()
        sends[step - 1].wait_send()
    total = slots[0]
    for index in range(1, n):
        total = total + slots[index]
    return total


def two_round_kernel(x_ref, o_ref, col_slots, row_slots, send_a, recv_a, send_b, recv_b):
    here = {name: lax.axis_index(name) for name in ("aux", "row", "col")}
    peers = []
    for axis in ("col", "row"):
        n = lax.axis_size(axis)
        for step in range(1, n):
            place = dict(here)
            place[axis] = lax.rem(here[axis] + step, n)
            peers.append((place["aux"], place["row"], place["col"]))
    barrier = pltpu.get_barrier_semaphore()
    for peer in peers:
        pl.semaphore_signal(barrier, inc=1, device_id=peer, device_id_type=pl.DeviceIdType.MESH)
    pl.semaphore_wait(barrier, len(peers))
    by_col = gather_round("col", here, x_ref[...], col_slots, send_a, recv_a)
    o_ref[...] = gather_round("row", here, by_col, row_slots, send_b, recv_b)


def doubling_sum(partial):
    cols, rows = lax.axis_size("col"), lax.axis_size("row")
    return pl.pallas_call(
        two_round_kernel,
        out_shape=jax.ShapeDtypeStruct(partial.shape, partial.dtype),
        in_specs=[pl.BlockSpec(memory_space=pltpu.VMEM)],
        out_specs=pl.BlockSpec(memory_space=pltpu.VMEM),
        scratch_shapes=[
            pltpu.VMEM((cols,) + partial.shape, partial.dtype),
            pltpu.VMEM((rows,) + partial.shape, partial.dtype),
            pltpu.SemaphoreType.DMA((cols,)),
            pltpu.SemaphoreType.DMA((cols,)),
            pltpu.SemaphoreType.DMA((rows,)),
            pltpu.SemaphoreType.DMA((rows,)),
        ],
        compiler_params=pltpu.CompilerParams(collective_id=0, has_side_effects=True),
    )(partial)


def gather_half(local):
    width = local.shape[1] // 2
    part = lax.dynamic_slice_in_dim(local, lax.axis_index("aux") * width, width, axis=1)
    return lax.all_gather(part, "row", axis=0, tiled=True)


def join_halves(own, other, axis):
    first = lax.axis_index("aux") == 0
    return jnp.where(
        first,
        jnp.concatenate([own, other], axis=axis),
        jnp.concatenate([other, own], axis=axis),
    )


def swapped_core(value):
    return lax.ppermute(value, "aux", [(0, 1), (1, 0)])


def exchange_kernel(x_ref, o_ref, send_sem, recv_sem, local_sem):
    here = {name: lax.axis_index(name) for name in ("aux", "row", "col")}
    me, n = here["row"], lax.axis_size("row")
    depth = x_ref.shape[0] // n
    height = x_ref.shape[1]

    def device(index):
        return (here["aux"], index, here["col"])

    def piece(index):
        return x_ref.at[pl.ds(index * depth, depth)]

    def slot(index):
        return o_ref.at[:, pl.ds(index * height, height)]

    barrier = pltpu.get_barrier_semaphore()
    for step in range(1, n):
        pl.semaphore_signal(
            barrier, inc=1, device_id=device(lax.rem(me + step, n)),
            device_id_type=pl.DeviceIdType.MESH,
        )
    pl.semaphore_wait(barrier, n - 1)

    local = pltpu.make_async_copy(piece(me), slot(me), local_sem)
    local.start()
    sends = []
    for step in range(1, n):
        dest = lax.rem(me + step, n)
        copy = pltpu.make_async_remote_copy(
            src_ref=piece(dest),
            dst_ref=slot(me),
            send_sem=send_sem.at[step],
            recv_sem=recv_sem.at[step],
            device_id=device(dest),
            device_id_type=pl.DeviceIdType.MESH,
        )
        copy.start()
        sends.append(copy)
    for step in range(1, n):
        source = lax.rem(me + n - step, n)
        incoming = pltpu.make_async_remote_copy(
            src_ref=piece(me),
            dst_ref=slot(source),
            send_sem=send_sem.at[step],
            recv_sem=recv_sem.at[step],
            device_id=device(source),
            device_id_type=pl.DeviceIdType.MESH,
        )
        incoming.wait_recv()
        sends[step - 1].wait_send()
    local.wait()


def exchange_rows(x):
    n = lax.axis_size("row")
    shape = (x.shape[0] // n, x.shape[1] * n) + x.shape[2:]
    nbytes = x.size * x.dtype.itemsize
    return pl.pallas_call(
        exchange_kernel,
        out_shape=jax.ShapeDtypeStruct(shape, x.dtype),
        in_specs=[pl.BlockSpec(memory_space=pl.ANY)],
        out_specs=pl.BlockSpec(memory_space=pl.ANY),
        scratch_shapes=[
            pltpu.SemaphoreType.DMA((n,)),
            pltpu.SemaphoreType.DMA((n,)),
            pltpu.SemaphoreType.DMA(()),
        ],
        compiler_params=pltpu.CompilerParams(collective_id=1, has_side_effects=True),
        cost_estimate=pl.CostEstimate(flops=0, bytes_accessed=2 * nbytes, transcendentals=0),
    )(x)


def shards(coulomb, occupied, virtual, tile_mask):
    rows = lax.axis_size("row")
    cols = lax.axis_size("col")
    pdev, mrow, ncol = coulomb.shape
    nao = mrow * rows
    row_idx = lax.axis_index("row")
    col_idx = lax.axis_index("col")
    aux_idx = lax.axis_index("aux")
    tiles_r = mrow // TILE
    tiles_c = ncol // TILE
    local_tiles = lax.dynamic_slice(
        tile_mask, (row_idx * tiles_r, col_idx * tiles_c), (tiles_r, tiles_c)
    )
    local_mask = jnp.repeat(jnp.repeat(local_tiles, TILE, axis=0), TILE, axis=1).astype(
        jnp.bfloat16
    )
    screened = coulomb * local_mask[None]
    occ_own, virt_own = gather_half(occupied), gather_half(virtual)
    moved = exchange_rows(screened)
    occ_own, moved = lax.optimization_barrier((occ_own, moved))
    pieces = moved.shape[0]
    occ_other = swapped_core(occ_own)
    half_own = jnp.einsum("ml,pmn->pln", occ_own, moved, preferred_element_type=jnp.float32)
    half_other = jnp.einsum("ml,pmn->pln", occ_other, moved, preferred_element_type=jnp.float32)
    half = join_halves(half_own.astype(jnp.bfloat16), half_other.astype(jnp.bfloat16), axis=1)
    jpart = mrow // cols
    shaped = half.reshape(pieces, rows, cols, jpart, ncol)
    spread = lax.all_to_all(shaped, "col", split_axis=2, concat_axis=4, tiled=True)
    spread = spread.reshape(pieces, rows * jpart, nao)
    virt_own, spread = lax.optimization_barrier((virt_own, spread))
    virt_other = swapped_core(virt_own)
    dressed_own = jnp.einsum("pln,ns->pls", spread, virt_own, preferred_element_type=jnp.float32)
    dressed_other = jnp.einsum(
        "pln,ns->pls", spread, virt_other, preferred_element_type=jnp.float32
    )
    dressed = join_halves(
        dressed_own.astype(jnp.bfloat16), dressed_other.astype(jnp.bfloat16), axis=2
    )
    layered = dressed.reshape(pieces, rows, 1, jpart, cols, ncol)
    returned = lax.all_to_all(
        lax.all_to_all(layered, "row", split_axis=1, concat_axis=0, tiled=True),
        "col",
        split_axis=4,
        concat_axis=2,
        tiled=True,
    )
    aligned = returned.reshape(pdev, mrow, ncol)
    theirs = swapped(screened, "aux", 0)
    with_mine = jnp.einsum("pls,qls->pq", aligned, screened, preferred_element_type=jnp.float32)
    with_theirs = jnp.einsum("pls,qls->pq", aligned, theirs, preferred_element_type=jnp.float32)
    first_half = jnp.where(aux_idx == 0, with_mine, with_theirs)
    second_half = jnp.where(aux_idx == 0, with_theirs, with_mine)
    partial_chi = jnp.concatenate([first_half, second_half], axis=1)
    total_chi = doubling_sum(partial_chi)
    return total_chi / NAO


def solution(mesh):
    placed = (P("aux", "row", "col"), P("row", None), P("row", None), P())
    return jax.shard_map(
        shards, mesh=mesh, in_specs=placed, out_specs=P("aux", None), check_vma=False
    )
```

```python
import functools

import jax
import jax.numpy as jnp
from jax import lax
from jax.sharding import PartitionSpec as P
from jax.experimental import pallas as pl
from jax.experimental.pallas import tpu as pltpu

NAO = 2048
TILE = 128


def swapped(value, axis, apart):
    mask = 2**apart
    pairs = [(source, source ^ mask) for source in range(lax.axis_size(axis))]
    return lax.ppermute(value, axis, pairs)


def gather_round(axis, here, own, slots, send_sem, recv_sem):
    me, n = here[axis], lax.axis_size(axis)

    def device(index):
        place = dict(here)
        place[axis] = index
        return (place["aux"], place["row"], place["col"])

    slots[me] = own
    sends = []
    for step in range(1, n):
        dest = lax.rem(me + step, n)
        copy = pltpu.make_async_remote_copy(
            src_ref=slots.at[me],
            dst_ref=slots.at[me],
            send_sem=send_sem.at[step],
            recv_sem=recv_sem.at[step],
            device_id=device(dest),
            device_id_type=pl.DeviceIdType.MESH,
        )
        copy.start()
        sends.append(copy)
    for step in range(1, n):
        source = lax.rem(me + n - step, n)
        incoming = pltpu.make_async_remote_copy(
            src_ref=slots.at[me],
            dst_ref=slots.at[source],
            send_sem=send_sem.at[step],
            recv_sem=recv_sem.at[step],
            device_id=device(source),
            device_id_type=pl.DeviceIdType.MESH,
        )
        incoming.wait_recv()
        sends[step - 1].wait_send()
    total = slots[0]
    for index in range(1, n):
        total = total + slots[index]
    return total


def two_round_kernel(x_ref, o_ref, col_slots, row_slots, send_a, recv_a, send_b, recv_b):
    here = {name: lax.axis_index(name) for name in ("aux", "row", "col")}
    peers = []
    for axis in ("col", "row"):
        n = lax.axis_size(axis)
        for step in range(1, n):
            place = dict(here)
            place[axis] = lax.rem(here[axis] + step, n)
            peers.append((place["aux"], place["row"], place["col"]))
    barrier = pltpu.get_barrier_semaphore()
    for peer in peers:
        pl.semaphore_signal(barrier, inc=1, device_id=peer, device_id_type=pl.DeviceIdType.MESH)
    pl.semaphore_wait(barrier, len(peers))
    by_col = gather_round("col", here, x_ref[...], col_slots, send_a, recv_a)
    o_ref[...] = gather_round("row", here, by_col, row_slots, send_b, recv_b)


def doubling_sum(partial):
    cols, rows = lax.axis_size("col"), lax.axis_size("row")
    return pl.pallas_call(
        two_round_kernel,
        out_shape=jax.ShapeDtypeStruct(partial.shape, partial.dtype),
        in_specs=[pl.BlockSpec(memory_space=pltpu.VMEM)],
        out_specs=pl.BlockSpec(memory_space=pltpu.VMEM),
        scratch_shapes=[
            pltpu.VMEM((cols,) + partial.shape, partial.dtype),
            pltpu.VMEM((rows,) + partial.shape, partial.dtype),
            pltpu.SemaphoreType.DMA((cols,)),
            pltpu.SemaphoreType.DMA((cols,)),
            pltpu.SemaphoreType.DMA((rows,)),
            pltpu.SemaphoreType.DMA((rows,)),
        ],
        compiler_params=pltpu.CompilerParams(collective_id=0, has_side_effects=True),
    )(partial)


def gather_half(local):
    width = local.shape[1] // 2
    part = lax.dynamic_slice_in_dim(local, lax.axis_index("aux") * width, width, axis=1)
    return lax.all_gather(part, "row", axis=0, tiled=True)


def join_halves(own, other, axis):
    first = lax.axis_index("aux") == 0
    return jnp.where(
        first,
        jnp.concatenate([own, other], axis=axis),
        jnp.concatenate([other, own], axis=axis),
    )


def swapped_core(value):
    return lax.ppermute(value, "aux", [(0, 1), (1, 0)])


def sliced(ref, axis, start, size):
    index = [slice(None)] * len(ref.shape)
    index[axis] = pl.ds(start, size)
    return ref.at[tuple(index)]


def exchange_kernel(mesh_axis, split_axis, concat_axis, x_ref, o_ref, send_sem, recv_sem, local_sem):
    here = {name: lax.axis_index(name) for name in ("aux", "row", "col")}
    me, n = here[mesh_axis], lax.axis_size(mesh_axis)
    depth = x_ref.shape[split_axis] // n
    height = o_ref.shape[concat_axis] // n

    def device(index):
        place = dict(here)
        place[mesh_axis] = index
        return (place["aux"], place["row"], place["col"])

    def piece(index):
        return sliced(x_ref, split_axis, index * depth, depth)

    def slot(index):
        return sliced(o_ref, concat_axis, index * height, height)

    barrier = pltpu.get_barrier_semaphore()
    for step in range(1, n):
        pl.semaphore_signal(
            barrier, inc=1, device_id=device(lax.rem(me + step, n)),
            device_id_type=pl.DeviceIdType.MESH,
        )
    pl.semaphore_wait(barrier, n - 1)

    local = pltpu.make_async_copy(piece(me), slot(me), local_sem)
    local.start()
    sends = []
    for step in range(1, n):
        dest = lax.rem(me + step, n)
        copy = pltpu.make_async_remote_copy(
            src_ref=piece(dest),
            dst_ref=slot(me),
            send_sem=send_sem.at[step],
            recv_sem=recv_sem.at[step],
            device_id=device(dest),
            device_id_type=pl.DeviceIdType.MESH,
        )
        copy.start()
        sends.append(copy)
    for step in range(1, n):
        source = lax.rem(me + n - step, n)
        incoming = pltpu.make_async_remote_copy(
            src_ref=piece(me),
            dst_ref=slot(source),
            send_sem=send_sem.at[step],
            recv_sem=recv_sem.at[step],
            device_id=device(source),
            device_id_type=pl.DeviceIdType.MESH,
        )
        incoming.wait_recv()
        sends[step - 1].wait_send()
    local.wait()


def exchange(x, mesh_axis, split_axis, concat_axis, collective_id):
    n = lax.axis_size(mesh_axis)
    shape = list(x.shape)
    shape[split_axis] //= n
    shape[concat_axis] *= n
    nbytes = x.size * x.dtype.itemsize
    return pl.pallas_call(
        functools.partial(exchange_kernel, mesh_axis, split_axis, concat_axis),
        out_shape=jax.ShapeDtypeStruct(tuple(shape), x.dtype),
        in_specs=[pl.BlockSpec(memory_space=pl.ANY)],
        out_specs=pl.BlockSpec(memory_space=pl.ANY),
        scratch_shapes=[
            pltpu.SemaphoreType.DMA((n,)),
            pltpu.SemaphoreType.DMA((n,)),
            pltpu.SemaphoreType.DMA(()),
        ],
        compiler_params=pltpu.CompilerParams(
            collective_id=collective_id, has_side_effects=True
        ),
        cost_estimate=pl.CostEstimate(flops=0, bytes_accessed=2 * nbytes, transcendentals=0),
    )(x)


def shards(coulomb, occupied, virtual, tile_mask):
    rows = lax.axis_size("row")
    cols = lax.axis_size("col")
    pdev, mrow, ncol = coulomb.shape
    nao = mrow * rows
    row_idx = lax.axis_index("row")
    col_idx = lax.axis_index("col")
    aux_idx = lax.axis_index("aux")
    tiles_r = mrow // TILE
    tiles_c = ncol // TILE
    local_tiles = lax.dynamic_slice(
        tile_mask, (row_idx * tiles_r, col_idx * tiles_c), (tiles_r, tiles_c)
    )
    local_mask = jnp.repeat(jnp.repeat(local_tiles, TILE, axis=0), TILE, axis=1).astype(
        jnp.bfloat16
    )
    screened = coulomb * local_mask[None]
    occ_own, virt_own = gather_half(occupied), gather_half(virtual)
    moved = exchange(screened, "row", 0, 1, 1)
    occ_own, moved = lax.optimization_barrier((occ_own, moved))
    pieces = moved.shape[0]
    occ_other = swapped_core(occ_own)
    half_own = jnp.einsum("ml,pmn->pln", occ_own, moved, preferred_element_type=jnp.float32)
    half_other = jnp.einsum("ml,pmn->pln", occ_other, moved, preferred_element_type=jnp.float32)
    half = join_halves(half_own.astype(jnp.bfloat16), half_other.astype(jnp.bfloat16), axis=1)
    jpart = mrow // cols
    shaped = half.reshape(pieces, rows, cols, jpart, ncol)
    spread = lax.all_to_all(shaped, "col", split_axis=2, concat_axis=4, tiled=True)
    spread = spread.reshape(pieces, rows * jpart, nao)
    virt_own, spread = lax.optimization_barrier((virt_own, spread))
    virt_other = swapped_core(virt_own)
    theirs = swapped(screened, "aux", 0)
    chunks = 2
    per = pieces // chunks
    mine_parts, theirs_parts = [], []
    for chunk in range(chunks):
        part = spread[chunk * per:(chunk + 1) * per]
        dressed_own = jnp.einsum("pln,ns->pls", part, virt_own, preferred_element_type=jnp.float32)
        dressed_other = jnp.einsum(
            "pln,ns->pls", part, virt_other, preferred_element_type=jnp.float32
        )
        dressed = join_halves(
            dressed_own.astype(jnp.bfloat16), dressed_other.astype(jnp.bfloat16), axis=2
        )
        by_row = exchange(dressed, "row", 1, 0, 2).reshape(rows * per, 1, 1, jpart, cols, ncol)
        returned = lax.all_to_all(by_row, "col", split_axis=4, concat_axis=2, tiled=True)
        aligned = returned.reshape(rows * per, mrow, ncol)
        mine_parts.append(
            jnp.einsum("pls,qls->pq", aligned, screened, preferred_element_type=jnp.float32)
        )
        theirs_parts.append(
            jnp.einsum("pls,qls->pq", aligned, theirs, preferred_element_type=jnp.float32)
        )

    def in_order(parts):
        stacked = jnp.stack(parts).reshape(chunks, rows, per, pdev)
        return stacked.transpose(1, 0, 2, 3).reshape(pdev, pdev)

    with_mine, with_theirs = in_order(mine_parts), in_order(theirs_parts)
    first_half = jnp.where(aux_idx == 0, with_mine, with_theirs)
    second_half = jnp.where(aux_idx == 0, with_theirs, with_mine)
    partial_chi = jnp.concatenate([first_half, second_half], axis=1)
    total_chi = doubling_sum(partial_chi)
    return total_chi / NAO


def solution(mesh):
    placed = (P("aux", "row", "col"), P("row", None), P("row", None), P())
    return jax.shard_map(
        shards, mesh=mesh, in_specs=placed, out_specs=P("aux", None), check_vma=False
    )
```

```python
import functools

import jax
import jax.numpy as jnp
from jax import lax
from jax.sharding import PartitionSpec as P
from jax.experimental import pallas as pl
from jax.experimental.pallas import tpu as pltpu

NAO = 2048
TILE = 128


def swapped(value, axis, apart):
    mask = 2**apart
    pairs = [(source, source ^ mask) for source in range(lax.axis_size(axis))]
    return lax.ppermute(value, axis, pairs)


def gather_round(axis, here, own, slots, send_sem, recv_sem):
    me, n = here[axis], lax.axis_size(axis)

    def device(index):
        place = dict(here)
        place[axis] = index
        return (place["aux"], place["row"], place["col"])

    slots[me] = own
    sends = []
    for step in range(1, n):
        dest = lax.rem(me + step, n)
        copy = pltpu.make_async_remote_copy(
            src_ref=slots.at[me],
            dst_ref=slots.at[me],
            send_sem=send_sem.at[step],
            recv_sem=recv_sem.at[step],
            device_id=device(dest),
            device_id_type=pl.DeviceIdType.MESH,
        )
        copy.start()
        sends.append(copy)
    for step in range(1, n):
        source = lax.rem(me + n - step, n)
        incoming = pltpu.make_async_remote_copy(
            src_ref=slots.at[me],
            dst_ref=slots.at[source],
            send_sem=send_sem.at[step],
            recv_sem=recv_sem.at[step],
            device_id=device(source),
            device_id_type=pl.DeviceIdType.MESH,
        )
        incoming.wait_recv()
        sends[step - 1].wait_send()
    total = slots[0]
    for index in range(1, n):
        total = total + slots[index]
    return total


def two_round_kernel(x_ref, o_ref, col_slots, row_slots, send_a, recv_a, send_b, recv_b):
    here = {name: lax.axis_index(name) for name in ("aux", "row", "col")}
    peers = []
    for axis in ("col", "row"):
        n = lax.axis_size(axis)
        for step in range(1, n):
            place = dict(here)
            place[axis] = lax.rem(here[axis] + step, n)
            peers.append((place["aux"], place["row"], place["col"]))
    barrier = pltpu.get_barrier_semaphore()
    for peer in peers:
        pl.semaphore_signal(barrier, inc=1, device_id=peer, device_id_type=pl.DeviceIdType.MESH)
    pl.semaphore_wait(barrier, len(peers))
    by_col = gather_round("col", here, x_ref[...], col_slots, send_a, recv_a)
    o_ref[...] = gather_round("row", here, by_col, row_slots, send_b, recv_b)


def doubling_sum(partial):
    cols, rows = lax.axis_size("col"), lax.axis_size("row")
    return pl.pallas_call(
        two_round_kernel,
        out_shape=jax.ShapeDtypeStruct(partial.shape, partial.dtype),
        in_specs=[pl.BlockSpec(memory_space=pltpu.VMEM)],
        out_specs=pl.BlockSpec(memory_space=pltpu.VMEM),
        scratch_shapes=[
            pltpu.VMEM((cols,) + partial.shape, partial.dtype),
            pltpu.VMEM((rows,) + partial.shape, partial.dtype),
            pltpu.SemaphoreType.DMA((cols,)),
            pltpu.SemaphoreType.DMA((cols,)),
            pltpu.SemaphoreType.DMA((rows,)),
            pltpu.SemaphoreType.DMA((rows,)),
        ],
        compiler_params=pltpu.CompilerParams(collective_id=0, has_side_effects=True),
    )(partial)


def gather_half(local):
    width = local.shape[1] // 2
    part = lax.dynamic_slice_in_dim(local, lax.axis_index("aux") * width, width, axis=1)
    return lax.all_gather(part, "row", axis=0, tiled=True)


def join_halves(own, other, axis):
    first = lax.axis_index("aux") == 0
    return jnp.where(
        first,
        jnp.concatenate([own, other], axis=axis),
        jnp.concatenate([other, own], axis=axis),
    )


def swapped_core(value):
    return lax.ppermute(value, "aux", [(0, 1), (1, 0)])


def sliced(ref, axis, start, size):
    index = [slice(None)] * len(ref.shape)
    index[axis] = pl.ds(start, size)
    return ref.at[tuple(index)]


def exchange_kernel(mesh_axis, split_axis, concat_axis, x_ref, o_ref, send_sem, recv_sem, local_sem):
    here = {name: lax.axis_index(name) for name in ("aux", "row", "col")}
    me, n = here[mesh_axis], lax.axis_size(mesh_axis)
    depth = x_ref.shape[split_axis] // n
    height = o_ref.shape[concat_axis] // n

    def device(index):
        place = dict(here)
        place[mesh_axis] = index
        return (place["aux"], place["row"], place["col"])

    def piece(index):
        return sliced(x_ref, split_axis, index * depth, depth)

    def slot(index):
        return sliced(o_ref, concat_axis, index * height, height)

    barrier = pltpu.get_barrier_semaphore()
    for step in range(1, n):
        pl.semaphore_signal(
            barrier, inc=1, device_id=device(lax.rem(me + step, n)),
            device_id_type=pl.DeviceIdType.MESH,
        )
    pl.semaphore_wait(barrier, n - 1)

    local = pltpu.make_async_copy(piece(me), slot(me), local_sem)
    local.start()
    sends = []
    for step in range(1, n):
        dest = lax.rem(me + step, n)
        copy = pltpu.make_async_remote_copy(
            src_ref=piece(dest),
            dst_ref=slot(me),
            send_sem=send_sem.at[step],
            recv_sem=recv_sem.at[step],
            device_id=device(dest),
            device_id_type=pl.DeviceIdType.MESH,
        )
        copy.start()
        sends.append(copy)
    for step in range(1, n):
        source = lax.rem(me + n - step, n)
        incoming = pltpu.make_async_remote_copy(
            src_ref=piece(me),
            dst_ref=slot(source),
            send_sem=send_sem.at[step],
            recv_sem=recv_sem.at[step],
            device_id=device(source),
            device_id_type=pl.DeviceIdType.MESH,
        )
        incoming.wait_recv()
        sends[step - 1].wait_send()
    local.wait()


def exchange(x, mesh_axis, split_axis, concat_axis, collective_id):
    n = lax.axis_size(mesh_axis)
    shape = list(x.shape)
    shape[split_axis] //= n
    shape[concat_axis] *= n
    nbytes = x.size * x.dtype.itemsize
    return pl.pallas_call(
        functools.partial(exchange_kernel, mesh_axis, split_axis, concat_axis),
        out_shape=jax.ShapeDtypeStruct(tuple(shape), x.dtype),
        in_specs=[pl.BlockSpec(memory_space=pl.ANY)],
        out_specs=pl.BlockSpec(memory_space=pl.ANY),
        scratch_shapes=[
            pltpu.SemaphoreType.DMA((n,)),
            pltpu.SemaphoreType.DMA((n,)),
            pltpu.SemaphoreType.DMA(()),
        ],
        compiler_params=pltpu.CompilerParams(
            collective_id=collective_id, has_side_effects=True
        ),
        cost_estimate=pl.CostEstimate(flops=0, bytes_accessed=2 * nbytes, transcendentals=0),
    )(x)


def gather_occ_rows(local):
    rows, cols = lax.axis_size("row"), lax.axis_size("col")
    width = local.shape[1] // cols
    piece = lax.dynamic_slice_in_dim(local, lax.axis_index("col") * width, width, axis=1)
    column = exchange(jnp.tile(piece, (rows, 1)), "row", 0, 0, 5)
    height = column.shape[0] // 2
    part = lax.dynamic_slice_in_dim(column, lax.axis_index("aux") * height, height, axis=0)
    return lax.all_gather(part, "col", axis=1, tiled=True)


def shards(coulomb, occupied, virtual, tile_mask):
    rows = lax.axis_size("row")
    cols = lax.axis_size("col")
    pdev, mrow, ncol = coulomb.shape
    nao = mrow * rows
    row_idx = lax.axis_index("row")
    col_idx = lax.axis_index("col")
    aux_idx = lax.axis_index("aux")
    tiles_r = mrow // TILE
    tiles_c = ncol // TILE
    local_tiles = lax.dynamic_slice(
        tile_mask, (row_idx * tiles_r, col_idx * tiles_c), (tiles_r, tiles_c)
    )
    local_mask = jnp.repeat(jnp.repeat(local_tiles, TILE, axis=0), TILE, axis=1).astype(
        jnp.bfloat16
    )
    screened = coulomb * local_mask[None]
    occ_rows = gather_occ_rows(occupied)
    virt_own = gather_half(virtual)
    moved = exchange(screened, "row", 0, 1, 1)
    occ_rows, moved = lax.optimization_barrier((occ_rows, moved))
    pieces = moved.shape[0]
    occ_other = swapped_core(occ_rows)
    depth = occ_rows.shape[0]
    mine = lax.dynamic_slice_in_dim(moved, aux_idx * depth, depth, axis=1)
    other = lax.dynamic_slice_in_dim(moved, (1 - aux_idx) * depth, depth, axis=1)
    half = (
        jnp.einsum("ml,pmn->pln", occ_rows, mine, preferred_element_type=jnp.float32)
        + jnp.einsum("ml,pmn->pln", occ_other, other, preferred_element_type=jnp.float32)
    ).astype(jnp.bfloat16)
    jpart = mrow // cols
    shaped = half.reshape(pieces, rows, cols, jpart, ncol)
    spread = lax.all_to_all(shaped, "col", split_axis=2, concat_axis=4, tiled=True)
    spread = spread.reshape(pieces, rows * jpart, nao)
    virt_own, spread = lax.optimization_barrier((virt_own, spread))
    virt_other = swapped_core(virt_own)
    dressed_own = jnp.einsum("pln,ns->pls", spread, virt_own, preferred_element_type=jnp.float32)
    dressed_other = jnp.einsum(
        "pln,ns->pls", spread, virt_other, preferred_element_type=jnp.float32
    )
    dressed = join_halves(
        dressed_own.astype(jnp.bfloat16), dressed_other.astype(jnp.bfloat16), axis=2
    )
    layered = dressed.reshape(pieces, rows, 1, jpart, cols, ncol)
    returned = lax.all_to_all(
        lax.all_to_all(layered, "row", split_axis=1, concat_axis=0, tiled=True),
        "col",
        split_axis=4,
        concat_axis=2,
        tiled=True,
    )
    aligned = returned.reshape(pdev, mrow, ncol)
    theirs = swapped(screened, "aux", 0)
    with_mine = jnp.einsum("pls,qls->pq", aligned, screened, preferred_element_type=jnp.float32)
    with_theirs = jnp.einsum("pls,qls->pq", aligned, theirs, preferred_element_type=jnp.float32)
    first_half = jnp.where(aux_idx == 0, with_mine, with_theirs)
    second_half = jnp.where(aux_idx == 0, with_theirs, with_mine)
    partial_chi = jnp.concatenate([first_half, second_half], axis=1)
    total_chi = doubling_sum(partial_chi)
    return total_chi / NAO


def solution(mesh):
    placed = (P("aux", "row", "col"), P("row", None), P("row", None), P())
    return jax.shard_map(
        shards, mesh=mesh, in_specs=placed, out_specs=P("aux", None), check_vma=False
    )
```

```python
import functools

import jax
import jax.numpy as jnp
from jax import lax
from jax.sharding import PartitionSpec as P
from jax.experimental import pallas as pl
from jax.experimental.pallas import tpu as pltpu

NAO = 2048
TILE = 128


def swapped(value, axis, apart):
    mask = 2**apart
    pairs = [(source, source ^ mask) for source in range(lax.axis_size(axis))]
    return lax.ppermute(value, axis, pairs)


def gather_round(axis, here, own, slots, send_sem, recv_sem):
    me, n = here[axis], lax.axis_size(axis)

    def device(index):
        place = dict(here)
        place[axis] = index
        return (place["aux"], place["row"], place["col"])

    slots[me] = own
    sends = []
    for step in range(1, n):
        dest = lax.rem(me + step, n)
        copy = pltpu.make_async_remote_copy(
            src_ref=slots.at[me],
            dst_ref=slots.at[me],
            send_sem=send_sem.at[step],
            recv_sem=recv_sem.at[step],
            device_id=device(dest),
            device_id_type=pl.DeviceIdType.MESH,
        )
        copy.start()
        sends.append(copy)
    for step in range(1, n):
        source = lax.rem(me + n - step, n)
        incoming = pltpu.make_async_remote_copy(
            src_ref=slots.at[me],
            dst_ref=slots.at[source],
            send_sem=send_sem.at[step],
            recv_sem=recv_sem.at[step],
            device_id=device(source),
            device_id_type=pl.DeviceIdType.MESH,
        )
        incoming.wait_recv()
        sends[step - 1].wait_send()
    total = slots[0]
    for index in range(1, n):
        total = total + slots[index]
    return total


def two_round_kernel(x_ref, o_ref, col_slots, row_slots, send_a, recv_a, send_b, recv_b):
    here = {name: lax.axis_index(name) for name in ("aux", "row", "col")}
    peers = []
    for axis in ("col", "row"):
        n = lax.axis_size(axis)
        for step in range(1, n):
            place = dict(here)
            place[axis] = lax.rem(here[axis] + step, n)
            peers.append((place["aux"], place["row"], place["col"]))
    barrier = pltpu.get_barrier_semaphore()
    for peer in peers:
        pl.semaphore_signal(barrier, inc=1, device_id=peer, device_id_type=pl.DeviceIdType.MESH)
    pl.semaphore_wait(barrier, len(peers))
    by_col = gather_round("col", here, x_ref[...], col_slots, send_a, recv_a)
    o_ref[...] = gather_round("row", here, by_col, row_slots, send_b, recv_b)


def doubling_sum(partial):
    cols, rows = lax.axis_size("col"), lax.axis_size("row")
    return pl.pallas_call(
        two_round_kernel,
        out_shape=jax.ShapeDtypeStruct(partial.shape, partial.dtype),
        in_specs=[pl.BlockSpec(memory_space=pltpu.VMEM)],
        out_specs=pl.BlockSpec(memory_space=pltpu.VMEM),
        scratch_shapes=[
            pltpu.VMEM((cols,) + partial.shape, partial.dtype),
            pltpu.VMEM((rows,) + partial.shape, partial.dtype),
            pltpu.SemaphoreType.DMA((cols,)),
            pltpu.SemaphoreType.DMA((cols,)),
            pltpu.SemaphoreType.DMA((rows,)),
            pltpu.SemaphoreType.DMA((rows,)),
        ],
        compiler_params=pltpu.CompilerParams(collective_id=0, has_side_effects=True),
    )(partial)


def gather_half(local):
    width = local.shape[1] // 2
    part = lax.dynamic_slice_in_dim(local, lax.axis_index("aux") * width, width, axis=1)
    return lax.all_gather(part, "row", axis=0, tiled=True)


def join_halves(own, other, axis):
    first = lax.axis_index("aux") == 0
    return jnp.where(
        first,
        jnp.concatenate([own, other], axis=axis),
        jnp.concatenate([other, own], axis=axis),
    )


def swapped_core(value):
    return lax.ppermute(value, "aux", [(0, 1), (1, 0)])


def sliced(ref, axis, start, size):
    index = [slice(None)] * len(ref.shape)
    index[axis] = pl.ds(start, size)
    return ref.at[tuple(index)]


def exchange_kernel(mesh_axis, split_axis, concat_axis, x_ref, o_ref, send_sem, recv_sem, local_sem):
    here = {name: lax.axis_index(name) for name in ("aux", "row", "col")}
    me, n = here[mesh_axis], lax.axis_size(mesh_axis)
    depth = x_ref.shape[split_axis] // n
    height = o_ref.shape[concat_axis] // n

    def device(index):
        place = dict(here)
        place[mesh_axis] = index
        return (place["aux"], place["row"], place["col"])

    def piece(index):
        return sliced(x_ref, split_axis, index * depth, depth)

    def slot(index):
        return sliced(o_ref, concat_axis, index * height, height)

    barrier = pltpu.get_barrier_semaphore()
    for step in range(1, n):
        pl.semaphore_signal(
            barrier, inc=1, device_id=device(lax.rem(me + step, n)),
            device_id_type=pl.DeviceIdType.MESH,
        )
    pl.semaphore_wait(barrier, n - 1)

    local = pltpu.make_async_copy(piece(me), slot(me), local_sem)
    local.start()
    sends = []
    for step in range(1, n):
        dest = lax.rem(me + step, n)
        copy = pltpu.make_async_remote_copy(
            src_ref=piece(dest),
            dst_ref=slot(me),
            send_sem=send_sem.at[step],
            recv_sem=recv_sem.at[step],
            device_id=device(dest),
            device_id_type=pl.DeviceIdType.MESH,
        )
        copy.start()
        sends.append(copy)
    for step in range(1, n):
        source = lax.rem(me + n - step, n)
        incoming = pltpu.make_async_remote_copy(
            src_ref=piece(me),
            dst_ref=slot(source),
            send_sem=send_sem.at[step],
            recv_sem=recv_sem.at[step],
            device_id=device(source),
            device_id_type=pl.DeviceIdType.MESH,
        )
        incoming.wait_recv()
        sends[step - 1].wait_send()
    local.wait()


def exchange(x, mesh_axis, split_axis, concat_axis, collective_id):
    n = lax.axis_size(mesh_axis)
    shape = list(x.shape)
    shape[split_axis] //= n
    shape[concat_axis] *= n
    nbytes = x.size * x.dtype.itemsize
    return pl.pallas_call(
        functools.partial(exchange_kernel, mesh_axis, split_axis, concat_axis),
        out_shape=jax.ShapeDtypeStruct(tuple(shape), x.dtype),
        in_specs=[pl.BlockSpec(memory_space=pl.ANY)],
        out_specs=pl.BlockSpec(memory_space=pl.ANY),
        scratch_shapes=[
            pltpu.SemaphoreType.DMA((n,)),
            pltpu.SemaphoreType.DMA((n,)),
            pltpu.SemaphoreType.DMA(()),
        ],
        compiler_params=pltpu.CompilerParams(
            collective_id=collective_id, has_side_effects=True
        ),
        cost_estimate=pl.CostEstimate(flops=0, bytes_accessed=2 * nbytes, transcendentals=0),
    )(x)


def gather_occ_rows(local):
    rows, cols = lax.axis_size("row"), lax.axis_size("col")
    width = local.shape[1] // cols
    height = local.shape[0] // 2
    piece = lax.dynamic_slice(
        local, (lax.axis_index("aux") * height, lax.axis_index("col") * width), (height, width)
    )
    column = exchange(jnp.tile(piece, (rows, 1)), "row", 0, 0, 5)
    return lax.all_gather(column, "col", axis=1, tiled=True)


def core_rows(moved, core):
    pieces, nao, ncol = moved.shape
    rows = lax.axis_size("row")
    split = moved.reshape(pieces, rows, 2, nao // (2 * rows), ncol)
    picked = lax.dynamic_index_in_dim(split, core, axis=2, keepdims=False)
    return picked.reshape(pieces, nao // 2, ncol)


def shards(coulomb, occupied, virtual, tile_mask):
    rows = lax.axis_size("row")
    cols = lax.axis_size("col")
    pdev, mrow, ncol = coulomb.shape
    nao = mrow * rows
    row_idx = lax.axis_index("row")
    col_idx = lax.axis_index("col")
    aux_idx = lax.axis_index("aux")
    tiles_r = mrow // TILE
    tiles_c = ncol // TILE
    local_tiles = lax.dynamic_slice(
        tile_mask, (row_idx * tiles_r, col_idx * tiles_c), (tiles_r, tiles_c)
    )
    local_mask = jnp.repeat(jnp.repeat(local_tiles, TILE, axis=0), TILE, axis=1).astype(
        jnp.bfloat16
    )
    screened = coulomb * local_mask[None]
    occ_rows = gather_occ_rows(occupied)
    virt_own = gather_half(virtual)
    moved = exchange(screened, "row", 0, 1, 1)
    occ_rows, moved = lax.optimization_barrier((occ_rows, moved))
    pieces = moved.shape[0]
    occ_other = swapped_core(occ_rows)
    mine = core_rows(moved, aux_idx)
    other = core_rows(moved, 1 - aux_idx)
    half = (
        jnp.einsum("ml,pmn->pln", occ_rows, mine, preferred_element_type=jnp.float32)
        + jnp.einsum("ml,pmn->pln", occ_other, other, preferred_element_type=jnp.float32)
    ).astype(jnp.bfloat16)
    jpart = mrow // cols
    shaped = half.reshape(pieces, rows, cols, jpart, ncol)
    spread = lax.all_to_all(shaped, "col", split_axis=2, concat_axis=4, tiled=True)
    spread = spread.reshape(pieces, rows * jpart, nao)
    virt_own, spread = lax.optimization_barrier((virt_own, spread))
    virt_other = swapped_core(virt_own)
    dressed_own = jnp.einsum("pln,ns->pls", spread, virt_own, preferred_element_type=jnp.float32)
    dressed_other = jnp.einsum(
        "pln,ns->pls", spread, virt_other, preferred_element_type=jnp.float32
    )
    dressed = join_halves(
        dressed_own.astype(jnp.bfloat16), dressed_other.astype(jnp.bfloat16), axis=2
    )
    layered = dressed.reshape(pieces, rows, 1, jpart, cols, ncol)
    returned = lax.all_to_all(
        lax.all_to_all(layered, "row", split_axis=1, concat_axis=0, tiled=True),
        "col",
        split_axis=4,
        concat_axis=2,
        tiled=True,
    )
    aligned = returned.reshape(pdev, mrow, ncol)
    theirs = swapped(screened, "aux", 0)
    with_mine = jnp.einsum("pls,qls->pq", aligned, screened, preferred_element_type=jnp.float32)
    with_theirs = jnp.einsum("pls,qls->pq", aligned, theirs, preferred_element_type=jnp.float32)
    first_half = jnp.where(aux_idx == 0, with_mine, with_theirs)
    second_half = jnp.where(aux_idx == 0, with_theirs, with_mine)
    partial_chi = jnp.concatenate([first_half, second_half], axis=1)
    total_chi = doubling_sum(partial_chi)
    return total_chi / NAO


def solution(mesh):
    placed = (P("aux", "row", "col"), P("row", None), P("row", None), P())
    return jax.shard_map(
        shards, mesh=mesh, in_specs=placed, out_specs=P("aux", None), check_vma=False
    )
```

```python
import functools

import jax
import jax.numpy as jnp
from jax import lax
from jax.sharding import PartitionSpec as P
from jax.experimental import pallas as pl
from jax.experimental.pallas import tpu as pltpu

NAO = 2048
TILE = 128


def swapped(value, axis, apart):
    mask = 2**apart
    pairs = [(source, source ^ mask) for source in range(lax.axis_size(axis))]
    return lax.ppermute(value, axis, pairs)


def gather_round(axis, here, own, slots, send_sem, recv_sem):
    me, n = here[axis], lax.axis_size(axis)

    def device(index):
        place = dict(here)
        place[axis] = index
        return (place["aux"], place["row"], place["col"])

    slots[me] = own
    sends = []
    for step in range(1, n):
        dest = lax.rem(me + step, n)
        copy = pltpu.make_async_remote_copy(
            src_ref=slots.at[me],
            dst_ref=slots.at[me],
            send_sem=send_sem.at[step],
            recv_sem=recv_sem.at[step],
            device_id=device(dest),
            device_id_type=pl.DeviceIdType.MESH,
        )
        copy.start()
        sends.append(copy)
    for step in range(1, n):
        source = lax.rem(me + n - step, n)
        incoming = pltpu.make_async_remote_copy(
            src_ref=slots.at[me],
            dst_ref=slots.at[source],
            send_sem=send_sem.at[step],
            recv_sem=recv_sem.at[step],
            device_id=device(source),
            device_id_type=pl.DeviceIdType.MESH,
        )
        incoming.wait_recv()
        sends[step - 1].wait_send()
    total = slots[0]
    for index in range(1, n):
        total = total + slots[index]
    return total


def two_round_kernel(x_ref, o_ref, col_slots, row_slots, send_a, recv_a, send_b, recv_b):
    here = {name: lax.axis_index(name) for name in ("aux", "row", "col")}
    peers = []
    for axis in ("col", "row"):
        n = lax.axis_size(axis)
        for step in range(1, n):
            place = dict(here)
            place[axis] = lax.rem(here[axis] + step, n)
            peers.append((place["aux"], place["row"], place["col"]))
    barrier = pltpu.get_barrier_semaphore()
    for peer in peers:
        pl.semaphore_signal(barrier, inc=1, device_id=peer, device_id_type=pl.DeviceIdType.MESH)
    pl.semaphore_wait(barrier, len(peers))
    by_col = gather_round("col", here, x_ref[...], col_slots, send_a, recv_a)
    o_ref[...] = gather_round("row", here, by_col, row_slots, send_b, recv_b)


def doubling_sum(partial):
    cols, rows = lax.axis_size("col"), lax.axis_size("row")
    return pl.pallas_call(
        two_round_kernel,
        out_shape=jax.ShapeDtypeStruct(partial.shape, partial.dtype),
        in_specs=[pl.BlockSpec(memory_space=pltpu.VMEM)],
        out_specs=pl.BlockSpec(memory_space=pltpu.VMEM),
        scratch_shapes=[
            pltpu.VMEM((cols,) + partial.shape, partial.dtype),
            pltpu.VMEM((rows,) + partial.shape, partial.dtype),
            pltpu.SemaphoreType.DMA((cols,)),
            pltpu.SemaphoreType.DMA((cols,)),
            pltpu.SemaphoreType.DMA((rows,)),
            pltpu.SemaphoreType.DMA((rows,)),
        ],
        compiler_params=pltpu.CompilerParams(collective_id=0, has_side_effects=True),
    )(partial)


def gather_half(local):
    width = local.shape[1] // 2
    part = lax.dynamic_slice_in_dim(local, lax.axis_index("aux") * width, width, axis=1)
    return lax.all_gather(part, "row", axis=0, tiled=True)


def join_halves(own, other, axis):
    first = lax.axis_index("aux") == 0
    return jnp.where(
        first,
        jnp.concatenate([own, other], axis=axis),
        jnp.concatenate([other, own], axis=axis),
    )


def swapped_core(value):
    return lax.ppermute(value, "aux", [(0, 1), (1, 0)])


def sliced(ref, axis, start, size):
    index = [slice(None)] * len(ref.shape)
    index[axis] = pl.ds(start, size)
    return ref.at[tuple(index)]


def exchange_kernel(mesh_axis, split_axis, concat_axis, x_ref, o_ref, send_sem, recv_sem, local_sem):
    here = {name: lax.axis_index(name) for name in ("aux", "row", "col")}
    me, n = here[mesh_axis], lax.axis_size(mesh_axis)
    depth = x_ref.shape[split_axis] // n
    height = o_ref.shape[concat_axis] // n

    def device(index):
        place = dict(here)
        place[mesh_axis] = index
        return (place["aux"], place["row"], place["col"])

    def piece(index):
        return sliced(x_ref, split_axis, index * depth, depth)

    def slot(index):
        return sliced(o_ref, concat_axis, index * height, height)

    barrier = pltpu.get_barrier_semaphore()
    for step in range(1, n):
        pl.semaphore_signal(
            barrier, inc=1, device_id=device(lax.rem(me + step, n)),
            device_id_type=pl.DeviceIdType.MESH,
        )
    pl.semaphore_wait(barrier, n - 1)

    local = pltpu.make_async_copy(piece(me), slot(me), local_sem)
    local.start()
    sends = []
    for step in range(1, n):
        dest = lax.rem(me + step, n)
        copy = pltpu.make_async_remote_copy(
            src_ref=piece(dest),
            dst_ref=slot(me),
            send_sem=send_sem.at[step],
            recv_sem=recv_sem.at[step],
            device_id=device(dest),
            device_id_type=pl.DeviceIdType.MESH,
        )
        copy.start()
        sends.append(copy)
    for step in range(1, n):
        source = lax.rem(me + n - step, n)
        incoming = pltpu.make_async_remote_copy(
            src_ref=piece(me),
            dst_ref=slot(source),
            send_sem=send_sem.at[step],
            recv_sem=recv_sem.at[step],
            device_id=device(source),
            device_id_type=pl.DeviceIdType.MESH,
        )
        incoming.wait_recv()
        sends[step - 1].wait_send()
    local.wait()


def exchange(x, mesh_axis, split_axis, concat_axis, collective_id):
    n = lax.axis_size(mesh_axis)
    shape = list(x.shape)
    shape[split_axis] //= n
    shape[concat_axis] *= n
    nbytes = x.size * x.dtype.itemsize
    return pl.pallas_call(
        functools.partial(exchange_kernel, mesh_axis, split_axis, concat_axis),
        out_shape=jax.ShapeDtypeStruct(tuple(shape), x.dtype),
        in_specs=[pl.BlockSpec(memory_space=pl.ANY)],
        out_specs=pl.BlockSpec(memory_space=pl.ANY),
        scratch_shapes=[
            pltpu.SemaphoreType.DMA((n,)),
            pltpu.SemaphoreType.DMA((n,)),
            pltpu.SemaphoreType.DMA(()),
        ],
        compiler_params=pltpu.CompilerParams(
            collective_id=collective_id, has_side_effects=True
        ),
        cost_estimate=pl.CostEstimate(flops=0, bytes_accessed=2 * nbytes, transcendentals=0),
    )(x)


def gather_occ_rows(local):
    rows, cols = lax.axis_size("row"), lax.axis_size("col")
    width = local.shape[1] // cols
    height = local.shape[0] // 2
    piece = lax.dynamic_slice(
        local, (lax.axis_index("aux") * height, lax.axis_index("col") * width), (height, width)
    )
    column = exchange(jnp.tile(piece, (rows, 1)), "row", 0, 0, 5)
    return lax.all_gather(column, "col", axis=1, tiled=True)


def core_rows(moved, core):
    pieces, nao, ncol = moved.shape
    rows = lax.axis_size("row")
    split = moved.reshape(pieces, rows, 2, nao // (2 * rows), ncol)
    picked = lax.dynamic_index_in_dim(split, core, axis=2, keepdims=False)
    return picked.reshape(pieces, nao // 2, ncol)


def shards(coulomb, occupied, virtual, tile_mask):
    rows = lax.axis_size("row")
    cols = lax.axis_size("col")
    pdev, mrow, ncol = coulomb.shape
    nao = mrow * rows
    row_idx = lax.axis_index("row")
    col_idx = lax.axis_index("col")
    aux_idx = lax.axis_index("aux")
    tiles_r = mrow // TILE
    tiles_c = ncol // TILE
    local_tiles = lax.dynamic_slice(
        tile_mask, (row_idx * tiles_r, col_idx * tiles_c), (tiles_r, tiles_c)
    )
    local_mask = jnp.repeat(jnp.repeat(local_tiles, TILE, axis=0), TILE, axis=1).astype(
        jnp.bfloat16
    )
    screened = coulomb * local_mask[None]
    occ_rows = gather_occ_rows(occupied)
    virt_own = gather_half(virtual)
    moved = exchange(screened, "row", 0, 1, 1)
    occ_rows, moved = lax.optimization_barrier((occ_rows, moved))
    pieces = moved.shape[0]
    occ_other = swapped_core(occ_rows)
    mine = core_rows(moved, aux_idx)
    other = core_rows(moved, 1 - aux_idx)
    half = (
        jnp.einsum("ml,pmn->pln", occ_rows, mine, preferred_element_type=jnp.float32)
        + jnp.einsum("ml,pmn->pln", occ_other, other, preferred_element_type=jnp.float32)
    ).astype(jnp.bfloat16)
    jpart = mrow // cols
    shaped = half.reshape(pieces, rows, cols, jpart, ncol)
    spread = lax.all_to_all(shaped, "col", split_axis=2, concat_axis=4, tiled=True)
    spread = spread.reshape(pieces, rows * jpart, nao)
    virt_own, spread = lax.optimization_barrier((virt_own, spread))
    virt_other = swapped_core(virt_own)
    dressed_own = jnp.einsum("pln,ns->pls", spread, virt_own, preferred_element_type=jnp.float32)
    dressed_other = jnp.einsum(
        "pln,ns->pls", spread, virt_other, preferred_element_type=jnp.float32
    )
    dressed = join_halves(
        dressed_own.astype(jnp.bfloat16), dressed_other.astype(jnp.bfloat16), axis=2
    )
    by_dest = (
        dressed.reshape(pieces, rows, jpart, cols, ncol)
        .transpose(1, 3, 0, 2, 4)
        .reshape(rows * cols, pieces, jpart, ncol)
    )
    got = lax.all_to_all(by_dest, ("row", "col"), split_axis=0, concat_axis=0, tiled=True)
    returned = got.reshape(rows, cols, pieces, jpart, ncol).transpose(0, 2, 1, 3, 4)
    aligned = returned.reshape(pdev, mrow, ncol)
    theirs = swapped(screened, "aux", 0)
    with_mine = jnp.einsum("pls,qls->pq", aligned, screened, preferred_element_type=jnp.float32)
    with_theirs = jnp.einsum("pls,qls->pq", aligned, theirs, preferred_element_type=jnp.float32)
    first_half = jnp.where(aux_idx == 0, with_mine, with_theirs)
    second_half = jnp.where(aux_idx == 0, with_theirs, with_mine)
    partial_chi = jnp.concatenate([first_half, second_half], axis=1)
    total_chi = doubling_sum(partial_chi)
    return total_chi / NAO


def solution(mesh):
    placed = (P("aux", "row", "col"), P("row", None), P("row", None), P())
    return jax.shard_map(
        shards, mesh=mesh, in_specs=placed, out_specs=P("aux", None), check_vma=False
    )
```

```python
import functools

import jax
import jax.numpy as jnp
from jax import lax
from jax.sharding import PartitionSpec as P
from jax.experimental import pallas as pl
from jax.experimental.pallas import tpu as pltpu

NAO = 2048
TILE = 128


def swapped(value, axis, apart):
    mask = 2**apart
    pairs = [(source, source ^ mask) for source in range(lax.axis_size(axis))]
    return lax.ppermute(value, axis, pairs)


def gather_round(axis, here, own, slots, send_sem, recv_sem):
    me, n = here[axis], lax.axis_size(axis)

    def device(index):
        place = dict(here)
        place[axis] = index
        return (place["aux"], place["row"], place["col"])

    slots[me] = own
    sends = []
    for step in range(1, n):
        dest = lax.rem(me + step, n)
        copy = pltpu.make_async_remote_copy(
            src_ref=slots.at[me],
            dst_ref=slots.at[me],
            send_sem=send_sem.at[step],
            recv_sem=recv_sem.at[step],
            device_id=device(dest),
            device_id_type=pl.DeviceIdType.MESH,
        )
        copy.start()
        sends.append(copy)
    for step in range(1, n):
        source = lax.rem(me + n - step, n)
        incoming = pltpu.make_async_remote_copy(
            src_ref=slots.at[me],
            dst_ref=slots.at[source],
            send_sem=send_sem.at[step],
            recv_sem=recv_sem.at[step],
            device_id=device(source),
            device_id_type=pl.DeviceIdType.MESH,
        )
        incoming.wait_recv()
        sends[step - 1].wait_send()
    total = slots[0]
    for index in range(1, n):
        total = total + slots[index]
    return total


def two_round_kernel(x_ref, o_ref, col_slots, row_slots, send_a, recv_a, send_b, recv_b):
    here = {name: lax.axis_index(name) for name in ("aux", "row", "col")}
    peers = []
    for axis in ("col", "row"):
        n = lax.axis_size(axis)
        for step in range(1, n):
            place = dict(here)
            place[axis] = lax.rem(here[axis] + step, n)
            peers.append((place["aux"], place["row"], place["col"]))
    barrier = pltpu.get_barrier_semaphore()
    for peer in peers:
        pl.semaphore_signal(barrier, inc=1, device_id=peer, device_id_type=pl.DeviceIdType.MESH)
    pl.semaphore_wait(barrier, len(peers))
    by_col = gather_round("col", here, x_ref[...], col_slots, send_a, recv_a)
    o_ref[...] = gather_round("row", here, by_col, row_slots, send_b, recv_b)


def doubling_sum(partial):
    cols, rows = lax.axis_size("col"), lax.axis_size("row")
    return pl.pallas_call(
        two_round_kernel,
        out_shape=jax.ShapeDtypeStruct(partial.shape, partial.dtype),
        in_specs=[pl.BlockSpec(memory_space=pltpu.VMEM)],
        out_specs=pl.BlockSpec(memory_space=pltpu.VMEM),
        scratch_shapes=[
            pltpu.VMEM((cols,) + partial.shape, partial.dtype),
            pltpu.VMEM((rows,) + partial.shape, partial.dtype),
            pltpu.SemaphoreType.DMA((cols,)),
            pltpu.SemaphoreType.DMA((cols,)),
            pltpu.SemaphoreType.DMA((rows,)),
            pltpu.SemaphoreType.DMA((rows,)),
        ],
        compiler_params=pltpu.CompilerParams(collective_id=0, has_side_effects=True),
    )(partial)


def gather_half(local):
    width = local.shape[1] // 2
    part = lax.dynamic_slice_in_dim(local, lax.axis_index("aux") * width, width, axis=1)
    return lax.all_gather(part, "row", axis=0, tiled=True)


def join_halves(own, other, axis):
    first = lax.axis_index("aux") == 0
    return jnp.where(
        first,
        jnp.concatenate([own, other], axis=axis),
        jnp.concatenate([other, own], axis=axis),
    )


def swapped_core(value):
    return lax.ppermute(value, "aux", [(0, 1), (1, 0)])


def sliced(ref, axis, start, size):
    index = [slice(None)] * len(ref.shape)
    index[axis] = pl.ds(start, size)
    return ref.at[tuple(index)]


def exchange_kernel(mesh_axis, split_axis, concat_axis, x_ref, o_ref, send_sem, recv_sem, local_sem):
    here = {name: lax.axis_index(name) for name in ("aux", "row", "col")}
    me, n = here[mesh_axis], lax.axis_size(mesh_axis)
    depth = x_ref.shape[split_axis] // n
    height = o_ref.shape[concat_axis] // n

    def device(index):
        place = dict(here)
        place[mesh_axis] = index
        return (place["aux"], place["row"], place["col"])

    def piece(index):
        return sliced(x_ref, split_axis, index * depth, depth)

    def slot(index):
        return sliced(o_ref, concat_axis, index * height, height)

    barrier = pltpu.get_barrier_semaphore()
    for step in range(1, n):
        pl.semaphore_signal(
            barrier, inc=1, device_id=device(lax.rem(me + step, n)),
            device_id_type=pl.DeviceIdType.MESH,
        )
    pl.semaphore_wait(barrier, n - 1)

    local = pltpu.make_async_copy(piece(me), slot(me), local_sem)
    local.start()
    sends = []
    for step in range(1, n):
        dest = lax.rem(me + step, n)
        copy = pltpu.make_async_remote_copy(
            src_ref=piece(dest),
            dst_ref=slot(me),
            send_sem=send_sem.at[step],
            recv_sem=recv_sem.at[step],
            device_id=device(dest),
            device_id_type=pl.DeviceIdType.MESH,
        )
        copy.start()
        sends.append(copy)
    for step in range(1, n):
        source = lax.rem(me + n - step, n)
        incoming = pltpu.make_async_remote_copy(
            src_ref=piece(me),
            dst_ref=slot(source),
            send_sem=send_sem.at[step],
            recv_sem=recv_sem.at[step],
            device_id=device(source),
            device_id_type=pl.DeviceIdType.MESH,
        )
        incoming.wait_recv()
        sends[step - 1].wait_send()
    local.wait()


def exchange(x, mesh_axis, split_axis, concat_axis, collective_id):
    n = lax.axis_size(mesh_axis)
    shape = list(x.shape)
    shape[split_axis] //= n
    shape[concat_axis] *= n
    nbytes = x.size * x.dtype.itemsize
    return pl.pallas_call(
        functools.partial(exchange_kernel, mesh_axis, split_axis, concat_axis),
        out_shape=jax.ShapeDtypeStruct(tuple(shape), x.dtype),
        in_specs=[pl.BlockSpec(memory_space=pl.ANY)],
        out_specs=pl.BlockSpec(memory_space=pl.ANY),
        scratch_shapes=[
            pltpu.SemaphoreType.DMA((n,)),
            pltpu.SemaphoreType.DMA((n,)),
            pltpu.SemaphoreType.DMA(()),
        ],
        compiler_params=pltpu.CompilerParams(
            collective_id=collective_id, has_side_effects=True
        ),
        cost_estimate=pl.CostEstimate(flops=0, bytes_accessed=2 * nbytes, transcendentals=0),
    )(x)


def gather_occ_rows(local):
    rows, cols = lax.axis_size("row"), lax.axis_size("col")
    width = local.shape[1] // cols
    height = local.shape[0] // 2
    piece = lax.dynamic_slice(
        local, (lax.axis_index("aux") * height, lax.axis_index("col") * width), (height, width)
    )
    blocks = lax.all_gather(piece, ("row", "col"), axis=0, tiled=False)
    blocks = blocks.reshape(rows, cols, height, width).transpose(0, 2, 1, 3)
    return blocks.reshape(rows * height, cols * width)


def core_rows(moved, core):
    pieces, nao, ncol = moved.shape
    rows = lax.axis_size("row")
    split = moved.reshape(pieces, rows, 2, nao // (2 * rows), ncol)
    picked = lax.dynamic_index_in_dim(split, core, axis=2, keepdims=False)
    return picked.reshape(pieces, nao // 2, ncol)


def shards(coulomb, occupied, virtual, tile_mask):
    rows = lax.axis_size("row")
    cols = lax.axis_size("col")
    pdev, mrow, ncol = coulomb.shape
    nao = mrow * rows
    row_idx = lax.axis_index("row")
    col_idx = lax.axis_index("col")
    aux_idx = lax.axis_index("aux")
    tiles_r = mrow // TILE
    tiles_c = ncol // TILE
    local_tiles = lax.dynamic_slice(
        tile_mask, (row_idx * tiles_r, col_idx * tiles_c), (tiles_r, tiles_c)
    )
    local_mask = jnp.repeat(jnp.repeat(local_tiles, TILE, axis=0), TILE, axis=1).astype(
        jnp.bfloat16
    )
    screened = coulomb * local_mask[None]
    occ_rows = gather_occ_rows(occupied)
    virt_own = gather_half(virtual)
    moved = exchange(screened, "row", 0, 1, 1)
    occ_rows, moved = lax.optimization_barrier((occ_rows, moved))
    pieces = moved.shape[0]
    occ_other = swapped_core(occ_rows)
    mine = core_rows(moved, aux_idx)
    other = core_rows(moved, 1 - aux_idx)
    half = (
        jnp.einsum("ml,pmn->pln", occ_rows, mine, preferred_element_type=jnp.float32)
        + jnp.einsum("ml,pmn->pln", occ_other, other, preferred_element_type=jnp.float32)
    ).astype(jnp.bfloat16)
    jpart = mrow // cols
    shaped = half.reshape(pieces, rows, cols, jpart, ncol)
    spread = lax.all_to_all(shaped, "col", split_axis=2, concat_axis=4, tiled=True)
    spread = spread.reshape(pieces, rows * jpart, nao)
    virt_own, spread = lax.optimization_barrier((virt_own, spread))
    virt_other = swapped_core(virt_own)
    dressed_own = jnp.einsum("pln,ns->pls", spread, virt_own, preferred_element_type=jnp.float32)
    dressed_other = jnp.einsum(
        "pln,ns->pls", spread, virt_other, preferred_element_type=jnp.float32
    )
    dressed = join_halves(
        dressed_own.astype(jnp.bfloat16), dressed_other.astype(jnp.bfloat16), axis=2
    )
    by_dest = (
        dressed.reshape(pieces, rows, jpart, cols, ncol)
        .transpose(1, 3, 0, 2, 4)
        .reshape(rows * cols, pieces, jpart, ncol)
    )
    got = lax.all_to_all(by_dest, ("row", "col"), split_axis=0, concat_axis=0, tiled=True)
    returned = got.reshape(rows, cols, pieces, jpart, ncol).transpose(0, 2, 1, 3, 4)
    aligned = returned.reshape(pdev, mrow, ncol)
    theirs = swapped(screened, "aux", 0)
    with_mine = jnp.einsum("pls,qls->pq", aligned, screened, preferred_element_type=jnp.float32)
    with_theirs = jnp.einsum("pls,qls->pq", aligned, theirs, preferred_element_type=jnp.float32)
    first_half = jnp.where(aux_idx == 0, with_mine, with_theirs)
    second_half = jnp.where(aux_idx == 0, with_theirs, with_mine)
    partial_chi = jnp.concatenate([first_half, second_half], axis=1)
    total_chi = doubling_sum(partial_chi)
    return total_chi / NAO


def solution(mesh):
    placed = (P("aux", "row", "col"), P("row", None), P("row", None), P())
    return jax.shard_map(
        shards, mesh=mesh, in_specs=placed, out_specs=P("aux", None), check_vma=False
    )
```

```python
import functools

import jax
import jax.numpy as jnp
from jax import lax
from jax.sharding import PartitionSpec as P
from jax.experimental import pallas as pl
from jax.experimental.pallas import tpu as pltpu

NAO = 2048
TILE = 128


def swapped(value, axis, apart):
    mask = 2**apart
    pairs = [(source, source ^ mask) for source in range(lax.axis_size(axis))]
    return lax.ppermute(value, axis, pairs)


def gather_round(axis, here, own, slots, send_sem, recv_sem):
    me, n = here[axis], lax.axis_size(axis)

    def device(index):
        place = dict(here)
        place[axis] = index
        return (place["aux"], place["row"], place["col"])

    slots[me] = own
    sends = []
    for step in range(1, n):
        dest = lax.rem(me + step, n)
        copy = pltpu.make_async_remote_copy(
            src_ref=slots.at[me],
            dst_ref=slots.at[me],
            send_sem=send_sem.at[step],
            recv_sem=recv_sem.at[step],
            device_id=device(dest),
            device_id_type=pl.DeviceIdType.MESH,
        )
        copy.start()
        sends.append(copy)
    for step in range(1, n):
        source = lax.rem(me + n - step, n)
        incoming = pltpu.make_async_remote_copy(
            src_ref=slots.at[me],
            dst_ref=slots.at[source],
            send_sem=send_sem.at[step],
            recv_sem=recv_sem.at[step],
            device_id=device(source),
            device_id_type=pl.DeviceIdType.MESH,
        )
        incoming.wait_recv()
        sends[step - 1].wait_send()
    total = slots[0]
    for index in range(1, n):
        total = total + slots[index]
    return total


def two_round_kernel(x_ref, o_ref, col_slots, row_slots, send_a, recv_a, send_b, recv_b):
    here = {name: lax.axis_index(name) for name in ("aux", "row", "col")}
    peers = []
    for axis in ("col", "row"):
        n = lax.axis_size(axis)
        for step in range(1, n):
            place = dict(here)
            place[axis] = lax.rem(here[axis] + step, n)
            peers.append((place["aux"], place["row"], place["col"]))
    barrier = pltpu.get_barrier_semaphore()
    for peer in peers:
        pl.semaphore_signal(barrier, inc=1, device_id=peer, device_id_type=pl.DeviceIdType.MESH)
    pl.semaphore_wait(barrier, len(peers))
    by_col = gather_round("col", here, x_ref[...], col_slots, send_a, recv_a)
    o_ref[...] = gather_round("row", here, by_col, row_slots, send_b, recv_b)


def doubling_sum(partial):
    cols, rows = lax.axis_size("col"), lax.axis_size("row")
    return pl.pallas_call(
        two_round_kernel,
        out_shape=jax.ShapeDtypeStruct(partial.shape, partial.dtype),
        in_specs=[pl.BlockSpec(memory_space=pltpu.VMEM)],
        out_specs=pl.BlockSpec(memory_space=pltpu.VMEM),
        scratch_shapes=[
            pltpu.VMEM((cols,) + partial.shape, partial.dtype),
            pltpu.VMEM((rows,) + partial.shape, partial.dtype),
            pltpu.SemaphoreType.DMA((cols,)),
            pltpu.SemaphoreType.DMA((cols,)),
            pltpu.SemaphoreType.DMA((rows,)),
            pltpu.SemaphoreType.DMA((rows,)),
        ],
        compiler_params=pltpu.CompilerParams(collective_id=0, has_side_effects=True),
    )(partial)


def gather_half(local):
    width = local.shape[1] // 2
    part = lax.dynamic_slice_in_dim(local, lax.axis_index("aux") * width, width, axis=1)
    return lax.all_gather(part, "row", axis=0, tiled=True)


def join_halves(own, other, axis):
    first = lax.axis_index("aux") == 0
    return jnp.where(
        first,
        jnp.concatenate([own, other], axis=axis),
        jnp.concatenate([other, own], axis=axis),
    )


def swapped_core(value):
    return lax.ppermute(value, "aux", [(0, 1), (1, 0)])


def sliced(ref, axis, start, size):
    index = [slice(None)] * len(ref.shape)
    index[axis] = pl.ds(start, size)
    return ref.at[tuple(index)]


def exchange_kernel(mesh_axis, split_axis, concat_axis, x_ref, o_ref, send_sem, recv_sem, local_sem):
    here = {name: lax.axis_index(name) for name in ("aux", "row", "col")}
    me, n = here[mesh_axis], lax.axis_size(mesh_axis)
    depth = x_ref.shape[split_axis] // n
    height = o_ref.shape[concat_axis] // n

    def device(index):
        place = dict(here)
        place[mesh_axis] = index
        return (place["aux"], place["row"], place["col"])

    def piece(index):
        return sliced(x_ref, split_axis, index * depth, depth)

    def slot(index):
        return sliced(o_ref, concat_axis, index * height, height)

    barrier = pltpu.get_barrier_semaphore()
    for step in range(1, n):
        pl.semaphore_signal(
            barrier, inc=1, device_id=device(lax.rem(me + step, n)),
            device_id_type=pl.DeviceIdType.MESH,
        )
    pl.semaphore_wait(barrier, n - 1)

    local = pltpu.make_async_copy(piece(me), slot(me), local_sem)
    local.start()
    sends = []
    for step in range(1, n):
        dest = lax.rem(me + step, n)
        copy = pltpu.make_async_remote_copy(
            src_ref=piece(dest),
            dst_ref=slot(me),
            send_sem=send_sem.at[step],
            recv_sem=recv_sem.at[step],
            device_id=device(dest),
            device_id_type=pl.DeviceIdType.MESH,
        )
        copy.start()
        sends.append(copy)
    for step in range(1, n):
        source = lax.rem(me + n - step, n)
        incoming = pltpu.make_async_remote_copy(
            src_ref=piece(me),
            dst_ref=slot(source),
            send_sem=send_sem.at[step],
            recv_sem=recv_sem.at[step],
            device_id=device(source),
            device_id_type=pl.DeviceIdType.MESH,
        )
        incoming.wait_recv()
        sends[step - 1].wait_send()
    local.wait()


def exchange(x, mesh_axis, split_axis, concat_axis, collective_id):
    n = lax.axis_size(mesh_axis)
    shape = list(x.shape)
    shape[split_axis] //= n
    shape[concat_axis] *= n
    nbytes = x.size * x.dtype.itemsize
    return pl.pallas_call(
        functools.partial(exchange_kernel, mesh_axis, split_axis, concat_axis),
        out_shape=jax.ShapeDtypeStruct(tuple(shape), x.dtype),
        in_specs=[pl.BlockSpec(memory_space=pl.ANY)],
        out_specs=pl.BlockSpec(memory_space=pl.ANY),
        scratch_shapes=[
            pltpu.SemaphoreType.DMA((n,)),
            pltpu.SemaphoreType.DMA((n,)),
            pltpu.SemaphoreType.DMA(()),
        ],
        compiler_params=pltpu.CompilerParams(
            collective_id=collective_id, has_side_effects=True
        ),
        cost_estimate=pl.CostEstimate(flops=0, bytes_accessed=2 * nbytes, transcendentals=0),
    )(x)


def gather_occ_rows(local):
    rows, cols = lax.axis_size("row"), lax.axis_size("col")
    width = local.shape[1] // cols
    height = local.shape[0] // 2
    piece = lax.dynamic_slice(
        local, (lax.axis_index("aux") * height, lax.axis_index("col") * width), (height, width)
    )
    column = exchange(jnp.tile(piece, (rows, 1)), "row", 0, 0, 5)
    return lax.all_gather(column, "col", axis=1, tiled=True)


def core_rows(moved, core):
    pieces, nao, ncol = moved.shape
    rows = lax.axis_size("row")
    split = moved.reshape(pieces, rows, 2, nao // (2 * rows), ncol)
    picked = lax.dynamic_index_in_dim(split, core, axis=2, keepdims=False)
    return picked.reshape(pieces, nao // 2, ncol)


def shards(coulomb, occupied, virtual, tile_mask):
    rows = lax.axis_size("row")
    cols = lax.axis_size("col")
    pdev, mrow, ncol = coulomb.shape
    nao = mrow * rows
    row_idx = lax.axis_index("row")
    col_idx = lax.axis_index("col")
    aux_idx = lax.axis_index("aux")
    tiles_r = mrow // TILE
    tiles_c = ncol // TILE
    local_tiles = lax.dynamic_slice(
        tile_mask, (row_idx * tiles_r, col_idx * tiles_c), (tiles_r, tiles_c)
    )
    local_mask = jnp.repeat(jnp.repeat(local_tiles, TILE, axis=0), TILE, axis=1).astype(
        jnp.bfloat16
    )
    screened = coulomb * local_mask[None]
    occ_rows = gather_occ_rows(occupied)
    virt_own = gather_half(virtual)
    moved = exchange(screened, "row", 0, 1, 1)
    occ_rows, moved = lax.optimization_barrier((occ_rows, moved))
    pieces = moved.shape[0]
    occ_other = swapped_core(occ_rows)
    mine = core_rows(moved, aux_idx)
    other = core_rows(moved, 1 - aux_idx)
    half = (
        jnp.einsum("ml,pmn->pln", occ_rows, mine, preferred_element_type=jnp.float32)
        + jnp.einsum("ml,pmn->pln", occ_other, other, preferred_element_type=jnp.float32)
    ).astype(jnp.bfloat16)
    jpart = mrow // cols
    shaped = half.reshape(pieces, rows, cols, jpart, ncol)
    spread = lax.all_to_all(shaped, "col", split_axis=2, concat_axis=4, tiled=True)
    spread = spread.reshape(pieces, rows * jpart, nao)
    virt_own, spread = lax.optimization_barrier((virt_own, spread))
    virt_other = swapped_core(virt_own)
    dressed_own = jnp.einsum("pln,ns->pls", spread, virt_own, preferred_element_type=jnp.float32)
    dressed_other = jnp.einsum(
        "pln,ns->pls", spread, virt_other, preferred_element_type=jnp.float32
    )
    dressed = join_halves(
        dressed_own.astype(jnp.bfloat16), dressed_other.astype(jnp.bfloat16), axis=2
    )
    by_dest = (
        dressed.reshape(pieces, rows, jpart, cols, ncol)
        .transpose(1, 3, 0, 2, 4)
        .reshape(rows * cols, pieces, jpart, ncol)
    )
    got = lax.all_to_all(by_dest, ("row", "col"), split_axis=0, concat_axis=0, tiled=True)
    returned = got.reshape(rows, cols, pieces, jpart, ncol)
    theirs = swapped(screened, "aux", 0)

    def against(block):
        split = block.reshape(pdev, cols, jpart, ncol)
        return jnp.einsum(
            "rcpjs,qcjs->rpq", returned, split, preferred_element_type=jnp.float32
        ).reshape(pdev, pdev)

    with_mine, with_theirs = against(screened), against(theirs)
    first_half = jnp.where(aux_idx == 0, with_mine, with_theirs)
    second_half = jnp.where(aux_idx == 0, with_theirs, with_mine)
    partial_chi = jnp.concatenate([first_half, second_half], axis=1)
    total_chi = doubling_sum(partial_chi)
    return total_chi / NAO


def solution(mesh):
    placed = (P("aux", "row", "col"), P("row", None), P("row", None), P())
    return jax.shard_map(
        shards, mesh=mesh, in_specs=placed, out_specs=P("aux", None), check_vma=False
    )
```

```python
import functools

import jax
import jax.numpy as jnp
from jax import lax
from jax.sharding import PartitionSpec as P
from jax.experimental import pallas as pl
from jax.experimental.pallas import tpu as pltpu

NAO = 2048
TILE = 128


def swapped(value, axis, apart):
    mask = 2**apart
    pairs = [(source, source ^ mask) for source in range(lax.axis_size(axis))]
    return lax.ppermute(value, axis, pairs)


def gather_round(axis, here, own, slots, send_sem, recv_sem):
    me, n = here[axis], lax.axis_size(axis)

    def device(index):
        place = dict(here)
        place[axis] = index
        return (place["aux"], place["row"], place["col"])

    slots[me] = own
    sends = []
    for step in range(1, n):
        dest = lax.rem(me + step, n)
        copy = pltpu.make_async_remote_copy(
            src_ref=slots.at[me],
            dst_ref=slots.at[me],
            send_sem=send_sem.at[step],
            recv_sem=recv_sem.at[step],
            device_id=device(dest),
            device_id_type=pl.DeviceIdType.MESH,
        )
        copy.start()
        sends.append(copy)
    for step in range(1, n):
        source = lax.rem(me + n - step, n)
        incoming = pltpu.make_async_remote_copy(
            src_ref=slots.at[me],
            dst_ref=slots.at[source],
            send_sem=send_sem.at[step],
            recv_sem=recv_sem.at[step],
            device_id=device(source),
            device_id_type=pl.DeviceIdType.MESH,
        )
        incoming.wait_recv()
        sends[step - 1].wait_send()
    total = slots[0]
    for index in range(1, n):
        total = total + slots[index]
    return total


def two_round_kernel(x_ref, o_ref, col_slots, row_slots, send_a, recv_a, send_b, recv_b):
    here = {name: lax.axis_index(name) for name in ("aux", "row", "col")}
    peers = []
    for axis in ("col", "row"):
        n = lax.axis_size(axis)
        for step in range(1, n):
            place = dict(here)
            place[axis] = lax.rem(here[axis] + step, n)
            peers.append((place["aux"], place["row"], place["col"]))
    barrier = pltpu.get_barrier_semaphore()
    for peer in peers:
        pl.semaphore_signal(barrier, inc=1, device_id=peer, device_id_type=pl.DeviceIdType.MESH)
    pl.semaphore_wait(barrier, len(peers))
    by_col = gather_round("col", here, x_ref[...], col_slots, send_a, recv_a)
    o_ref[...] = gather_round("row", here, by_col, row_slots, send_b, recv_b)


def doubling_sum(partial):
    cols, rows = lax.axis_size("col"), lax.axis_size("row")
    return pl.pallas_call(
        two_round_kernel,
        out_shape=jax.ShapeDtypeStruct(partial.shape, partial.dtype),
        in_specs=[pl.BlockSpec(memory_space=pltpu.VMEM)],
        out_specs=pl.BlockSpec(memory_space=pltpu.VMEM),
        scratch_shapes=[
            pltpu.VMEM((cols,) + partial.shape, partial.dtype),
            pltpu.VMEM((rows,) + partial.shape, partial.dtype),
            pltpu.SemaphoreType.DMA((cols,)),
            pltpu.SemaphoreType.DMA((cols,)),
            pltpu.SemaphoreType.DMA((rows,)),
            pltpu.SemaphoreType.DMA((rows,)),
        ],
        compiler_params=pltpu.CompilerParams(collective_id=0, has_side_effects=True),
    )(partial)


def gather_half(local):
    width = local.shape[1] // 2
    part = lax.dynamic_slice_in_dim(local, lax.axis_index("aux") * width, width, axis=1)
    return lax.all_gather(part, "row", axis=0, tiled=True)


def join_halves(own, other, axis):
    first = lax.axis_index("aux") == 0
    return jnp.where(
        first,
        jnp.concatenate([own, other], axis=axis),
        jnp.concatenate([other, own], axis=axis),
    )


def swapped_core(value):
    return lax.ppermute(value, "aux", [(0, 1), (1, 0)])


def sliced(ref, axis, start, size):
    index = [slice(None)] * len(ref.shape)
    index[axis] = pl.ds(start, size)
    return ref.at[tuple(index)]


def exchange_kernel(mesh_axis, split_axis, concat_axis, x_ref, o_ref, send_sem, recv_sem, local_sem):
    here = {name: lax.axis_index(name) for name in ("aux", "row", "col")}
    me, n = here[mesh_axis], lax.axis_size(mesh_axis)
    depth = x_ref.shape[split_axis] // n
    height = o_ref.shape[concat_axis] // n

    def device(index):
        place = dict(here)
        place[mesh_axis] = index
        return (place["aux"], place["row"], place["col"])

    def piece(index):
        return sliced(x_ref, split_axis, index * depth, depth)

    def slot(index):
        return sliced(o_ref, concat_axis, index * height, height)

    barrier = pltpu.get_barrier_semaphore()
    for step in range(1, n):
        pl.semaphore_signal(
            barrier, inc=1, device_id=device(lax.rem(me + step, n)),
            device_id_type=pl.DeviceIdType.MESH,
        )
    pl.semaphore_wait(barrier, n - 1)

    local = pltpu.make_async_copy(piece(me), slot(me), local_sem)
    local.start()
    sends = []
    for step in range(1, n):
        dest = lax.rem(me + step, n)
        copy = pltpu.make_async_remote_copy(
            src_ref=piece(dest),
            dst_ref=slot(me),
            send_sem=send_sem.at[step],
            recv_sem=recv_sem.at[step],
            device_id=device(dest),
            device_id_type=pl.DeviceIdType.MESH,
        )
        copy.start()
        sends.append(copy)
    for step in range(1, n):
        source = lax.rem(me + n - step, n)
        incoming = pltpu.make_async_remote_copy(
            src_ref=piece(me),
            dst_ref=slot(source),
            send_sem=send_sem.at[step],
            recv_sem=recv_sem.at[step],
            device_id=device(source),
            device_id_type=pl.DeviceIdType.MESH,
        )
        incoming.wait_recv()
        sends[step - 1].wait_send()
    local.wait()


def exchange(x, mesh_axis, split_axis, concat_axis, collective_id):
    n = lax.axis_size(mesh_axis)
    shape = list(x.shape)
    shape[split_axis] //= n
    shape[concat_axis] *= n
    nbytes = x.size * x.dtype.itemsize
    return pl.pallas_call(
        functools.partial(exchange_kernel, mesh_axis, split_axis, concat_axis),
        out_shape=jax.ShapeDtypeStruct(tuple(shape), x.dtype),
        in_specs=[pl.BlockSpec(memory_space=pl.ANY)],
        out_specs=pl.BlockSpec(memory_space=pl.ANY),
        scratch_shapes=[
            pltpu.SemaphoreType.DMA((n,)),
            pltpu.SemaphoreType.DMA((n,)),
            pltpu.SemaphoreType.DMA(()),
        ],
        compiler_params=pltpu.CompilerParams(
            collective_id=collective_id, has_side_effects=True
        ),
        cost_estimate=pl.CostEstimate(flops=0, bytes_accessed=2 * nbytes, transcendentals=0),
    )(x)


def gather_occ_rows(local):
    rows, cols = lax.axis_size("row"), lax.axis_size("col")
    width = local.shape[1] // cols
    height = local.shape[0] // 2
    piece = lax.dynamic_slice(
        local, (lax.axis_index("aux") * height, lax.axis_index("col") * width), (height, width)
    )
    column = exchange(jnp.tile(piece, (rows, 1)), "row", 0, 0, 5)
    return lax.all_gather(column, "col", axis=1, tiled=True)


def core_rows(moved, core):
    pieces, nao, ncol = moved.shape
    rows = lax.axis_size("row")
    split = moved.reshape(pieces, rows, 2, nao // (2 * rows), ncol)
    picked = lax.dynamic_index_in_dim(split, core, axis=2, keepdims=False)
    return picked.reshape(pieces, nao // 2, ncol)


def shards(coulomb, occupied, virtual, tile_mask):
    rows = lax.axis_size("row")
    cols = lax.axis_size("col")
    pdev, mrow, ncol = coulomb.shape
    nao = mrow * rows
    row_idx = lax.axis_index("row")
    col_idx = lax.axis_index("col")
    aux_idx = lax.axis_index("aux")
    tiles_r = mrow // TILE
    tiles_c = ncol // TILE
    local_tiles = lax.dynamic_slice(
        tile_mask, (row_idx * tiles_r, col_idx * tiles_c), (tiles_r, tiles_c)
    )
    local_mask = jnp.repeat(jnp.repeat(local_tiles, TILE, axis=0), TILE, axis=1).astype(
        jnp.bfloat16
    )
    screened = coulomb * local_mask[None]
    occ_rows = gather_occ_rows(occupied)
    virt_own = gather_half(virtual)
    moved = exchange(screened, "row", 0, 1, 1)
    occ_rows, moved = lax.optimization_barrier((occ_rows, moved))
    pieces = moved.shape[0]
    occ_other = swapped_core(occ_rows)
    mine = core_rows(moved, aux_idx)
    other = core_rows(moved, 1 - aux_idx)
    half = (
        jnp.einsum("ml,pmn->pnl", occ_rows, mine, preferred_element_type=jnp.float32)
        + jnp.einsum("ml,pmn->pnl", occ_other, other, preferred_element_type=jnp.float32)
    ).astype(jnp.bfloat16)
    jpart = mrow // cols
    by_col = half.reshape(pieces, ncol, rows, cols, jpart).transpose(3, 0, 1, 2, 4)
    spread = lax.all_to_all(by_col, "col", split_axis=0, concat_axis=0, tiled=True)
    virt_own, spread = lax.optimization_barrier((virt_own, spread))
    virt_other = swapped_core(virt_own)

    def dress(columns):
        split = columns.reshape(cols, ncol, columns.shape[1])
        out = jnp.einsum("cpnrj,cns->prjs", spread, split, preferred_element_type=jnp.float32)
        return out.reshape(pieces, rows * jpart, columns.shape[1])

    dressed_own = dress(virt_own)
    dressed_other = dress(virt_other)
    dressed = join_halves(
        dressed_own.astype(jnp.bfloat16), dressed_other.astype(jnp.bfloat16), axis=2
    )
    by_dest = (
        dressed.reshape(pieces, rows, jpart, cols, ncol)
        .transpose(1, 3, 0, 2, 4)
        .reshape(rows * cols, pieces, jpart, ncol)
    )
    got = lax.all_to_all(by_dest, ("row", "col"), split_axis=0, concat_axis=0, tiled=True)
    returned = got.reshape(rows, cols, pieces, jpart, ncol)
    theirs = swapped(screened, "aux", 0)

    def against(block):
        split = block.reshape(pdev, cols, jpart, ncol)
        return jnp.einsum(
            "rcpjs,qcjs->rpq", returned, split, preferred_element_type=jnp.float32
        ).reshape(pdev, pdev)

    with_mine, with_theirs = against(screened), against(theirs)
    first_half = jnp.where(aux_idx == 0, with_mine, with_theirs)
    second_half = jnp.where(aux_idx == 0, with_theirs, with_mine)
    partial_chi = jnp.concatenate([first_half, second_half], axis=1)
    total_chi = doubling_sum(partial_chi)
    return total_chi / NAO


def solution(mesh):
    placed = (P("aux", "row", "col"), P("row", None), P("row", None), P())
    return jax.shard_map(
        shards, mesh=mesh, in_specs=placed, out_specs=P("aux", None), check_vma=False
    )
```

```python
import functools

import jax
import jax.numpy as jnp
from jax import lax
from jax.sharding import PartitionSpec as P
from jax.experimental import pallas as pl
from jax.experimental.pallas import tpu as pltpu

NAO = 2048
TILE = 128


def swapped(value, axis, apart):
    mask = 2**apart
    pairs = [(source, source ^ mask) for source in range(lax.axis_size(axis))]
    return lax.ppermute(value, axis, pairs)


def gather_round(axis, here, own, slots, send_sem, recv_sem):
    me, n = here[axis], lax.axis_size(axis)

    def device(index):
        place = dict(here)
        place[axis] = index
        return (place["aux"], place["row"], place["col"])

    slots[me] = own
    sends = []
    for step in range(1, n):
        dest = lax.rem(me + step, n)
        copy = pltpu.make_async_remote_copy(
            src_ref=slots.at[me],
            dst_ref=slots.at[me],
            send_sem=send_sem.at[step],
            recv_sem=recv_sem.at[step],
            device_id=device(dest),
            device_id_type=pl.DeviceIdType.MESH,
        )
        copy.start()
        sends.append(copy)
    for step in range(1, n):
        source = lax.rem(me + n - step, n)
        incoming = pltpu.make_async_remote_copy(
            src_ref=slots.at[me],
            dst_ref=slots.at[source],
            send_sem=send_sem.at[step],
            recv_sem=recv_sem.at[step],
            device_id=device(source),
            device_id_type=pl.DeviceIdType.MESH,
        )
        incoming.wait_recv()
        sends[step - 1].wait_send()
    total = slots[0]
    for index in range(1, n):
        total = total + slots[index]
    return total


def two_round_kernel(x_ref, o_ref, col_slots, row_slots, send_a, recv_a, send_b, recv_b):
    here = {name: lax.axis_index(name) for name in ("aux", "row", "col")}
    peers = []
    for axis in ("col", "row"):
        n = lax.axis_size(axis)
        for step in range(1, n):
            place = dict(here)
            place[axis] = lax.rem(here[axis] + step, n)
            peers.append((place["aux"], place["row"], place["col"]))
    barrier = pltpu.get_barrier_semaphore()
    for peer in peers:
        pl.semaphore_signal(barrier, inc=1, device_id=peer, device_id_type=pl.DeviceIdType.MESH)
    pl.semaphore_wait(barrier, len(peers))
    by_col = gather_round("col", here, x_ref[...], col_slots, send_a, recv_a)
    o_ref[...] = gather_round("row", here, by_col, row_slots, send_b, recv_b)


def doubling_sum(partial):
    cols, rows = lax.axis_size("col"), lax.axis_size("row")
    return pl.pallas_call(
        two_round_kernel,
        out_shape=jax.ShapeDtypeStruct(partial.shape, partial.dtype),
        in_specs=[pl.BlockSpec(memory_space=pltpu.VMEM)],
        out_specs=pl.BlockSpec(memory_space=pltpu.VMEM),
        scratch_shapes=[
            pltpu.VMEM((cols,) + partial.shape, partial.dtype),
            pltpu.VMEM((rows,) + partial.shape, partial.dtype),
            pltpu.SemaphoreType.DMA((cols,)),
            pltpu.SemaphoreType.DMA((cols,)),
            pltpu.SemaphoreType.DMA((rows,)),
            pltpu.SemaphoreType.DMA((rows,)),
        ],
        compiler_params=pltpu.CompilerParams(collective_id=0, has_side_effects=True),
    )(partial)


def gather_half(local):
    width = local.shape[1] // 2
    part = lax.dynamic_slice_in_dim(local, lax.axis_index("aux") * width, width, axis=1)
    return lax.all_gather(part, "row", axis=0, tiled=True)


def join_halves(own, other, axis):
    first = lax.axis_index("aux") == 0
    return jnp.where(
        first,
        jnp.concatenate([own, other], axis=axis),
        jnp.concatenate([other, own], axis=axis),
    )


def swapped_core(value):
    return lax.ppermute(value, "aux", [(0, 1), (1, 0)])


def sliced(ref, axis, start, size):
    index = [slice(None)] * len(ref.shape)
    index[axis] = pl.ds(start, size)
    return ref.at[tuple(index)]


def exchange_kernel(mesh_axis, split_axis, concat_axis, x_ref, o_ref, send_sem, recv_sem, local_sem):
    here = {name: lax.axis_index(name) for name in ("aux", "row", "col")}
    me, n = here[mesh_axis], lax.axis_size(mesh_axis)
    depth = x_ref.shape[split_axis] // n
    height = o_ref.shape[concat_axis] // n

    def device(index):
        place = dict(here)
        place[mesh_axis] = index
        return (place["aux"], place["row"], place["col"])

    def piece(index):
        return sliced(x_ref, split_axis, index * depth, depth)

    def slot(index):
        return sliced(o_ref, concat_axis, index * height, height)

    barrier = pltpu.get_barrier_semaphore()
    for step in range(1, n):
        pl.semaphore_signal(
            barrier, inc=1, device_id=device(lax.rem(me + step, n)),
            device_id_type=pl.DeviceIdType.MESH,
        )
    pl.semaphore_wait(barrier, n - 1)

    local = pltpu.make_async_copy(piece(me), slot(me), local_sem)
    local.start()
    sends = []
    for step in range(1, n):
        dest = lax.rem(me + step, n)
        copy = pltpu.make_async_remote_copy(
            src_ref=piece(dest),
            dst_ref=slot(me),
            send_sem=send_sem.at[step],
            recv_sem=recv_sem.at[step],
            device_id=device(dest),
            device_id_type=pl.DeviceIdType.MESH,
        )
        copy.start()
        sends.append(copy)
    for step in range(1, n):
        source = lax.rem(me + n - step, n)
        incoming = pltpu.make_async_remote_copy(
            src_ref=piece(me),
            dst_ref=slot(source),
            send_sem=send_sem.at[step],
            recv_sem=recv_sem.at[step],
            device_id=device(source),
            device_id_type=pl.DeviceIdType.MESH,
        )
        incoming.wait_recv()
        sends[step - 1].wait_send()
    local.wait()


def exchange(x, mesh_axis, split_axis, concat_axis, collective_id):
    n = lax.axis_size(mesh_axis)
    shape = list(x.shape)
    shape[split_axis] //= n
    shape[concat_axis] *= n
    nbytes = x.size * x.dtype.itemsize
    return pl.pallas_call(
        functools.partial(exchange_kernel, mesh_axis, split_axis, concat_axis),
        out_shape=jax.ShapeDtypeStruct(tuple(shape), x.dtype),
        in_specs=[pl.BlockSpec(memory_space=pl.ANY)],
        out_specs=pl.BlockSpec(memory_space=pl.ANY),
        scratch_shapes=[
            pltpu.SemaphoreType.DMA((n,)),
            pltpu.SemaphoreType.DMA((n,)),
            pltpu.SemaphoreType.DMA(()),
        ],
        compiler_params=pltpu.CompilerParams(
            collective_id=collective_id, has_side_effects=True
        ),
        cost_estimate=pl.CostEstimate(flops=0, bytes_accessed=2 * nbytes, transcendentals=0),
    )(x)


def gather_occ_rows(local):
    rows, cols = lax.axis_size("row"), lax.axis_size("col")
    width = local.shape[1] // cols
    height = local.shape[0] // 2
    piece = lax.dynamic_slice(
        local, (lax.axis_index("aux") * height, lax.axis_index("col") * width), (height, width)
    )
    column = exchange(jnp.tile(piece, (rows, 1)), "row", 0, 0, 5)
    return lax.all_gather(column, "col", axis=1, tiled=True)


def core_rows(moved, core):
    pieces, nao, ncol = moved.shape
    rows = lax.axis_size("row")
    split = moved.reshape(pieces, rows, 2, nao // (2 * rows), ncol)
    picked = lax.dynamic_index_in_dim(split, core, axis=2, keepdims=False)
    return picked.reshape(pieces, nao // 2, ncol)


def ring_half(local, after):
    width = local.shape[1] // 2
    part = lax.dynamic_slice_in_dim(local, lax.axis_index("aux") * width, width, axis=1)
    part, after = lax.optimization_barrier((part, after))
    n, me = lax.axis_size("row"), lax.axis_index("row")
    ahead, back = part[:, : width // 2], part[:, width // 2:]
    got_ahead, got_back = [ahead], [back]
    for _ in range(1, n):
        ahead = lax.ppermute(ahead, "row", [(i, (i + 1) % n) for i in range(n)])
        back = lax.ppermute(back, "row", [(i, (i - 1) % n) for i in range(n)])
        got_ahead.append(ahead)
        got_back.append(back)
    by_offset_ahead = jnp.stack([got_ahead[(n - j) % n] for j in range(n)])
    by_offset_back = jnp.stack(got_back)

    def placed(by_offset):
        twice = jnp.concatenate([by_offset, by_offset])
        return lax.dynamic_slice_in_dim(twice, (n - me) % n, n, axis=0)

    joined = jnp.concatenate([placed(by_offset_ahead), placed(by_offset_back)], axis=2)
    return joined.reshape(n * local.shape[0], width)


def shards(coulomb, occupied, virtual, tile_mask):
    rows = lax.axis_size("row")
    cols = lax.axis_size("col")
    pdev, mrow, ncol = coulomb.shape
    nao = mrow * rows
    row_idx = lax.axis_index("row")
    col_idx = lax.axis_index("col")
    aux_idx = lax.axis_index("aux")
    tiles_r = mrow // TILE
    tiles_c = ncol // TILE
    local_tiles = lax.dynamic_slice(
        tile_mask, (row_idx * tiles_r, col_idx * tiles_c), (tiles_r, tiles_c)
    )
    local_mask = jnp.repeat(jnp.repeat(local_tiles, TILE, axis=0), TILE, axis=1).astype(
        jnp.bfloat16
    )
    screened = coulomb * local_mask[None]
    occ_rows = gather_occ_rows(occupied)
    moved = exchange(screened, "row", 0, 1, 1)
    virt_own = ring_half(virtual, moved)
    occ_rows, moved = lax.optimization_barrier((occ_rows, moved))
    pieces = moved.shape[0]
    occ_other = swapped_core(occ_rows)
    mine = core_rows(moved, aux_idx)
    other = core_rows(moved, 1 - aux_idx)
    half = (
        jnp.einsum("ml,pmn->pnl", occ_rows, mine, preferred_element_type=jnp.float32)
        + jnp.einsum("ml,pmn->pnl", occ_other, other, preferred_element_type=jnp.float32)
    ).astype(jnp.bfloat16)
    jpart = mrow // cols
    by_col = half.reshape(pieces, ncol, rows, cols, jpart).transpose(3, 0, 1, 2, 4)
    spread = lax.all_to_all(by_col, "col", split_axis=0, concat_axis=0, tiled=True)
    virt_own, spread = lax.optimization_barrier((virt_own, spread))
    virt_other = swapped_core(virt_own)

    def dress(columns):
        split = columns.reshape(cols, ncol, columns.shape[1])
        out = jnp.einsum("cpnrj,cns->prjs", spread, split, preferred_element_type=jnp.float32)
        return out.reshape(pieces, rows * jpart, columns.shape[1])

    dressed_own = dress(virt_own)
    dressed_other = dress(virt_other)
    dressed = join_halves(
        dressed_own.astype(jnp.bfloat16), dressed_other.astype(jnp.bfloat16), axis=2
    )
    by_dest = (
        dressed.reshape(pieces, rows, jpart, cols, ncol)
        .transpose(1, 3, 0, 2, 4)
        .reshape(rows * cols, pieces, jpart, ncol)
    )
    got = lax.all_to_all(by_dest, ("row", "col"), split_axis=0, concat_axis=0, tiled=True)
    returned = got.reshape(rows, cols, pieces, jpart, ncol)
    theirs = swapped(screened, "aux", 0)

    def against(block):
        split = block.reshape(pdev, cols, jpart, ncol)
        return jnp.einsum(
            "rcpjs,qcjs->rpq", returned, split, preferred_element_type=jnp.float32
        ).reshape(pdev, pdev)

    with_mine, with_theirs = against(screened), against(theirs)
    first_half = jnp.where(aux_idx == 0, with_mine, with_theirs)
    second_half = jnp.where(aux_idx == 0, with_theirs, with_mine)
    partial_chi = jnp.concatenate([first_half, second_half], axis=1)
    total_chi = doubling_sum(partial_chi)
    return total_chi / NAO


def solution(mesh):
    placed = (P("aux", "row", "col"), P("row", None), P("row", None), P())
    return jax.shard_map(
        shards, mesh=mesh, in_specs=placed, out_specs=P("aux", None), check_vma=False
    )
```

```python
import functools

import jax
import jax.numpy as jnp
from jax import lax
from jax.sharding import PartitionSpec as P
from jax.experimental import pallas as pl
from jax.experimental.pallas import tpu as pltpu

NAO = 2048
TILE = 128


def swapped(value, axis, apart):
    mask = 2**apart
    pairs = [(source, source ^ mask) for source in range(lax.axis_size(axis))]
    return lax.ppermute(value, axis, pairs)


def gather_round(axis, here, own, slots, send_sem, recv_sem):
    me, n = here[axis], lax.axis_size(axis)

    def device(index):
        place = dict(here)
        place[axis] = index
        return (place["aux"], place["row"], place["col"])

    slots[me] = own
    sends = []
    for step in range(1, n):
        dest = lax.rem(me + step, n)
        copy = pltpu.make_async_remote_copy(
            src_ref=slots.at[me],
            dst_ref=slots.at[me],
            send_sem=send_sem.at[step],
            recv_sem=recv_sem.at[step],
            device_id=device(dest),
            device_id_type=pl.DeviceIdType.MESH,
        )
        copy.start()
        sends.append(copy)
    for step in range(1, n):
        source = lax.rem(me + n - step, n)
        incoming = pltpu.make_async_remote_copy(
            src_ref=slots.at[me],
            dst_ref=slots.at[source],
            send_sem=send_sem.at[step],
            recv_sem=recv_sem.at[step],
            device_id=device(source),
            device_id_type=pl.DeviceIdType.MESH,
        )
        incoming.wait_recv()
        sends[step - 1].wait_send()
    total = slots[0]
    for index in range(1, n):
        total = total + slots[index]
    return total


def two_round_kernel(x_ref, o_ref, col_slots, row_slots, send_a, recv_a, send_b, recv_b):
    here = {name: lax.axis_index(name) for name in ("aux", "row", "col")}
    peers = []
    for axis in ("col", "row"):
        n = lax.axis_size(axis)
        for step in range(1, n):
            place = dict(here)
            place[axis] = lax.rem(here[axis] + step, n)
            peers.append((place["aux"], place["row"], place["col"]))
    barrier = pltpu.get_barrier_semaphore()
    for peer in peers:
        pl.semaphore_signal(barrier, inc=1, device_id=peer, device_id_type=pl.DeviceIdType.MESH)
    pl.semaphore_wait(barrier, len(peers))
    by_col = gather_round("col", here, x_ref[...], col_slots, send_a, recv_a)
    o_ref[...] = gather_round("row", here, by_col, row_slots, send_b, recv_b)


def doubling_sum(partial):
    cols, rows = lax.axis_size("col"), lax.axis_size("row")
    return pl.pallas_call(
        two_round_kernel,
        out_shape=jax.ShapeDtypeStruct(partial.shape, partial.dtype),
        in_specs=[pl.BlockSpec(memory_space=pltpu.VMEM)],
        out_specs=pl.BlockSpec(memory_space=pltpu.VMEM),
        scratch_shapes=[
            pltpu.VMEM((cols,) + partial.shape, partial.dtype),
            pltpu.VMEM((rows,) + partial.shape, partial.dtype),
            pltpu.SemaphoreType.DMA((cols,)),
            pltpu.SemaphoreType.DMA((cols,)),
            pltpu.SemaphoreType.DMA((rows,)),
            pltpu.SemaphoreType.DMA((rows,)),
        ],
        compiler_params=pltpu.CompilerParams(collective_id=0, has_side_effects=True),
    )(partial)


def gather_half(local):
    width = local.shape[1] // 2
    part = lax.dynamic_slice_in_dim(local, lax.axis_index("aux") * width, width, axis=1)
    return lax.all_gather(part, "row", axis=0, tiled=True)


def join_halves(own, other, axis):
    first = lax.axis_index("aux") == 0
    return jnp.where(
        first,
        jnp.concatenate([own, other], axis=axis),
        jnp.concatenate([other, own], axis=axis),
    )


def swapped_core(value):
    return lax.ppermute(value, "aux", [(0, 1), (1, 0)])


def sliced(ref, axis, start, size):
    index = [slice(None)] * len(ref.shape)
    index[axis] = pl.ds(start, size)
    return ref.at[tuple(index)]


def exchange_kernel(mesh_axis, split_axis, concat_axis, x_ref, o_ref, send_sem, recv_sem, local_sem):
    here = {name: lax.axis_index(name) for name in ("aux", "row", "col")}
    me, n = here[mesh_axis], lax.axis_size(mesh_axis)
    depth = x_ref.shape[split_axis] // n
    height = o_ref.shape[concat_axis] // n

    def device(index):
        place = dict(here)
        place[mesh_axis] = index
        return (place["aux"], place["row"], place["col"])

    def piece(index):
        return sliced(x_ref, split_axis, index * depth, depth)

    def slot(index):
        return sliced(o_ref, concat_axis, index * height, height)

    barrier = pltpu.get_barrier_semaphore()
    for step in range(1, n):
        pl.semaphore_signal(
            barrier, inc=1, device_id=device(lax.rem(me + step, n)),
            device_id_type=pl.DeviceIdType.MESH,
        )
    pl.semaphore_wait(barrier, n - 1)

    local = pltpu.make_async_copy(piece(me), slot(me), local_sem)
    local.start()
    sends = []
    for step in range(1, n):
        dest = lax.rem(me + step, n)
        copy = pltpu.make_async_remote_copy(
            src_ref=piece(dest),
            dst_ref=slot(me),
            send_sem=send_sem.at[step],
            recv_sem=recv_sem.at[step],
            device_id=device(dest),
            device_id_type=pl.DeviceIdType.MESH,
        )
        copy.start()
        sends.append(copy)
    for step in range(1, n):
        source = lax.rem(me + n - step, n)
        incoming = pltpu.make_async_remote_copy(
            src_ref=piece(me),
            dst_ref=slot(source),
            send_sem=send_sem.at[step],
            recv_sem=recv_sem.at[step],
            device_id=device(source),
            device_id_type=pl.DeviceIdType.MESH,
        )
        incoming.wait_recv()
        sends[step - 1].wait_send()
    local.wait()


def exchange(x, mesh_axis, split_axis, concat_axis, collective_id):
    n = lax.axis_size(mesh_axis)
    shape = list(x.shape)
    shape[split_axis] //= n
    shape[concat_axis] *= n
    nbytes = x.size * x.dtype.itemsize
    return pl.pallas_call(
        functools.partial(exchange_kernel, mesh_axis, split_axis, concat_axis),
        out_shape=jax.ShapeDtypeStruct(tuple(shape), x.dtype),
        in_specs=[pl.BlockSpec(memory_space=pl.ANY)],
        out_specs=pl.BlockSpec(memory_space=pl.ANY),
        scratch_shapes=[
            pltpu.SemaphoreType.DMA((n,)),
            pltpu.SemaphoreType.DMA((n,)),
            pltpu.SemaphoreType.DMA(()),
        ],
        compiler_params=pltpu.CompilerParams(
            collective_id=collective_id, has_side_effects=True
        ),
        cost_estimate=pl.CostEstimate(flops=0, bytes_accessed=2 * nbytes, transcendentals=0),
    )(x)


def gather_occ_rows(local):
    rows, cols = lax.axis_size("row"), lax.axis_size("col")
    width = local.shape[1] // cols
    height = local.shape[0] // 2
    piece = lax.dynamic_slice(
        local, (lax.axis_index("aux") * height, lax.axis_index("col") * width), (height, width)
    )
    column = exchange(jnp.tile(piece, (rows, 1)), "row", 0, 0, 5)
    top, bottom = column[: height * rows // 2], column[height * rows // 2:]
    by_gather = lax.all_gather(top, "col", axis=1, tiled=True)
    copies = jnp.broadcast_to(bottom[None], (cols,) + bottom.shape)
    by_swap = lax.all_to_all(copies, "col", split_axis=0, concat_axis=0, tiled=True)
    by_swap = by_swap.transpose(1, 0, 2).reshape(bottom.shape[0], cols * width)
    return jnp.concatenate([by_gather, by_swap], axis=0)


def core_rows(moved, core):
    pieces, nao, ncol = moved.shape
    rows = lax.axis_size("row")
    split = moved.reshape(pieces, rows, 2, nao // (2 * rows), ncol)
    picked = lax.dynamic_index_in_dim(split, core, axis=2, keepdims=False)
    return picked.reshape(pieces, nao // 2, ncol)


def shards(coulomb, occupied, virtual, tile_mask):
    rows = lax.axis_size("row")
    cols = lax.axis_size("col")
    pdev, mrow, ncol = coulomb.shape
    nao = mrow * rows
    row_idx = lax.axis_index("row")
    col_idx = lax.axis_index("col")
    aux_idx = lax.axis_index("aux")
    tiles_r = mrow // TILE
    tiles_c = ncol // TILE
    local_tiles = lax.dynamic_slice(
        tile_mask, (row_idx * tiles_r, col_idx * tiles_c), (tiles_r, tiles_c)
    )
    local_mask = jnp.repeat(jnp.repeat(local_tiles, TILE, axis=0), TILE, axis=1).astype(
        jnp.bfloat16
    )
    screened = coulomb * local_mask[None]
    occ_rows = gather_occ_rows(occupied)
    virt_own = gather_half(virtual)
    moved = exchange(screened, "row", 0, 1, 1)
    occ_rows, moved = lax.optimization_barrier((occ_rows, moved))
    pieces = moved.shape[0]
    occ_other = swapped_core(occ_rows)
    mine = core_rows(moved, aux_idx)
    other = core_rows(moved, 1 - aux_idx)
    half = (
        jnp.einsum("ml,pmn->pln", occ_rows, mine, preferred_element_type=jnp.float32)
        + jnp.einsum("ml,pmn->pln", occ_other, other, preferred_element_type=jnp.float32)
    ).astype(jnp.bfloat16)
    jpart = mrow // cols
    shaped = half.reshape(pieces, rows, cols, jpart, ncol)
    spread = lax.all_to_all(shaped, "col", split_axis=2, concat_axis=4, tiled=True)
    spread = spread.reshape(pieces, rows * jpart, nao)
    virt_own, spread = lax.optimization_barrier((virt_own, spread))
    virt_other = swapped_core(virt_own)
    dressed_own = jnp.einsum("pln,ns->pls", spread, virt_own, preferred_element_type=jnp.float32)
    dressed_other = jnp.einsum(
        "pln,ns->pls", spread, virt_other, preferred_element_type=jnp.float32
    )
    dressed = join_halves(
        dressed_own.astype(jnp.bfloat16), dressed_other.astype(jnp.bfloat16), axis=2
    )
    by_dest = (
        dressed.reshape(pieces, rows, jpart, cols, ncol)
        .transpose(1, 3, 0, 2, 4)
        .reshape(rows * cols, pieces, jpart, ncol)
    )
    got = lax.all_to_all(by_dest, ("row", "col"), split_axis=0, concat_axis=0, tiled=True)
    returned = got.reshape(rows, cols, pieces, jpart, ncol)
    theirs = swapped(screened, "aux", 0)

    def against(block):
        split = block.reshape(pdev, cols, jpart, ncol)
        return jnp.einsum(
            "rcpjs,qcjs->rpq", returned, split, preferred_element_type=jnp.float32
        ).reshape(pdev, pdev)

    with_mine, with_theirs = against(screened), against(theirs)
    first_half = jnp.where(aux_idx == 0, with_mine, with_theirs)
    second_half = jnp.where(aux_idx == 0, with_theirs, with_mine)
    partial_chi = jnp.concatenate([first_half, second_half], axis=1)
    total_chi = doubling_sum(partial_chi)
    return total_chi / NAO


def solution(mesh):
    placed = (P("aux", "row", "col"), P("row", None), P("row", None), P())
    return jax.shard_map(
        shards, mesh=mesh, in_specs=placed, out_specs=P("aux", None), check_vma=False
    )
```

```python
import functools

import jax
import jax.numpy as jnp
from jax import lax
from jax.sharding import PartitionSpec as P
from jax.experimental import pallas as pl
from jax.experimental.pallas import tpu as pltpu

NAO = 2048
TILE = 128


def swapped(value, axis, apart):
    mask = 2**apart
    pairs = [(source, source ^ mask) for source in range(lax.axis_size(axis))]
    return lax.ppermute(value, axis, pairs)


def gather_round(axis, here, own, slots, send_sem, recv_sem):
    me, n = here[axis], lax.axis_size(axis)

    def device(index):
        place = dict(here)
        place[axis] = index
        return (place["aux"], place["row"], place["col"])

    slots[me] = own
    sends = []
    for step in range(1, n):
        dest = lax.rem(me + step, n)
        copy = pltpu.make_async_remote_copy(
            src_ref=slots.at[me],
            dst_ref=slots.at[me],
            send_sem=send_sem.at[step],
            recv_sem=recv_sem.at[step],
            device_id=device(dest),
            device_id_type=pl.DeviceIdType.MESH,
        )
        copy.start()
        sends.append(copy)
    for step in range(1, n):
        source = lax.rem(me + n - step, n)
        incoming = pltpu.make_async_remote_copy(
            src_ref=slots.at[me],
            dst_ref=slots.at[source],
            send_sem=send_sem.at[step],
            recv_sem=recv_sem.at[step],
            device_id=device(source),
            device_id_type=pl.DeviceIdType.MESH,
        )
        incoming.wait_recv()
        sends[step - 1].wait_send()
    total = slots[0]
    for index in range(1, n):
        total = total + slots[index]
    return total


def two_round_kernel(x_ref, o_ref, col_slots, row_slots, send_a, recv_a, send_b, recv_b):
    here = {name: lax.axis_index(name) for name in ("aux", "row", "col")}
    peers = []
    for axis in ("col", "row"):
        n = lax.axis_size(axis)
        for step in range(1, n):
            place = dict(here)
            place[axis] = lax.rem(here[axis] + step, n)
            peers.append((place["aux"], place["row"], place["col"]))
    barrier = pltpu.get_barrier_semaphore()
    for peer in peers:
        pl.semaphore_signal(barrier, inc=1, device_id=peer, device_id_type=pl.DeviceIdType.MESH)
    pl.semaphore_wait(barrier, len(peers))
    by_col = gather_round("col", here, x_ref[...], col_slots, send_a, recv_a)
    total = gather_round("row", here, by_col, row_slots, send_b, recv_b)
    o_ref[...] = total * (1.0 / NAO)


def doubling_sum(partial):
    cols, rows = lax.axis_size("col"), lax.axis_size("row")
    return pl.pallas_call(
        two_round_kernel,
        out_shape=jax.ShapeDtypeStruct(partial.shape, partial.dtype),
        in_specs=[pl.BlockSpec(memory_space=pltpu.VMEM)],
        out_specs=pl.BlockSpec(memory_space=pltpu.VMEM),
        scratch_shapes=[
            pltpu.VMEM((cols,) + partial.shape, partial.dtype),
            pltpu.VMEM((rows,) + partial.shape, partial.dtype),
            pltpu.SemaphoreType.DMA((cols,)),
            pltpu.SemaphoreType.DMA((cols,)),
            pltpu.SemaphoreType.DMA((rows,)),
            pltpu.SemaphoreType.DMA((rows,)),
        ],
        compiler_params=pltpu.CompilerParams(collective_id=0, has_side_effects=True),
    )(partial)


def gather_half(local):
    width = local.shape[1] // 2
    part = lax.dynamic_slice_in_dim(local, lax.axis_index("aux") * width, width, axis=1)
    return lax.all_gather(part, "row", axis=0, tiled=True)


def join_halves(own, other, axis):
    first = lax.axis_index("aux") == 0
    return jnp.where(
        first,
        jnp.concatenate([own, other], axis=axis),
        jnp.concatenate([other, own], axis=axis),
    )


def swapped_core(value):
    return lax.ppermute(value, "aux", [(0, 1), (1, 0)])


def sliced(ref, axis, start, size):
    index = [slice(None)] * len(ref.shape)
    index[axis] = pl.ds(start, size)
    return ref.at[tuple(index)]


def exchange_kernel(mesh_axis, split_axis, concat_axis, x_ref, o_ref, send_sem, recv_sem, local_sem):
    here = {name: lax.axis_index(name) for name in ("aux", "row", "col")}
    me, n = here[mesh_axis], lax.axis_size(mesh_axis)
    depth = x_ref.shape[split_axis] // n
    height = o_ref.shape[concat_axis] // n

    def device(index):
        place = dict(here)
        place[mesh_axis] = index
        return (place["aux"], place["row"], place["col"])

    def piece(index):
        return sliced(x_ref, split_axis, index * depth, depth)

    def slot(index):
        return sliced(o_ref, concat_axis, index * height, height)

    barrier = pltpu.get_barrier_semaphore()
    for step in range(1, n):
        pl.semaphore_signal(
            barrier, inc=1, device_id=device(lax.rem(me + step, n)),
            device_id_type=pl.DeviceIdType.MESH,
        )
    pl.semaphore_wait(barrier, n - 1)

    local = pltpu.make_async_copy(piece(me), slot(me), local_sem)
    local.start()
    sends = []
    for step in range(1, n):
        dest = lax.rem(me + step, n)
        copy = pltpu.make_async_remote_copy(
            src_ref=piece(dest),
            dst_ref=slot(me),
            send_sem=send_sem.at[step],
            recv_sem=recv_sem.at[step],
            device_id=device(dest),
            device_id_type=pl.DeviceIdType.MESH,
        )
        copy.start()
        sends.append(copy)
    for step in range(1, n):
        source = lax.rem(me + n - step, n)
        incoming = pltpu.make_async_remote_copy(
            src_ref=piece(me),
            dst_ref=slot(source),
            send_sem=send_sem.at[step],
            recv_sem=recv_sem.at[step],
            device_id=device(source),
            device_id_type=pl.DeviceIdType.MESH,
        )
        incoming.wait_recv()
        sends[step - 1].wait_send()
    local.wait()


def exchange(x, mesh_axis, split_axis, concat_axis, collective_id):
    n = lax.axis_size(mesh_axis)
    shape = list(x.shape)
    shape[split_axis] //= n
    shape[concat_axis] *= n
    nbytes = x.size * x.dtype.itemsize
    return pl.pallas_call(
        functools.partial(exchange_kernel, mesh_axis, split_axis, concat_axis),
        out_shape=jax.ShapeDtypeStruct(tuple(shape), x.dtype),
        in_specs=[pl.BlockSpec(memory_space=pl.ANY)],
        out_specs=pl.BlockSpec(memory_space=pl.ANY),
        scratch_shapes=[
            pltpu.SemaphoreType.DMA((n,)),
            pltpu.SemaphoreType.DMA((n,)),
            pltpu.SemaphoreType.DMA(()),
        ],
        compiler_params=pltpu.CompilerParams(
            collective_id=collective_id, has_side_effects=True
        ),
        cost_estimate=pl.CostEstimate(flops=0, bytes_accessed=2 * nbytes, transcendentals=0),
    )(x)


def gather_occ_rows(local):
    rows, cols = lax.axis_size("row"), lax.axis_size("col")
    width = local.shape[1] // cols
    height = local.shape[0] // 2
    piece = lax.dynamic_slice(
        local, (lax.axis_index("aux") * height, lax.axis_index("col") * width), (height, width)
    )
    column = exchange(jnp.tile(piece, (rows, 1)), "row", 0, 0, 5)
    return lax.all_gather(column, "col", axis=1, tiled=True)


def core_rows(moved, core):
    pieces, nao, ncol = moved.shape
    rows = lax.axis_size("row")
    split = moved.reshape(pieces, rows, 2, nao // (2 * rows), ncol)
    picked = lax.dynamic_index_in_dim(split, core, axis=2, keepdims=False)
    return picked.reshape(pieces, nao // 2, ncol)


def shards(coulomb, occupied, virtual, tile_mask):
    rows = lax.axis_size("row")
    cols = lax.axis_size("col")
    pdev, mrow, ncol = coulomb.shape
    nao = mrow * rows
    row_idx = lax.axis_index("row")
    col_idx = lax.axis_index("col")
    aux_idx = lax.axis_index("aux")
    tiles_r = mrow // TILE
    tiles_c = ncol // TILE
    local_tiles = lax.dynamic_slice(
        tile_mask, (row_idx * tiles_r, col_idx * tiles_c), (tiles_r, tiles_c)
    )
    local_mask = jnp.repeat(jnp.repeat(local_tiles, TILE, axis=0), TILE, axis=1).astype(
        jnp.bfloat16
    )
    screened = coulomb * local_mask[None]
    occ_rows = gather_occ_rows(occupied)
    virt_own = gather_half(virtual)
    moved = exchange(screened, "row", 0, 1, 1)
    occ_rows, moved = lax.optimization_barrier((occ_rows, moved))
    pieces = moved.shape[0]
    occ_other = swapped_core(occ_rows)
    mine = core_rows(moved, aux_idx)
    other = core_rows(moved, 1 - aux_idx)
    half = (
        jnp.einsum("ml,pmn->pln", occ_rows, mine, preferred_element_type=jnp.float32)
        + jnp.einsum("ml,pmn->pln", occ_other, other, preferred_element_type=jnp.float32)
    ).astype(jnp.bfloat16)
    jpart = mrow // cols
    shaped = half.reshape(pieces, rows, cols, jpart, ncol)
    spread = lax.all_to_all(shaped, "col", split_axis=2, concat_axis=4, tiled=True)
    spread = spread.reshape(pieces, rows * jpart, nao)
    virt_own, spread = lax.optimization_barrier((virt_own, spread))
    virt_other = swapped_core(virt_own)
    dressed_own = jnp.einsum("pln,ns->pls", spread, virt_own, preferred_element_type=jnp.float32)
    dressed_other = jnp.einsum(
        "pln,ns->pls", spread, virt_other, preferred_element_type=jnp.float32
    )
    dressed = join_halves(
        dressed_own.astype(jnp.bfloat16), dressed_other.astype(jnp.bfloat16), axis=2
    )
    by_dest = (
        dressed.reshape(pieces, rows, jpart, cols, ncol)
        .transpose(1, 3, 0, 2, 4)
        .reshape(rows * cols, pieces, jpart, ncol)
    )
    got = lax.all_to_all(by_dest, ("row", "col"), split_axis=0, concat_axis=0, tiled=True)
    returned = got.reshape(rows, cols, pieces, jpart, ncol)
    theirs = swapped(screened, "aux", 0)

    def against(block):
        split = block.reshape(pdev, cols, jpart, ncol)
        return jnp.einsum(
            "rcpjs,qcjs->rpq", returned, split, preferred_element_type=jnp.float32
        ).reshape(pdev, pdev)

    with_mine, with_theirs = against(screened), against(theirs)
    first_half = jnp.where(aux_idx == 0, with_mine, with_theirs)
    second_half = jnp.where(aux_idx == 0, with_theirs, with_mine)
    partial_chi = jnp.concatenate([first_half, second_half], axis=1)
    return doubling_sum(partial_chi)


def solution(mesh):
    placed = (P("aux", "row", "col"), P("row", None), P("row", None), P())
    return jax.shard_map(
        shards, mesh=mesh, in_specs=placed, out_specs=P("aux", None), check_vma=False
    )
```

```python
import functools

import jax
import jax.numpy as jnp
from jax import lax
from jax.sharding import PartitionSpec as P
from jax.experimental import pallas as pl
from jax.experimental.pallas import tpu as pltpu

NAO = 2048
TILE = 128


def swapped(value, axis, apart):
    mask = 2**apart
    pairs = [(source, source ^ mask) for source in range(lax.axis_size(axis))]
    return lax.ppermute(value, axis, pairs)


def gather_round(axis, here, own, slots, send_sem, recv_sem):
    me, n = here[axis], lax.axis_size(axis)

    def device(index):
        place = dict(here)
        place[axis] = index
        return (place["aux"], place["row"], place["col"])

    slots[me] = own
    sends = []
    for step in range(1, n):
        dest = lax.rem(me + step, n)
        copy = pltpu.make_async_remote_copy(
            src_ref=slots.at[me],
            dst_ref=slots.at[me],
            send_sem=send_sem.at[step],
            recv_sem=recv_sem.at[step],
            device_id=device(dest),
            device_id_type=pl.DeviceIdType.MESH,
        )
        copy.start()
        sends.append(copy)
    for step in range(1, n):
        source = lax.rem(me + n - step, n)
        incoming = pltpu.make_async_remote_copy(
            src_ref=slots.at[me],
            dst_ref=slots.at[source],
            send_sem=send_sem.at[step],
            recv_sem=recv_sem.at[step],
            device_id=device(source),
            device_id_type=pl.DeviceIdType.MESH,
        )
        incoming.wait_recv()
        sends[step - 1].wait_send()
    total = slots[0]
    for index in range(1, n):
        total = total + slots[index]
    return total


def two_round_kernel(x_ref, o_ref, col_slots, row_slots, send_a, recv_a, send_b, recv_b):
    here = {name: lax.axis_index(name) for name in ("aux", "row", "col")}
    peers = []
    for axis in ("col", "row"):
        n = lax.axis_size(axis)
        for step in range(1, n):
            place = dict(here)
            place[axis] = lax.rem(here[axis] + step, n)
            peers.append((place["aux"], place["row"], place["col"]))
    barrier = pltpu.get_barrier_semaphore()
    for peer in peers:
        pl.semaphore_signal(barrier, inc=1, device_id=peer, device_id_type=pl.DeviceIdType.MESH)
    pl.semaphore_wait(barrier, len(peers))
    by_col = gather_round("col", here, x_ref[...], col_slots, send_a, recv_a)
    o_ref[...] = gather_round("row", here, by_col, row_slots, send_b, recv_b)


def doubling_sum(partial):
    cols, rows = lax.axis_size("col"), lax.axis_size("row")
    return pl.pallas_call(
        two_round_kernel,
        out_shape=jax.ShapeDtypeStruct(partial.shape, partial.dtype),
        in_specs=[pl.BlockSpec(memory_space=pltpu.VMEM)],
        out_specs=pl.BlockSpec(memory_space=pltpu.VMEM),
        scratch_shapes=[
            pltpu.VMEM((cols,) + partial.shape, partial.dtype),
            pltpu.VMEM((rows,) + partial.shape, partial.dtype),
            pltpu.SemaphoreType.DMA((cols,)),
            pltpu.SemaphoreType.DMA((cols,)),
            pltpu.SemaphoreType.DMA((rows,)),
            pltpu.SemaphoreType.DMA((rows,)),
        ],
        compiler_params=pltpu.CompilerParams(collective_id=0, has_side_effects=True),
    )(partial)


def gather_half(local):
    width = local.shape[1] // 2
    part = lax.dynamic_slice_in_dim(local, lax.axis_index("aux") * width, width, axis=1)
    return lax.all_gather(part, "row", axis=0, tiled=True)


def join_halves(own, other, axis):
    first = lax.axis_index("aux") == 0
    return jnp.where(
        first,
        jnp.concatenate([own, other], axis=axis),
        jnp.concatenate([other, own], axis=axis),
    )


def swapped_core(value):
    return lax.ppermute(value, "aux", [(0, 1), (1, 0)])


def sliced(ref, axis, start, size):
    index = [slice(None)] * len(ref.shape)
    index[axis] = pl.ds(start, size)
    return ref.at[tuple(index)]


def exchange_kernel(mesh_axis, split_axis, concat_axis, window, x_ref, o_ref, send_sem, recv_sem, local_sem):
    here = {name: lax.axis_index(name) for name in ("aux", "row", "col")}
    me, n = here[mesh_axis], lax.axis_size(mesh_axis)
    depth = x_ref.shape[split_axis] // n
    height = o_ref.shape[concat_axis] // n
    if window is not None:
        depth = window[0]

    def device(index):
        place = dict(here)
        place[mesh_axis] = index
        return (place["aux"], place["row"], place["col"])

    def piece(index):
        if window is not None:
            height, width = window
            return x_ref.at[
                pl.ds(here["aux"] * height, height), pl.ds(here["col"] * width, width)
            ]
        return sliced(x_ref, split_axis, index * depth, depth)

    def slot(index):
        return sliced(o_ref, concat_axis, index * height, height)

    barrier = pltpu.get_barrier_semaphore()
    for step in range(1, n):
        pl.semaphore_signal(
            barrier, inc=1, device_id=device(lax.rem(me + step, n)),
            device_id_type=pl.DeviceIdType.MESH,
        )
    pl.semaphore_wait(barrier, n - 1)

    local = pltpu.make_async_copy(piece(me), slot(me), local_sem)
    local.start()
    sends = []
    for step in range(1, n):
        dest = lax.rem(me + step, n)
        copy = pltpu.make_async_remote_copy(
            src_ref=piece(dest),
            dst_ref=slot(me),
            send_sem=send_sem.at[step],
            recv_sem=recv_sem.at[step],
            device_id=device(dest),
            device_id_type=pl.DeviceIdType.MESH,
        )
        copy.start()
        sends.append(copy)
    for step in range(1, n):
        source = lax.rem(me + n - step, n)
        incoming = pltpu.make_async_remote_copy(
            src_ref=piece(me),
            dst_ref=slot(source),
            send_sem=send_sem.at[step],
            recv_sem=recv_sem.at[step],
            device_id=device(source),
            device_id_type=pl.DeviceIdType.MESH,
        )
        incoming.wait_recv()
        sends[step - 1].wait_send()
    local.wait()


def exchange(x, mesh_axis, split_axis, concat_axis, collective_id, window=None):
    n = lax.axis_size(mesh_axis)
    shape = list(x.shape)
    if window is not None:
        shape = [window[0] * n, window[1]]
    else:
        shape[split_axis] //= n
        shape[concat_axis] *= n
    nbytes = x.size * x.dtype.itemsize
    return pl.pallas_call(
        functools.partial(exchange_kernel, mesh_axis, split_axis, concat_axis, window),
        out_shape=jax.ShapeDtypeStruct(tuple(shape), x.dtype),
        in_specs=[pl.BlockSpec(memory_space=pl.ANY)],
        out_specs=pl.BlockSpec(memory_space=pl.ANY),
        scratch_shapes=[
            pltpu.SemaphoreType.DMA((n,)),
            pltpu.SemaphoreType.DMA((n,)),
            pltpu.SemaphoreType.DMA(()),
        ],
        compiler_params=pltpu.CompilerParams(
            collective_id=collective_id, has_side_effects=True
        ),
        cost_estimate=pl.CostEstimate(flops=0, bytes_accessed=2 * nbytes, transcendentals=0),
    )(x)


def gather_occ_rows(local):
    rows, cols = lax.axis_size("row"), lax.axis_size("col")
    width = local.shape[1] // cols
    height = local.shape[0] // 2
    column = exchange(local, "row", 0, 0, 5, window=(height, width))
    return lax.all_gather(column, "col", axis=1, tiled=True)


def core_rows(moved, core):
    pieces, nao, ncol = moved.shape
    rows = lax.axis_size("row")
    split = moved.reshape(pieces, rows, 2, nao // (2 * rows), ncol)
    picked = lax.dynamic_index_in_dim(split, core, axis=2, keepdims=False)
    return picked.reshape(pieces, nao // 2, ncol)


def shards(coulomb, occupied, virtual, tile_mask):
    rows = lax.axis_size("row")
    cols = lax.axis_size("col")
    pdev, mrow, ncol = coulomb.shape
    nao = mrow * rows
    row_idx = lax.axis_index("row")
    col_idx = lax.axis_index("col")
    aux_idx = lax.axis_index("aux")
    tiles_r = mrow // TILE
    tiles_c = ncol // TILE
    local_tiles = lax.dynamic_slice(
        tile_mask, (row_idx * tiles_r, col_idx * tiles_c), (tiles_r, tiles_c)
    )
    local_mask = jnp.repeat(jnp.repeat(local_tiles, TILE, axis=0), TILE, axis=1).astype(
        jnp.bfloat16
    )
    screened = coulomb * local_mask[None]
    occ_rows = gather_occ_rows(occupied)
    virt_own = gather_half(virtual)
    moved = exchange(screened, "row", 0, 1, 1)
    occ_rows, moved = lax.optimization_barrier((occ_rows, moved))
    pieces = moved.shape[0]
    occ_other = swapped_core(occ_rows)
    mine = core_rows(moved, aux_idx)
    other = core_rows(moved, 1 - aux_idx)
    half = (
        jnp.einsum("ml,pmn->pln", occ_rows, mine, preferred_element_type=jnp.float32)
        + jnp.einsum("ml,pmn->pln", occ_other, other, preferred_element_type=jnp.float32)
    ).astype(jnp.bfloat16)
    jpart = mrow // cols
    shaped = half.reshape(pieces, rows, cols, jpart, ncol)
    spread = lax.all_to_all(shaped, "col", split_axis=2, concat_axis=4, tiled=True)
    spread = spread.reshape(pieces, rows * jpart, nao)
    virt_own, spread = lax.optimization_barrier((virt_own, spread))
    virt_other = swapped_core(virt_own)
    dressed_own = jnp.einsum("pln,ns->pls", spread, virt_own, preferred_element_type=jnp.float32)
    dressed_other = jnp.einsum(
        "pln,ns->pls", spread, virt_other, preferred_element_type=jnp.float32
    )
    dressed = join_halves(
        dressed_own.astype(jnp.bfloat16), dressed_other.astype(jnp.bfloat16), axis=2
    )
    by_dest = (
        dressed.reshape(pieces, rows, jpart, cols, ncol)
        .transpose(1, 3, 0, 2, 4)
        .reshape(rows * cols, pieces, jpart, ncol)
    )
    got = lax.all_to_all(by_dest, ("row", "col"), split_axis=0, concat_axis=0, tiled=True)
    returned = got.reshape(rows, cols, pieces, jpart, ncol)
    theirs = swapped(screened, "aux", 0)

    def against(block):
        split = block.reshape(pdev, cols, jpart, ncol)
        return jnp.einsum(
            "rcpjs,qcjs->rpq", returned, split, preferred_element_type=jnp.float32
        ).reshape(pdev, pdev)

    with_mine, with_theirs = against(screened), against(theirs)
    first_half = jnp.where(aux_idx == 0, with_mine, with_theirs)
    second_half = jnp.where(aux_idx == 0, with_theirs, with_mine)
    partial_chi = jnp.concatenate([first_half, second_half], axis=1)
    total_chi = doubling_sum(partial_chi)
    return total_chi / NAO


def solution(mesh):
    placed = (P("aux", "row", "col"), P("row", None), P("row", None), P())
    return jax.shard_map(
        shards, mesh=mesh, in_specs=placed, out_specs=P("aux", None), check_vma=False
    )
```

```python
import functools

import jax
import jax.numpy as jnp
from jax import lax
from jax.sharding import PartitionSpec as P
from jax.experimental import pallas as pl
from jax.experimental.pallas import tpu as pltpu

NAO = 2048
TILE = 128


def swapped(value, axis, apart):
    mask = 2**apart
    pairs = [(source, source ^ mask) for source in range(lax.axis_size(axis))]
    return lax.ppermute(value, axis, pairs)


def gather_round(axis, here, own, slots, send_sem, recv_sem):
    me, n = here[axis], lax.axis_size(axis)

    def device(index):
        place = dict(here)
        place[axis] = index
        return (place["aux"], place["row"], place["col"])

    slots[me] = own
    sends = []
    for step in range(1, n):
        dest = lax.rem(me + step, n)
        copy = pltpu.make_async_remote_copy(
            src_ref=slots.at[me],
            dst_ref=slots.at[me],
            send_sem=send_sem.at[step],
            recv_sem=recv_sem.at[step],
            device_id=device(dest),
            device_id_type=pl.DeviceIdType.MESH,
        )
        copy.start()
        sends.append(copy)
    for step in range(1, n):
        source = lax.rem(me + n - step, n)
        incoming = pltpu.make_async_remote_copy(
            src_ref=slots.at[me],
            dst_ref=slots.at[source],
            send_sem=send_sem.at[step],
            recv_sem=recv_sem.at[step],
            device_id=device(source),
            device_id_type=pl.DeviceIdType.MESH,
        )
        incoming.wait_recv()
        sends[step - 1].wait_send()
    total = slots[0]
    for index in range(1, n):
        total = total + slots[index]
    return total


def two_round_kernel(x_ref, o_ref, col_slots, row_slots, send_a, recv_a, send_b, recv_b):
    here = {name: lax.axis_index(name) for name in ("aux", "row", "col")}
    peers = []
    for axis in ("col", "row"):
        n = lax.axis_size(axis)
        for step in range(1, n):
            place = dict(here)
            place[axis] = lax.rem(here[axis] + step, n)
            peers.append((place["aux"], place["row"], place["col"]))
    barrier = pltpu.get_barrier_semaphore()
    for peer in peers:
        pl.semaphore_signal(barrier, inc=1, device_id=peer, device_id_type=pl.DeviceIdType.MESH)
    pl.semaphore_wait(barrier, len(peers))
    by_col = gather_round("col", here, x_ref[...], col_slots, send_a, recv_a)
    o_ref[...] = gather_round("row", here, by_col, row_slots, send_b, recv_b)


def doubling_sum(partial):
    cols, rows = lax.axis_size("col"), lax.axis_size("row")
    return pl.pallas_call(
        two_round_kernel,
        out_shape=jax.ShapeDtypeStruct(partial.shape, partial.dtype),
        in_specs=[pl.BlockSpec(memory_space=pltpu.VMEM)],
        out_specs=pl.BlockSpec(memory_space=pltpu.VMEM),
        scratch_shapes=[
            pltpu.VMEM((cols,) + partial.shape, partial.dtype),
            pltpu.VMEM((rows,) + partial.shape, partial.dtype),
            pltpu.SemaphoreType.DMA((cols,)),
            pltpu.SemaphoreType.DMA((cols,)),
            pltpu.SemaphoreType.DMA((rows,)),
            pltpu.SemaphoreType.DMA((rows,)),
        ],
        compiler_params=pltpu.CompilerParams(collective_id=0, has_side_effects=True),
    )(partial)


def gather_half(local):
    width = local.shape[1] // 2
    part = lax.dynamic_slice_in_dim(local, lax.axis_index("aux") * width, width, axis=1)
    return lax.all_gather(part, "row", axis=0, tiled=True)


def join_halves(own, other, axis):
    first = lax.axis_index("aux") == 0
    return jnp.where(
        first,
        jnp.concatenate([own, other], axis=axis),
        jnp.concatenate([other, own], axis=axis),
    )


def swapped_core(value):
    return lax.ppermute(value, "aux", [(0, 1), (1, 0)])


def sliced(ref, axis, start, size):
    index = [slice(None)] * len(ref.shape)
    index[axis] = pl.ds(start, size)
    return ref.at[tuple(index)]


def exchange_kernel(mesh_axis, split_axis, concat_axis, window, x_ref, o_ref, send_sem, recv_sem, local_sem):
    here = {name: lax.axis_index(name) for name in ("aux", "row", "col")}
    me, n = here[mesh_axis], lax.axis_size(mesh_axis)
    depth = x_ref.shape[split_axis] // n
    height = o_ref.shape[concat_axis] // n
    if window is not None:
        depth = window[0]

    def device(index):
        place = dict(here)
        place[mesh_axis] = index
        return (place["aux"], place["row"], place["col"])

    def piece(index):
        if window is not None:
            height, width = window
            return x_ref.at[
                pl.ds(here["aux"] * height, height), pl.ds(here["col"] * width, width)
            ]
        return sliced(x_ref, split_axis, index * depth, depth)

    def slot(index):
        return sliced(o_ref, concat_axis, index * height, height)

    barrier = pltpu.get_barrier_semaphore()
    for step in range(1, n):
        pl.semaphore_signal(
            barrier, inc=1, device_id=device(lax.rem(me + step, n)),
            device_id_type=pl.DeviceIdType.MESH,
        )
    pl.semaphore_wait(barrier, n - 1)

    local = pltpu.make_async_copy(piece(me), slot(me), local_sem)
    local.start()
    sends = []
    for step in range(1, n):
        dest = lax.rem(me + step, n)
        copy = pltpu.make_async_remote_copy(
            src_ref=piece(dest),
            dst_ref=slot(me),
            send_sem=send_sem.at[step],
            recv_sem=recv_sem.at[step],
            device_id=device(dest),
            device_id_type=pl.DeviceIdType.MESH,
        )
        copy.start()
        sends.append(copy)
    for step in range(1, n):
        source = lax.rem(me + n - step, n)
        incoming = pltpu.make_async_remote_copy(
            src_ref=piece(me),
            dst_ref=slot(source),
            send_sem=send_sem.at[step],
            recv_sem=recv_sem.at[step],
            device_id=device(source),
            device_id_type=pl.DeviceIdType.MESH,
        )
        incoming.wait_recv()
        sends[step - 1].wait_send()
    local.wait()


def exchange(x, mesh_axis, split_axis, concat_axis, collective_id, window=None):
    n = lax.axis_size(mesh_axis)
    shape = list(x.shape)
    if window is not None:
        shape = [window[0] * n, window[1]]
    else:
        shape[split_axis] //= n
        shape[concat_axis] *= n
    nbytes = x.size * x.dtype.itemsize
    return pl.pallas_call(
        functools.partial(exchange_kernel, mesh_axis, split_axis, concat_axis, window),
        out_shape=jax.ShapeDtypeStruct(tuple(shape), x.dtype),
        in_specs=[pl.BlockSpec(memory_space=pl.ANY)],
        out_specs=pl.BlockSpec(memory_space=pl.ANY),
        scratch_shapes=[
            pltpu.SemaphoreType.DMA((n,)),
            pltpu.SemaphoreType.DMA((n,)),
            pltpu.SemaphoreType.DMA(()),
        ],
        compiler_params=pltpu.CompilerParams(
            collective_id=collective_id, has_side_effects=True
        ),
        cost_estimate=pl.CostEstimate(flops=0, bytes_accessed=2 * nbytes, transcendentals=0),
    )(x)


def gather_occ_rows(local):
    rows, cols = lax.axis_size("row"), lax.axis_size("col")
    width = local.shape[1] // cols
    height = local.shape[0] // 2
    column = exchange(local, "row", 0, 0, 5, window=(height, width))
    return lax.all_gather(column, "col", axis=1, tiled=True)


def core_rows(moved, core):
    pieces, nao, ncol = moved.shape
    rows = lax.axis_size("row")
    split = moved.reshape(pieces, rows, 2, nao // (2 * rows), ncol)
    picked = lax.dynamic_index_in_dim(split, core, axis=2, keepdims=False)
    return picked.reshape(pieces, nao // 2, ncol)


def shards(coulomb, occupied, virtual, tile_mask):
    rows = lax.axis_size("row")
    cols = lax.axis_size("col")
    pdev, mrow, ncol = coulomb.shape
    nao = mrow * rows
    row_idx = lax.axis_index("row")
    col_idx = lax.axis_index("col")
    aux_idx = lax.axis_index("aux")
    tiles_r = mrow // TILE
    tiles_c = ncol // TILE
    local_tiles = lax.dynamic_slice(
        tile_mask, (row_idx * tiles_r, col_idx * tiles_c), (tiles_r, tiles_c)
    )
    local_mask = jnp.repeat(jnp.repeat(local_tiles, TILE, axis=0), TILE, axis=1).astype(
        jnp.bfloat16
    )
    screened = coulomb * local_mask[None]
    occ_rows = gather_occ_rows(occupied)
    virt_own = gather_half(virtual)
    moved = exchange(screened, "row", 0, 1, 1)
    pieces = moved.shape[0]
    mine = core_rows(moved, aux_idx)
    other = core_rows(moved, 1 - aux_idx)
    occ_rows, mine, other = lax.optimization_barrier((occ_rows, mine, other))
    occ_other = swapped_core(occ_rows)
    half = (
        jnp.einsum("ml,pmn->pln", occ_rows, mine, preferred_element_type=jnp.float32)
        + jnp.einsum("ml,pmn->pln", occ_other, other, preferred_element_type=jnp.float32)
    ).astype(jnp.bfloat16)
    jpart = mrow // cols
    shaped = half.reshape(pieces, rows, cols, jpart, ncol)
    spread = lax.all_to_all(shaped, "col", split_axis=2, concat_axis=4, tiled=True)
    spread = spread.reshape(pieces, rows * jpart, nao)
    virt_own, spread = lax.optimization_barrier((virt_own, spread))
    virt_other = swapped_core(virt_own)
    dressed_own = jnp.einsum("pln,ns->pls", spread, virt_own, preferred_element_type=jnp.float32)
    dressed_other = jnp.einsum(
        "pln,ns->pls", spread, virt_other, preferred_element_type=jnp.float32
    )
    dressed = join_halves(
        dressed_own.astype(jnp.bfloat16), dressed_other.astype(jnp.bfloat16), axis=2
    )
    by_dest = (
        dressed.reshape(pieces, rows, jpart, cols, ncol)
        .transpose(1, 3, 0, 2, 4)
        .reshape(rows * cols, pieces, jpart, ncol)
    )
    got = lax.all_to_all(by_dest, ("row", "col"), split_axis=0, concat_axis=0, tiled=True)
    returned = got.reshape(rows, cols, pieces, jpart, ncol)
    theirs = swapped(screened, "aux", 0)

    def against(block):
        split = block.reshape(pdev, cols, jpart, ncol)
        return jnp.einsum(
            "rcpjs,qcjs->rpq", returned, split, preferred_element_type=jnp.float32
        ).reshape(pdev, pdev)

    with_mine, with_theirs = against(screened), against(theirs)
    first_half = jnp.where(aux_idx == 0, with_mine, with_theirs)
    second_half = jnp.where(aux_idx == 0, with_theirs, with_mine)
    partial_chi = jnp.concatenate([first_half, second_half], axis=1)
    total_chi = doubling_sum(partial_chi)
    return total_chi / NAO


def solution(mesh):
    placed = (P("aux", "row", "col"), P("row", None), P("row", None), P())
    return jax.shard_map(
        shards, mesh=mesh, in_specs=placed, out_specs=P("aux", None), check_vma=False
    )
```
